32 devices in a mesh: ctx: 8 (over y, x, core), fsdp: 4 (over z).
Axes of the slice: x: 2, y: 2, z: 4, core: 2. Of those that a mesh axis runs over, the one named last changes fastest.
Arguments:
- inputs: bfloat16 [2, 8, 2, 128, 2048], P(None, 'ctx', None, 'fsdp'), may hold values from -6 to 6
- w_qkv: float32 [2048, 2304], P('fsdp'), may hold values from -0.1875 to 0.1875
- w_out: float32 [2048, 2048], P('fsdp'), may hold values from -0.75 to 0.75
- w_fc: float32 [2048, 8192], P('fsdp'), may hold values from -0.125 to 0.125
- w_proj: float32 [8192, 2048], P('fsdp'), may hold values from -0.0625 to 0.0625
- ln1_gain: float32 [2048], P('fsdp'), may hold values from 0.5 to 1.5
- ln1_bias: float32 [2048], P('fsdp'), may hold values from -1.8 to 1.8
- bias_q: float32 [2048], P('fsdp'), may hold values from -1.8 to 1.8
- bias_v: float32 [128], P('fsdp'), may hold values from -1.8 to 1.8
- bias_out: float32 [2048], P('fsdp'), may hold values from -1.8 to 1.8
- ln2_gain: float32 [2048], P('fsdp'), may hold values from 0.5 to 1.5
- ln2_bias: float32 [2048], P('fsdp'), may hold values from -1.8 to 1.8
- bias_fc: float32 [8192], P('fsdp'), may hold values from -1.8 to 1.8
- bias_proj: float32 [2048], P('fsdp'), may hold values from -1.8 to 1.8
- cotangent: bfloat16 [2, 8, 2, 128, 2048], P(None, 'ctx', None, 'fsdp'), may hold values from -6 to 6
- lengths: int32 [2, 2], replicated, may hold values from 512 to 1536, as said below
- pair_table: int32 [8], replicated, may hold values from 0 to 7, each once
Outputs:
- result: bfloat16 [2, 8, 2, 128, 2048], P(None, 'ctx', None, 'fsdp')
- grad_inputs: float32 [2, 8, 2, 128, 2048], P(None, 'ctx', None, 'fsdp')
- grad_w_qkv: float32 [2048, 2304], P('fsdp')
- grad_w_out: float32 [2048, 2048], P('fsdp')
- grad_w_fc: float32 [2048, 8192], P('fsdp')
- grad_w_proj: float32 [8192, 2048], P('fsdp')
- grad_ln1_gain: float32 [2048], P('fsdp')
- grad_ln1_bias: float32 [2048], P('fsdp')
- grad_bias_q: float32 [2048], P('fsdp')
- grad_bias_v: float32 [128], P('fsdp')
- grad_bias_out: float32 [2048], P('fsdp')
- grad_ln2_gain: float32 [2048], P('fsdp')
- grad_ln2_bias: float32 [2048], P('fsdp')
- grad_bias_fc: float32 [8192], P('fsdp')
- grad_bias_proj: float32 [2048], P('fsdp')
The draws below stay inside these ranges and needn't reach their ends.
Inputs may be any that keep to these rules, and one draw needn't show every extreme that they name: Each slot's two lengths are each at least 512 and add up to at most 2048; in every draw one slot holds exactly 512 and 1536, in some order. A permutation of the ctx indices' block pairs: index c holds blocks pair_table[c] and 15 - pair_table[c].
All inputs are finite; a program needn't handle non-finite values.
Results may differ from the reference program's by a relative error of at most 0.02.
Values may be sent and summed in bfloat16 or wider, within the bound.
No kernel may reach another device: no remote copies, remote signals or barrier semaphores. Data moves between devices by JAX's collectives and lax.ppermute only.
A program may use at most 448 MiB of HBM per device.

```python
import math
import jax
import jax.numpy as jnp
from jax import lax

D = 2048
HEADS = 16
HD = 128
FF = 8192
SLOTS = 2
BLOCK = 128
SEQ = 2048
N_CTX = 8


def draw_lengths(key, part):
    quarter = SEQ // 4
    key_list = jax.random.split(key, 4)
    first_len = jax.random.randint(key_list[0], (SLOTS,), quarter, SEQ - quarter + 1)
    spare_bits = jax.random.randint(key_list[1], (SLOTS,), 0, 1 << 24)
    second_len = quarter + spare_bits % (SEQ - quarter - first_len + 1)
    chosen = jax.random.randint(key_list[2], (), 0, SLOTS)
    order_bit = jax.random.randint(key_list[3], (), 0, 2)
    forced_len = jnp.where(order_bit == 0, SEQ - quarter, quarter)
    slot_ids = jnp.arange(SLOTS)
    first_len = jnp.where(slot_ids == chosen, forced_len, first_len)
    second_len = jnp.where(slot_ids == chosen, SEQ - forced_len, second_len)
    return jnp.stack([first_len, second_len], axis=1).astype(jnp.int32)


def steps_of(rng, extent, shards, least, high):
    loudness, own = 1.0, jax.random.fold_in(rng, 6)
    for axis_at, shards_of in shards:
        steps = jnp.exp(jax.random.uniform(jax.random.fold_in(own, axis_at), (shards_of,), jnp.float32, least / len(shards), high / len(shards)))
        loudness = loudness * jnp.repeat(steps, extent[axis_at] // shards_of).reshape([-1 if axis == axis_at else 1 for axis in range(len(extent))])
    return loudness


def scatter_about(own_key, shape, width, reach, pieces=(), held_as=jnp.bfloat16):
    values = jax.random.normal(own_key, shape, jnp.float32) * width
    if len(pieces) > 0:
        values = steps_of(own_key, shape, pieces, -0.22, 0.18) * values
    return jnp.clip(values, min=-reach, max=reach).astype(held_as)


def setup_inputs(seed: int = 0) -> dict:
    keys = jax.random.split(jax.random.key(seed), 18)
    return {
        "inputs": scatter_about(keys[0], (SLOTS, N_CTX, 2, BLOCK, D), 1.0, 6.0, ((1, 8), (3, 4))),
        "w_qkv": scatter_about(keys[1], (D, D + 2 * HD), (D // 2) ** -0.5, 0.1875, ((0, 4),), jnp.float32),
        "w_out": scatter_about(keys[2], (D, D), (D // 32) ** -0.5, 0.75, ((0, 4),), jnp.float32),
        "w_fc": scatter_about(keys[3], (D, FF), D ** -0.5, 0.125, ((0, 4),), jnp.float32),
        "w_proj": scatter_about(keys[4], (FF, D), FF ** -0.5, 0.0625, ((0, 4),), jnp.float32),
        "ln1_gain": jnp.clip(1.0 + 0.1 * jax.random.normal(keys[5], (D,), jnp.float32), 0.5, 1.5),
        "ln1_bias": scatter_about(keys[6], (D,), 0.3, 1.8, ((0, 4),), jnp.float32),
        "bias_q": scatter_about(keys[7], (D,), 0.3, 1.8, ((0, 4),), jnp.float32),
        "bias_v": scatter_about(keys[8], (HD,), 0.3, 1.8, ((0, 4),), jnp.float32),
        "bias_out": scatter_about(keys[9], (D,), 0.3, 1.8, ((0, 4),), jnp.float32),
        "ln2_gain": jnp.clip(1.0 + 0.1 * jax.random.normal(keys[10], (D,), jnp.float32), 0.5, 1.5),
        "ln2_bias": scatter_about(keys[11], (D,), 0.3, 1.8, ((0, 4),), jnp.float32),
        "bias_fc": scatter_about(keys[12], (FF,), 0.3, 1.8, ((0, 4),), jnp.float32),
        "bias_proj": scatter_about(keys[13], (D,), 0.3, 1.8, ((0, 4),), jnp.float32),
        "cotangent": scatter_about(keys[14], (SLOTS, N_CTX, 2, BLOCK, D), 1.0, 6.0, ((1, 8), (3, 4))),
        "lengths": draw_lengths(jax.random.fold_in(keys[17], 71), 0),
        "pair_table": jax.random.permutation(keys[16], N_CTX).astype(jnp.int32),
    }


@jax.custom_vjp
def low(v):
    return lax.optimization_barrier(v.astype(jnp.bfloat16)).astype(jnp.float32)

@jax.custom_vjp
def low_back(v):
    return v

def low_keep(v):
    return (low(v), None)

def low_pass(kept, grad):
    return (grad,)

def back_keep(v):
    return (v, None)

def back_low(kept, grad):
    return (low(grad),)
low.defvjp(low_keep, low_pass)
low_back.defvjp(back_keep, back_low)
highest = lax.Precision.HIGHEST
norm_eps = 1e-05
masked_score = -1e+30

def matmul(left_side, right_side):
    return jnp.dot(left_side, right_side, precision=highest, preferred_element_type=jnp.float32)

def layer_norm(values, gain_vec, shift_vec):
    centred = values - lax.optimization_barrier(jnp.mean(values, axis=-1, keepdims=True))
    inverse = lax.rsqrt(lax.optimization_barrier(jnp.mean(centred * centred, axis=-1, keepdims=True)) + norm_eps)
    return centred * inverse * gain_vec + shift_vec

def gelu_tanh(values):
    return jax.nn.gelu(values, approximate=True)

def slot_layer(slot_rows, slot_docs, positions, params):
    w_qkv, w_out, w_fc, w_proj, ln1_gain, ln1_bias, bias_q, bias_v, bias_out, ln2_gain, ln2_bias, bias_fc, bias_proj = params
    normed = low(layer_norm(slot_rows, ln1_gain, ln1_bias))
    projected = matmul(normed, w_qkv)
    query_rows = low(low_back(projected[:, :D] + bias_q))
    key_rows = low(low_back(projected[:, D:D + HD]))
    value_rows = low(low_back(projected[:, D + HD:] + bias_v))
    score_scale = 1.0 / math.sqrt(HD)

    def attend(block_item):
        query_blk, query_pos, query_doc = block_item
        scores = jnp.einsum('qhd,kd->qhk', query_blk, key_rows, precision=highest) * score_scale
        scores = low_back(scores)
        allowed = (query_doc[:, None, None] == slot_docs[None, None, :]) & (positions[None, None, :] <= query_pos[:, None, None])
        scores = jnp.where(allowed, scores, masked_score)
        weights = low(jax.nn.softmax(scores, axis=-1))
        return jnp.einsum('qhk,kd->qhd', weights, value_rows, precision=highest)
    blocks = SEQ // BLOCK
    attended = lax.map(jax.checkpoint(attend), (query_rows.reshape(blocks, BLOCK, HEADS, HD), positions.reshape(blocks, BLOCK), slot_docs.reshape(blocks, BLOCK)))
    attended = low(low_back(attended.reshape(SEQ, D)))
    branch = low_back(matmul(attended, w_out) + bias_out)
    middle = slot_rows + branch
    closing = low(layer_norm(middle, ln2_gain, ln2_bias))
    hidden = low_back(matmul(closing, w_fc) + bias_fc)
    activated = low(gelu_tanh(hidden))
    mlp_out = low_back(matmul(activated, w_proj) + bias_proj)
    return middle + mlp_out

def reference(inputs, w_qkv, w_out, w_fc, w_proj, ln1_gain, ln1_bias, bias_q, bias_v, bias_out, ln2_gain, ln2_bias, bias_fc, bias_proj, cotangent, lengths, pair_table):
    dealt_blocks = jnp.stack([pair_table, 2 * N_CTX - 1 - pair_table], axis=1).astype(jnp.int32)
    positions = (dealt_blocks[:, :, None] * BLOCK + jnp.arange(BLOCK, dtype=jnp.int32)[None, None, :]).reshape(SEQ).astype(jnp.int32)
    doc_start = lengths[:, 0:1]
    doc_end = lengths[:, 0:1] + lengths[:, 1:2]
    doc_index = (positions[None, :] >= doc_start).astype(jnp.int32) + (positions[None, :] >= doc_end).astype(jnp.int32)
    live_rows = (positions[None, :] < doc_end).astype(jnp.float32)
    rows_in = inputs.astype(jnp.float32).reshape(SLOTS, SEQ, D)
    grad_out = cotangent.astype(jnp.float32).reshape(SLOTS, SEQ, D) * live_rows[:, :, None]
    params = (w_qkv, w_out, w_fc, w_proj, ln1_gain, ln1_bias, bias_q, bias_v, bias_out, ln2_gain, ln2_bias, bias_fc, bias_proj)

    def forward(rows_all, param_set):
        rounded = tuple((low(master) for master in param_set))
        slot_fn = jax.checkpoint(lambda slot_rows, slot_docs: slot_layer(slot_rows, slot_docs, positions, rounded))

        def scan_step(carry_in, slot_pair):
            return (carry_in, slot_fn(slot_pair[0], slot_pair[1]))
        unused, outputs = lax.scan(scan_step, jnp.zeros((), jnp.float32), (rows_all, doc_index))
        return outputs
    outputs, pullback = jax.vjp(forward, rows_in, params)
    grad_rows, grad_params = pullback(grad_out)
    result = outputs.reshape(inputs.shape).astype(jnp.bfloat16)
    return (result, grad_rows.reshape(inputs.shape), grad_params[0], grad_params[1], grad_params[2], grad_params[3], grad_params[4], grad_params[5], grad_params[6], grad_params[7], grad_params[8], grad_params[9], grad_params[10], grad_params[11], grad_params[12])
```

```python
import functools
import math

import jax
import jax.numpy as jnp
from jax import lax
from jax.experimental import pallas as pl
from jax.experimental.pallas import tpu as pltpu
from jax.sharding import PartitionSpec as P

HEADS = 16
HD = 128
NORM_EPS = 1e-05
MASKED = -1e30
KEY_TILE = 512
LANE_ROWS = 256
SCALE = 1.0 / math.sqrt(HD)
F32 = jnp.float32
BF16 = jnp.bfloat16


def layer_norm(values, gain_vec, shift_vec):
    centred = values - jnp.mean(values, axis=-1, keepdims=True)
    inverse = lax.rsqrt(jnp.mean(centred * centred, axis=-1, keepdims=True) + NORM_EPS)
    normed = centred * inverse
    return (normed * gain_vec + shift_vec, normed, inverse)


def norm_backward(grad_norm, normed, inverse, gain_vec):
    scaled = grad_norm * gain_vec
    centred = scaled - jnp.mean(scaled, axis=-1, keepdims=True)
    centred = centred - normed * jnp.mean(scaled * normed, axis=-1, keepdims=True)
    return (centred * inverse, jnp.sum(grad_norm * normed, axis=0), jnp.sum(grad_norm, axis=0))


def gelu_tanh(values):
    return jax.nn.gelu(values, approximate=True)


def mm(left, right):
    return jnp.dot(left, right, preferred_element_type=F32)


def mm_t(left, right):
    return lax.dot_general(left, right, (((1,), (1,)), ((), ())), preferred_element_type=F32)


def mm_rows(left, right):
    return lax.dot_general(left, right, (((0,), (0,)), ((), ())), preferred_element_type=F32)


def ctx_swap(values, mask):
    count = lax.axis_size("ctx")
    return lax.ppermute(values, "ctx", [(at, at ^ mask) for at in range(count)])


def ctx_gather(values):
    chips = lax.axis_size("ctx") // 2
    mine = jnp.concatenate([values] + [ctx_swap(values, 2 * at) for at in range(1, chips)], axis=0)
    return mine, ctx_swap(mine, 1)


def ctx_scatter(even, odd):
    chips = lax.axis_size("ctx") // 2
    rows = even.shape[0] // chips
    both = even.astype(F32) + ctx_swap(odd.astype(BF16), 1).astype(F32)
    total = both[:rows]
    low = both.astype(BF16)
    for at in range(1, chips):
        total = total + ctx_swap(low[at * rows : (at + 1) * rows], 2 * at).astype(F32)
    return total


def z_masks(count):
    masks = []
    while count > 1:
        masks.append(count - 1)
        count //= 2
    return masks


def z_offsets(count):
    offsets = [0]
    for mask in z_masks(count):
        offsets = offsets + [at ^ mask for at in offsets]
    return offsets


def z_swap(values, mask):
    count = lax.axis_size("fsdp")
    return lax.ppermute(values, "fsdp", [(at, at ^ mask) for at in range(count)])


def z_gather_relative(values):
    blocks = [values]
    for mask in z_masks(lax.axis_size("fsdp")):
        blocks = blocks + [z_swap(block, mask) for block in blocks]
    return blocks


def z_gather(values, z_at):
    count = lax.axis_size("fsdp")
    blocks = z_gather_relative(values)
    out = jnp.zeros((count,) + values.shape, values.dtype)
    for offset, block in zip(z_offsets(count), blocks):
        out = lax.dynamic_update_index_in_dim(out, block, z_at ^ offset, 0)
    return out


def z_scatter(partial, z_at):
    count = lax.axis_size("fsdp")
    blocks = {
        offset: lax.dynamic_index_in_dim(partial, z_at ^ offset, 0, keepdims=False)
        for offset in z_offsets(count)
    }
    return z_scatter_relative(blocks)


def z_scatter_relative(blocks):
    count = lax.axis_size("fsdp")
    held = z_offsets(count)
    for mask in reversed(z_masks(count)):
        held = held[: len(held) // 2]
        blocks = {
            offset: blocks[offset].astype(F32)
            + z_swap(blocks[offset ^ mask].astype(BF16), mask).astype(F32)
            for offset in held
        }
    return blocks[0].astype(F32)


def z_broadcast(values, z_at, source_of):
    ctx_count, count = lax.axis_size("ctx"), lax.axis_size("fsdp")
    source = source_of(lax.axis_index("ctx"))
    known = [0]
    for mask in z_masks(count):
        pairs = [
            (c * count + (source_of(c) ^ at), c * count + (source_of(c) ^ at ^ mask))
            for c in range(ctx_count)
            for at in known
        ]
        got = lax.ppermute(values, ("ctx", "fsdp"), pairs)
        held = functools.reduce(jnp.logical_or, [z_at == (source ^ at) for at in known])
        values = jnp.where(held, values, got)
        known = known + [at ^ mask for at in known]
    return values


class Shape:
    def __init__(self, ctx_count, fsdp_count, slots, rows):
        self.ctx_count, self.fsdp_count, self.slots, self.rows = ctx_count, fsdp_count, slots, rows
        self.heads = HEADS // ctx_count
        self.block = rows * fsdp_count
        self.blocks = 2 * ctx_count
        self.keys = self.block * self.blocks
        self.tokens = slots * 2 * rows
        self.q_blocks = LANE_ROWS // (self.heads * rows)
        self.head_rows = self.q_blocks * rows
        self.q_tiles = self.blocks // self.q_blocks
        self.q_rows = self.q_tiles * LANE_ROWS
        self.chips = ctx_count // 2
        self.offsets = z_offsets(fsdp_count)


def for_blocks(shape, meta, act):
    me = meta[0]

    def step(chip, carry):
        for parity in range(2):
            first = meta[6 + (me ^ (2 * chip + parity))]
            for slot in range(shape.slots):
                for half in range(2):
                    block = first if half == 0 else shape.blocks - 1 - first
                    act(parity, chip, slot, half, block)
        return carry

    lax.fori_loop(0, shape.chips, step, 0)


def at_rows(start, size, unit):
    return pl.ds(pl.multiple_of(start, unit), size)


def q_source(shape, chip, slot, half):
    return at_rows(chip * shape.tokens + (slot * 2 + half) * shape.rows, shape.rows, shape.rows)


def q_target(shape, block, head):
    start = (block // shape.q_blocks) * LANE_ROWS + (block % shape.q_blocks) * shape.rows
    return at_rows(start + head * shape.head_rows, shape.rows, shape.rows)


def kv_source(shape, chip, order, slot, half):
    start = (chip * shape.fsdp_count + order) * shape.tokens + (slot * 2 + half) * shape.rows
    return at_rows(start, shape.rows, shape.rows)


def kv_target(shape, meta, block, order):
    start = block * shape.block + (meta[1] ^ shape.offsets[order]) * shape.rows
    return at_rows(start, shape.rows, shape.rows)


def query_bounds(shape, meta, slot, tile):
    lane = lax.broadcasted_iota(jnp.int32, (1, LANE_ROWS), 1)
    row = lane % shape.head_rows
    pos = (tile * shape.q_blocks + row // shape.rows) * shape.block + meta[1] * shape.rows + row % shape.rows
    first_end = meta[2 + 2 * slot]
    second_end = first_end + meta[3 + 2 * slot]

    def start_of(at):
        return jnp.where(at < first_end, 0, jnp.where(at < second_end, first_end, second_end))

    first_pos = tile * shape.q_blocks * shape.block + meta[1] * shape.rows
    last_pos = first_pos + (shape.q_blocks - 1) * shape.block + shape.rows - 1
    return pos, start_of(pos), start_of(first_pos) // KEY_TILE, last_pos // KEY_TILE + 1


def visible(pos, start, tile):
    key_pos = tile * KEY_TILE + lax.broadcasted_iota(jnp.int32, (KEY_TILE, LANE_ROWS), 0)
    return (key_pos <= pos) & (key_pos >= start)


def attend_kernel(shape, meta, q_even, q_odd, kv_even, kv_odd, o_even, o_odd, q_all, kv_all, o_t, lse, o_rows):
    queries, keys, outs = (q_even, q_odd), (kv_even, kv_odd), (o_even, o_odd)

    def place(parity, chip, slot, half, block):
        for head in range(shape.heads):
            q_all[slot, q_target(shape, block, head), :] = queries[parity][
                q_source(shape, chip, slot, half), head * HD : (head + 1) * HD
            ]
        for order in range(shape.fsdp_count):
            kv_all[slot, kv_target(shape, meta, block, order), :] = keys[parity][
                kv_source(shape, chip, order, slot, half), :
            ]

    for_blocks(shape, meta, place)

    def tile_step(item, carry):
        slot, tile = item // shape.q_tiles, item % shape.q_tiles
        pos, start, low, high = query_bounds(shape, meta, slot, tile)
        q_tile = q_all[slot, at_rows(tile * LANE_ROWS, LANE_ROWS, LANE_ROWS), :]

        def key_step(at, state):
            peak, total, acc = state
            part = at_rows(at * KEY_TILE, KEY_TILE, KEY_TILE)
            scores = mm_t(kv_all[slot, part, :HD], q_tile) * SCALE
            scores = jnp.where(visible(pos, start, at), scores, MASKED)
            new_peak = jnp.maximum(peak, jnp.max(scores, axis=0, keepdims=True))
            fade = jnp.exp(peak - new_peak)
            weights = jnp.exp(scores - new_peak)
            total = total * fade + jnp.sum(weights, axis=0, keepdims=True)
            acc = acc * fade + mm_rows(kv_all[slot, part, HD:], weights.astype(BF16))
            return new_peak, total, acc

        begin = (
            jnp.full((1, LANE_ROWS), MASKED, F32),
            jnp.zeros((1, LANE_ROWS), F32),
            jnp.zeros((HD, LANE_ROWS), F32),
        )
        peak, total, acc = lax.fori_loop(low, high, key_step, begin)
        acc = acc / total
        o_t[item] = acc
        lse[item] = peak + jnp.log(total)
        o_rows[slot, at_rows(tile * LANE_ROWS, LANE_ROWS, LANE_ROWS), :] = acc.T.astype(BF16)
        return carry

    lax.fori_loop(0, shape.slots * shape.q_tiles, tile_step, 0)

    def put_back(parity, chip, slot, half, block):
        for head in range(shape.heads):
            outs[parity][q_source(shape, chip, slot, half), head * HD : (head + 1) * HD] = o_rows[
                slot, q_target(shape, block, head), :
            ]

    for_blocks(shape, meta, put_back)


def attend_grad_kernel(
    shape, meta, q_all, kv_all, o_t, lse, go_even, go_odd, gq_even, gq_odd, gkv_even, gkv_odd, go_all, gq_all, gkv_all
):
    grads, g_queries, g_keys = (go_even, go_odd), (gq_even, gq_odd), (gkv_even, gkv_odd)

    def place(parity, chip, slot, half, block):
        for head in range(shape.heads):
            go_all[slot, q_target(shape, block, head), :] = grads[parity][
                q_source(shape, chip, slot, half), head * HD : (head + 1) * HD
            ]

    for_blocks(shape, meta, place)
    gkv_all[...] = jnp.zeros_like(gkv_all)

    def tile_step(item, carry):
        slot, tile = item // shape.q_tiles, item % shape.q_tiles
        pos, start, low, high = query_bounds(shape, meta, slot, tile)
        rows = at_rows(tile * LANE_ROWS, LANE_ROWS, LANE_ROWS)
        q_tile = q_all[slot, rows, :]
        go_tile = go_all[slot, rows, :]
        delta = jnp.sum(go_tile.astype(F32).T * o_t[item], axis=0, keepdims=True)
        lse_row = lse[item]

        def key_step(at, acc):
            part = at_rows(at * KEY_TILE, KEY_TILE, KEY_TILE)
            key_part, value_part = kv_all[slot, part, :HD], kv_all[slot, part, HD:]
            scores = mm_t(key_part, q_tile) * SCALE
            probs = jnp.where(visible(pos, start, at), jnp.exp(scores - lse_row), 0.0)
            g_scores = (probs * (mm_t(value_part, go_tile) - delta)).astype(BF16)
            gkv_all[slot, part, :HD] += mm(g_scores, q_tile)
            gkv_all[slot, part, HD:] += mm(probs.astype(BF16), go_tile)
            return acc + mm_rows(key_part, g_scores)

        acc = lax.fori_loop(low, high, key_step, jnp.zeros((HD, LANE_ROWS), F32))
        gq_all[slot, rows, :] = (acc * SCALE).T.astype(BF16)
        return carry

    lax.fori_loop(0, shape.slots * shape.q_tiles, tile_step, 0)

    def put_back(parity, chip, slot, half, block):
        for head in range(shape.heads):
            g_queries[parity][q_source(shape, chip, slot, half), head * HD : (head + 1) * HD] = gq_all[
                slot, q_target(shape, block, head), :
            ]
        for order in range(shape.fsdp_count):
            target = kv_target(shape, meta, block, order)
            source = kv_source(shape, chip, order, slot, half)
            g_keys[parity][source, :HD] = (gkv_all[slot, target, :HD] * SCALE).astype(BF16)
            g_keys[parity][source, HD:] = gkv_all[slot, target, HD:].astype(BF16)

    for_blocks(shape, meta, put_back)


def attend(shape, meta, q_even, q_odd, kv_even, kv_odd):
    items = shape.slots * shape.q_tiles
    q_like = jax.ShapeDtypeStruct(q_even.shape, BF16)
    pairs = items * LANE_ROWS * shape.keys // 2
    return pl.pallas_call(
        functools.partial(attend_kernel, shape),
        grid_spec=pltpu.PrefetchScalarGridSpec(
            num_scalar_prefetch=1,
            grid=(1,),
            in_specs=[pl.BlockSpec(memory_space=pltpu.VMEM)] * 4,
            out_specs=[pl.BlockSpec(memory_space=pltpu.VMEM)] * 6,
            scratch_shapes=[pltpu.VMEM((shape.slots, shape.q_rows, HD), BF16)],
        ),
        out_shape=[
            q_like,
            q_like,
            jax.ShapeDtypeStruct((shape.slots, shape.q_rows, HD), BF16),
            jax.ShapeDtypeStruct((shape.slots, shape.keys, 2 * HD), BF16),
            jax.ShapeDtypeStruct((items, HD, LANE_ROWS), F32),
            jax.ShapeDtypeStruct((items, 1, LANE_ROWS), F32),
        ],
        compiler_params=pltpu.CompilerParams(vmem_limit_bytes=56 * 2**20),
        cost_estimate=pl.CostEstimate(flops=pairs * HD * 4, transcendentals=pairs, bytes_accessed=8 * 2**20),
        name="attend",
    )(meta, q_even, q_odd, kv_even, kv_odd)


def attend_grad(shape, meta, q_all, kv_all, o_t, lse, go_even, go_odd):
    items = shape.slots * shape.q_tiles
    q_like = jax.ShapeDtypeStruct(go_even.shape, BF16)
    kv_like = jax.ShapeDtypeStruct((shape.chips * shape.fsdp_count * shape.tokens, 2 * HD), BF16)
    pairs = items * LANE_ROWS * shape.keys // 2
    return pl.pallas_call(
        functools.partial(attend_grad_kernel, shape),
        grid_spec=pltpu.PrefetchScalarGridSpec(
            num_scalar_prefetch=1,
            grid=(1,),
            in_specs=[pl.BlockSpec(memory_space=pltpu.VMEM)] * 6,
            out_specs=[pl.BlockSpec(memory_space=pltpu.VMEM)] * 4,
            scratch_shapes=[
                pltpu.VMEM((shape.slots, shape.q_rows, HD), BF16),
                pltpu.VMEM((shape.slots, shape.q_rows, HD), BF16),
                pltpu.VMEM((shape.slots, shape.keys, 2 * HD), F32),
            ],
        ),
        out_shape=[q_like, q_like, kv_like, kv_like],
        compiler_params=pltpu.CompilerParams(vmem_limit_bytes=56 * 2**20),
        cost_estimate=pl.CostEstimate(flops=pairs * HD * 10, transcendentals=pairs, bytes_accessed=10 * 2**20),
        name="attend_grad",
    )(meta, q_all, kv_all, o_t, lse, go_even, go_odd)


def spread_kernel(by_rows, meta, even_ref, odd_ref, out_ref):
    swapped = meta[0] % 2 == 1
    even, odd = even_ref[0].astype(F32), odd_ref[0].astype(F32)
    first = jnp.where(swapped, odd, even)
    second = jnp.where(swapped, even, odd)
    if by_rows:
        out_ref[0], out_ref[1] = first, second
    else:
        width = even.shape[1]
        out_ref[:, :width] = first
        out_ref[:, width:] = second


def spread_rows(meta, even, odd):
    chips, rows, columns = even.shape
    tile = min(rows, 128)
    out = pl.pallas_call(
        functools.partial(spread_kernel, True),
        grid_spec=pltpu.PrefetchScalarGridSpec(
            num_scalar_prefetch=1,
            grid=(chips, rows // tile),
            in_specs=[pl.BlockSpec((1, tile, columns), lambda k, i, m: (k ^ (m[0] // 2), i, 0))] * 2,
            out_specs=pl.BlockSpec((2, tile, columns), lambda k, i, m: (k, i, 0)),
        ),
        out_shape=jax.ShapeDtypeStruct((2 * chips, rows, columns), F32),
        compiler_params=pltpu.CompilerParams(vmem_limit_bytes=32 * 2**20),
        name="spread_rows",
    )(meta, even, odd)
    return out.reshape(2 * chips * rows, columns)


def spread_columns(meta, even, odd, groups):
    chips, rows, columns = even.shape
    width = columns // groups
    if width % 128:
        out = jnp.zeros((2 * chips, rows, groups, width), F32)
        for at in range(2 * chips):
            block = (even, odd)[at % 2][at // 2].reshape(rows, groups, width).astype(F32)
            out = lax.dynamic_update_index_in_dim(out, block, meta[0] ^ at, 0)
        return jnp.transpose(out, (1, 2, 0, 3)).reshape(rows, 2 * chips * columns)
    return pl.pallas_call(
        functools.partial(spread_kernel, False),
        grid_spec=pltpu.PrefetchScalarGridSpec(
            num_scalar_prefetch=1,
            grid=(groups, chips),
            in_specs=[pl.BlockSpec((1, rows, width), lambda g, k, m: (k ^ (m[0] // 2), 0, g))] * 2,
            out_specs=pl.BlockSpec((rows, 2 * width), lambda g, k, m: (0, g * chips + k)),
        ),
        out_shape=jax.ShapeDtypeStruct((rows, 2 * chips * columns), F32),
        compiler_params=pltpu.CompilerParams(vmem_limit_bytes=32 * 2**20),
        name="spread_columns",
    )(meta, even, odd)


def pick_block(pair_table, ctx_at, half_bit):
    ctx_total = pair_table.shape[0]
    chosen = jnp.sum(jnp.where(jnp.arange(ctx_total, dtype=jnp.int32) == ctx_at, pair_table, 0))
    return jnp.where(half_bit == 0, chosen, 2 * ctx_total - 1 - chosen)


def body(
    inputs,
    w_qkv,
    w_out,
    w_fc,
    w_proj,
    ln1_gain,
    ln1_bias,
    bias_q,
    bias_v,
    bias_out,
    ln2_gain,
    ln2_bias,
    bias_fc,
    bias_proj,
    cotangent,
    lengths,
    pair_table,
):
    slots, _, _, rows, width = inputs.shape
    ctx_count, fsdp_count = lax.axis_size("ctx"), lax.axis_size("fsdp")
    c_at, z_at = lax.axis_index("ctx"), lax.axis_index("fsdp")
    shape = Shape(ctx_count, fsdp_count, slots, rows)
    tokens, chips = shape.tokens, shape.chips
    q_width = width // ctx_count
    hidden_width = w_fc.shape[1]
    unit = hidden_width // (fsdp_count * ctx_count)
    meta = jnp.concatenate(
        [jnp.stack([c_at, z_at]).astype(jnp.int32), lengths.reshape(-1), pair_table]
    ).astype(jnp.int32)

    offsets = jnp.arange(2 * rows, dtype=jnp.int32)
    pos = (
        pick_block(pair_table, c_at, offsets // rows) * shape.block + z_at * rows + offsets % rows
    )
    live = (pos[None, :] < lengths[:, 0:1] + lengths[:, 1:2]).reshape(tokens, 1).astype(F32)

    x_low = inputs.reshape(tokens, width)
    x_even, x_odd = ctx_gather(x_low)
    vectors = [ln1_gain, ln1_bias, bias_q, bias_v, bias_out, ln2_gain, ln2_bias, bias_fc, bias_proj]
    sizes = [member.shape[0] for member in vectors]
    packed = z_gather(jnp.concatenate([member.astype(BF16) for member in vectors]), z_at)
    full, start = [], 0
    for size in sizes:
        full.append(packed[:, start : start + size].reshape(-1).astype(F32))
        start += size
    gain_one, shift_one, q_bias, v_bias, out_bias, gain_two, shift_two, fc_bias, proj_bias = full
    q_bias = lax.dynamic_slice_in_dim(q_bias, c_at * q_width, q_width)
    fc_bias = lax.dynamic_index_in_dim(
        fc_bias.reshape(fsdp_count, ctx_count, unit), c_at, 1, keepdims=False
    ).reshape(-1)

    w_kv = z_gather(w_qkv[:, width:].astype(BF16), z_at).reshape(width, 2 * HD)
    w_q = z_gather(
        lax.dynamic_slice_in_dim(w_qkv, c_at * q_width, q_width, axis=1).astype(BF16), z_at
    ).reshape(width, q_width)
    per_plane = ctx_count // fsdp_count
    w_o = z_broadcast(
        lax.dynamic_slice_in_dim(w_out, (c_at % per_plane) * q_width, q_width, axis=0).astype(BF16),
        z_at,
        lambda c: c // per_plane,
    )
    w_f = z_gather(
        lax.dynamic_index_in_dim(
            w_fc.reshape(-1, fsdp_count, ctx_count, unit), c_at, 2, keepdims=False
        )
        .reshape(-1, fsdp_count * unit)
        .astype(BF16),
        z_at,
    ).reshape(width, fsdp_count * unit)
    w_p = z_gather(
        lax.dynamic_slice_in_dim(w_proj, c_at * unit, unit, axis=0).astype(BF16), z_at
    ).reshape(fsdp_count * unit, width)

    x_own = x_low.astype(F32)
    first_norm, normed_one, inverse_one = layer_norm(x_own, gain_one, shift_one)
    kv_own = mm(first_norm.astype(BF16), w_kv)
    kv_own = jnp.concatenate([kv_own[:, :HD], kv_own[:, HD:] + v_bias], axis=1).astype(BF16)
    kv_even, kv_odd = ctx_gather(jnp.concatenate(z_gather_relative(kv_own), axis=0))
    a_even = layer_norm(x_even.astype(F32), gain_one, shift_one)[0].astype(BF16)
    a_odd = layer_norm(x_odd.astype(F32), gain_one, shift_one)[0].astype(BF16)
    q_even = (mm(a_even, w_q) + q_bias).astype(BF16)
    q_odd = (mm(a_odd, w_q) + q_bias).astype(BF16)
    o_even, o_odd, q_all, kv_all, o_t, lse = attend(shape, meta, q_even, q_odd, kv_even, kv_odd)
    branch = ctx_scatter(mm(o_even, w_o), mm(o_odd, w_o)) + out_bias
    middle = x_own + branch
    second_norm, normed_two, inverse_two = layer_norm(middle, gain_two, shift_two)

    grad_out = cotangent.reshape(tokens, width).astype(F32) * live
    grad_mlp = grad_out.astype(BF16)
    gm_even, gm_odd = ctx_gather(grad_mlp)
    cn_even, cn_odd = ctx_gather(second_norm.astype(BF16))
    acts, g_hidden, g_second, mlp = [], [], [], []
    for cn_part, gm_part in ((cn_even, gm_even), (cn_odd, gm_odd)):
        hidden = mm(cn_part, w_f) + fc_bias
        activated, pull = jax.vjp(gelu_tanh, hidden)
        acts.append(activated.astype(BF16))
        g_hidden.append(pull(mm_t(gm_part, w_p))[0].astype(BF16))
        g_second.append(mm_t(g_hidden[-1], w_f).astype(BF16))
        mlp.append(mm(acts[-1], w_p).astype(BF16))
    grad_second = ctx_scatter(*g_second)
    result = (middle + (ctx_scatter(*mlp) + proj_bias)).astype(BF16)

    def over_plane(left, right):
        return mm_rows(left[0], right[0]) + mm_rows(left[1], right[1])

    d_proj = over_plane(acts, (gm_even, gm_odd)).astype(BF16)
    d_fc = over_plane((cn_even, cn_odd), g_hidden).astype(BF16)
    d_proj = z_scatter(d_proj.reshape(fsdp_count, unit, width), z_at).astype(BF16)
    d_fc = z_scatter(d_fc.reshape(fsdp_count, -1, fsdp_count * unit), z_at).astype(BF16)

    def spread(values, by_rows, groups=1):
        even, odd = ctx_gather(values)
        even, odd = even.reshape((chips,) + values.shape), odd.reshape((chips,) + values.shape)
        return spread_rows(meta, even, odd) if by_rows else spread_columns(meta, even, odd, groups)

    grad_w_proj = spread(d_proj, True)
    grad_w_fc = spread(d_fc, False, fsdp_count)

    grad_mid_norm, grad_gain_two, grad_shift_two = norm_backward(
        grad_second, normed_two, inverse_two, gain_two
    )
    grad_middle = grad_out + grad_mid_norm
    grad_branch = grad_middle.astype(BF16)
    ga_even, ga_odd = ctx_gather(grad_branch)

    def o_blocks(from_mask):
        got = (o_even, o_odd)
        if from_mask:
            got = (ctx_swap(o_even, from_mask), ctx_swap(o_odd, from_mask))
        order = []
        for parity in range(2):
            for at in range(chips):
                source = (2 * at + parity) ^ from_mask
                part = got[source % 2]
                order.append(part[(source // 2) * tokens : (source // 2 + 1) * tokens])
        return jnp.concatenate(order, axis=0)

    ga_all = jnp.concatenate([ga_even, ga_odd], axis=0)
    ga_columns = lax.dynamic_slice_in_dim(ga_all, c_at * q_width, q_width, axis=1)
    o_full = jnp.zeros((ctx_count, ctx_count * tokens, q_width), BF16)
    for mask in range(ctx_count):
        o_full = lax.dynamic_update_index_in_dim(o_full, o_blocks(mask), c_at ^ mask, 0)
    d_out = lax.dot_general(
        o_full, ga_columns, (((1,), (0,)), ((), ())), preferred_element_type=F32
    ).astype(BF16)
    d_out = z_scatter(d_out.reshape(fsdp_count, -1, q_width), z_at).astype(BF16)
    grad_w_out = spread(d_out, False)

    go_even = mm_t(ga_even, w_o).astype(BF16)
    go_odd = mm_t(ga_odd, w_o).astype(BF16)
    gq_even, gq_odd, gkv_even, gkv_odd = attend_grad(
        shape, meta, q_all, kv_all, o_t, lse, go_even, go_odd
    )
    gkv_plane = ctx_scatter(gkv_even, gkv_odd).reshape(fsdp_count, tokens, 2 * HD)
    gkv_low = z_scatter_relative(
        {offset: gkv_plane[at] for at, offset in enumerate(shape.offsets)}
    ).astype(BF16)
    gkv_parts = ctx_gather(gkv_low)
    grad_first = ctx_scatter(mm_t(gq_even, w_q), mm_t(gq_odd, w_q)) + mm_t(gkv_low, w_kv)
    grad_in_norm, grad_gain_one, grad_shift_one = norm_backward(
        grad_first, normed_one, inverse_one, gain_one
    )
    grad_inputs = grad_middle + grad_in_norm
    d_q = over_plane((a_even, a_odd), (gq_even, gq_odd)).astype(BF16)
    d_q = z_scatter(d_q.reshape(fsdp_count, -1, q_width), z_at).astype(BF16)
    d_kv = over_plane((a_even, a_odd), gkv_parts).astype(BF16)
    d_kv = z_scatter(d_kv.reshape(fsdp_count, -1, 2 * HD), z_at).astype(BF16).astype(F32)
    grad_w_qkv = jnp.concatenate([spread(d_q, False), d_kv], axis=1)

    def column_sum(*parts):
        return sum(jnp.sum(part, axis=0, dtype=F32) for part in parts)

    g_bias_q = lax.dynamic_update_index_in_dim(
        jnp.zeros((ctx_count, q_width), F32), column_sum(gq_even, gq_odd), c_at, 0
    ).reshape(-1)
    g_bias_fc = lax.dynamic_update_index_in_dim(
        jnp.zeros((fsdp_count, ctx_count, unit), F32),
        column_sum(*g_hidden).reshape(fsdp_count, unit),
        c_at,
        1,
    ).reshape(-1)
    g_vectors = [
        grad_gain_one,
        grad_shift_one,
        g_bias_q,
        column_sum(gkv_low[:, HD:]),
        column_sum(grad_branch),
        grad_gain_two,
        grad_shift_two,
        g_bias_fc,
        column_sum(grad_mlp),
    ]
    stacked = jnp.concatenate(
        [member.reshape(fsdp_count, -1) for member in g_vectors], axis=1
    ).astype(BF16)
    own = z_scatter(stacked[:, None, :], z_at).astype(BF16)
    all_even, all_odd = ctx_gather(own)
    summed = column_sum(all_even, all_odd)
    vector_grads, start = [], 0
    for size in sizes:
        vector_grads.append(summed[start : start + size].astype(BF16).astype(F32))
        start += size
    return (
        result.reshape(inputs.shape),
        grad_inputs.reshape(inputs.shape),
        grad_w_qkv,
        grad_w_out,
        grad_w_fc,
        grad_w_proj,
        *vector_grads,
    )


def solution(mesh):
    rows_placed = P(None, "ctx", None, "fsdp", None)
    matrix, vector = P("fsdp", None), P("fsdp")
    return jax.shard_map(
        body,
        mesh=mesh,
        in_specs=(rows_placed,) + (matrix,) * 4 + (vector,) * 9 + (rows_placed, P(), P()),
        out_specs=(rows_placed, rows_placed) + (matrix,) * 4 + (vector,) * 9,
        check_vma=False,
    )
```

```python
import functools
import math

import jax
import jax.numpy as jnp
from jax import lax
from jax.experimental import pallas as pl
from jax.experimental.pallas import tpu as pltpu
from jax.sharding import PartitionSpec as P

HEADS = 16
HD = 128
NORM_EPS = 1e-05
MASKED = -1e30
KEY_TILE = 512
LANE_ROWS = 256
SCALE = 1.0 / math.sqrt(HD)
F32 = jnp.float32
BF16 = jnp.bfloat16


def layer_norm(values, gain_vec, shift_vec):
    centred = values - jnp.mean(values, axis=-1, keepdims=True)
    inverse = lax.rsqrt(jnp.mean(centred * centred, axis=-1, keepdims=True) + NORM_EPS)
    normed = centred * inverse
    return (normed * gain_vec + shift_vec, normed, inverse)


def norm_backward(grad_norm, normed, inverse, gain_vec):
    scaled = grad_norm * gain_vec
    centred = scaled - jnp.mean(scaled, axis=-1, keepdims=True)
    centred = centred - normed * jnp.mean(scaled * normed, axis=-1, keepdims=True)
    return (centred * inverse, jnp.sum(grad_norm * normed, axis=0), jnp.sum(grad_norm, axis=0))


def gelu_tanh(values):
    return jax.nn.gelu(values, approximate=True)


def mm(left, right):
    return jnp.dot(left, right, preferred_element_type=F32)


def mm_t(left, right):
    return lax.dot_general(left, right, (((1,), (1,)), ((), ())), preferred_element_type=F32)


def mm_rows(left, right):
    return lax.dot_general(left, right, (((0,), (0,)), ((), ())), preferred_element_type=F32)


def after(values, *ready):
    return lax.optimization_barrier((values, *ready))[0] if ready else values


def ctx_swap(values, mask):
    count = lax.axis_size("ctx")
    return lax.ppermute(values, "ctx", [(at, at ^ mask) for at in range(count)])


def ctx_gather(values, ready=()):
    chips = lax.axis_size("ctx") // 2
    mine = jnp.concatenate([values] + [ctx_swap(values, 2 * at) for at in range(1, chips)], axis=0)
    mine = after(mine, *ready)
    return mine, ctx_swap(mine, 1)


def ctx_gather_all(values):
    return jnp.concatenate(ctx_gather(values), axis=0)


def ctx_scatter(even, odd, ready=(), finish=()):
    chips = lax.axis_size("ctx") // 2
    rows = even.shape[0] // chips
    both = even.astype(F32) + ctx_swap(odd.astype(BF16), 1).astype(F32)
    total = both[:rows]
    low = after(both.astype(BF16), *ready)
    for at in range(1, chips):
        got = ctx_swap(low[at * rows : (at + 1) * rows], 2 * at)
        total = total + after(got, *finish).astype(F32)
    return total


def ctx_gather_small(values):
    chips = lax.axis_size("ctx") // 2
    held, mask = values, 2
    while mask < 2 * chips:
        held = jnp.concatenate([held, ctx_swap(held, mask)], axis=0)
        mask *= 2
    return held, ctx_swap(held, 1)


def chip_masks(side):
    masks, mask = [], lax.axis_size("ctx") // 2
    while mask > 1:
        masks.append(mask)
        mask //= 2
    return masks[1:] + masks[:1] if side else masks


def ctx_gather_halves(first, second, wait=lambda values: values, last=lambda values: values):
    held, offsets = [first[None], second[None]], [[0], [0]]
    steps = len(chip_masks(0))
    for step in range(steps):
        sent = []
        for side in range(2):
            mask = chip_masks(side)[step]
            sent.append((ctx_swap(held[side], mask), [at ^ mask for at in offsets[side]]))
        if step < steps - 1:
            for side in range(2):
                held[side] = jnp.concatenate([held[side], wait(sent[side][0])], axis=0)
                offsets[side] = offsets[side] + sent[side][1]
    gathered = []
    for side in range(2):
        parts = [(held[side], offsets[side]), (last(sent[side][0]), sent[side][1])]
        gathered.append(
            parts + [(ctx_swap(block, 1), [at ^ 1 for at in order]) for block, order in parts]
        )
    return gathered


def in_order(parts, parity):
    blocks = {
        offset: values[at]
        for values, order in parts
        for at, offset in enumerate(order)
        if offset % 2 == parity
    }
    return jnp.concatenate([blocks[offset] for offset in sorted(blocks)], axis=0)


def ctx_exchange(values):
    return lax.all_to_all(values, "ctx", 0, 0, tiled=True)


def z_masks(count):
    masks = []
    while count > 1:
        masks.append(count - 1)
        count //= 2
    return masks


def z_offsets(count):
    offsets = [0]
    for mask in z_masks(count):
        offsets = offsets + [at ^ mask for at in offsets]
    return offsets


def z_swap(values, mask):
    count = lax.axis_size("fsdp")
    return lax.ppermute(values, "fsdp", [(at, at ^ mask) for at in range(count)])


def z_gather_steps(values):
    held = values[None]
    own = z_swap(held, 1)
    for mask in z_masks(lax.axis_size("fsdp"))[:-1]:
        held = jnp.concatenate([held, z_swap(held, mask)], axis=0)
    return held, own


def z_gather_finish(held, own):
    if held.shape[0] == 1:
        return [held, own]
    return [held, own, z_swap(held[1:], 1)]


def z_gather_parts(values):
    return z_gather_finish(*z_gather_steps(values))


def z_gather_held(values):
    held = values[None]
    for mask in z_masks(lax.axis_size("fsdp"))[:-1]:
        held = jnp.concatenate([held, z_swap(held, mask)], axis=0)
    return held


def z_scatter_stacked(stacked):
    for mask in reversed(z_masks(lax.axis_size("fsdp"))):
        half = stacked.shape[0] // 2
        sent = z_swap(stacked[half:].astype(BF16), mask)
        stacked = stacked[:half].astype(F32) + sent.astype(F32)
    return stacked[0]


def z_gather_queued(values):
    return lax.all_gather(values, "fsdp", axis=0, tiled=True)


def z_scatter_queued(values):
    return lax.psum_scatter(values, "fsdp", scatter_dimension=0, tiled=True)


def place_kernel(plan, n_in, meta, *refs):
    ins, outs = refs[:n_in], refs[n_in:]
    for source, rows_in, target, rows_out in plan(meta):
        outs[target][rows_out] = ins[source][rows_in]


def place_blocks(meta, sources, outs, plan, name):
    return pl.pallas_call(
        functools.partial(place_kernel, plan, len(sources)),
        grid_spec=pltpu.PrefetchScalarGridSpec(
            num_scalar_prefetch=1,
            grid=(1,),
            in_specs=[pl.BlockSpec(memory_space=pltpu.VMEM)] * len(sources),
            out_specs=[pl.BlockSpec(memory_space=pltpu.VMEM)] * len(outs),
        ),
        out_shape=[jax.ShapeDtypeStruct(out, sources[0].dtype) for out in outs],
        compiler_params=pltpu.CompilerParams(vmem_limit_bytes=56 * 2**20),
        name=name,
    )(meta, *sources)


class Shape:
    def __init__(self, ctx_count, fsdp_count, slots, rows):
        self.ctx_count, self.fsdp_count, self.slots, self.rows = ctx_count, fsdp_count, slots, rows
        self.heads = HEADS // ctx_count
        self.block = rows * fsdp_count
        self.blocks = 2 * ctx_count
        self.keys = self.block * self.blocks
        self.tokens = slots * 2 * rows
        self.q_blocks = LANE_ROWS // (self.heads * rows)
        self.head_rows = self.q_blocks * rows
        self.q_tiles = self.blocks // self.q_blocks
        self.q_rows = self.q_tiles * LANE_ROWS
        self.chips = ctx_count // 2
        self.offsets = z_offsets(fsdp_count)


    def part_starts(self, count):
        half = self.fsdp_count // 2
        return [0, half, half + 1][:count]

    def part_of(self, at, count):
        starts = self.part_starts(count)
        part = max(index for index, start in enumerate(starts) if at >= start)
        return part, at - starts[part]


def for_blocks(shape, meta, act):
    me = meta[0]

    def step(chip, carry):
        for parity in range(2):
            first = meta[6 + (me ^ (2 * chip + parity))]
            for slot in range(shape.slots):
                for half in range(2):
                    block = first if half == 0 else shape.blocks - 1 - first
                    act(parity, chip, slot, half, block)
        return carry

    lax.fori_loop(0, shape.chips, step, 0)


def at_rows(start, size, unit):
    return pl.ds(pl.multiple_of(start, unit), size)


def q_source(shape, chip, slot, half):
    return at_rows(chip * shape.tokens + (slot * 2 + half) * shape.rows, shape.rows, shape.rows)


def q_target(shape, block, head):
    start = (block // shape.q_blocks) * LANE_ROWS + (block % shape.q_blocks) * shape.rows
    return at_rows(start + head * shape.head_rows, shape.rows, shape.rows)


def kv_source(shape, chip, order, slot, half):
    start = (chip * shape.fsdp_count + order) * shape.tokens + (slot * 2 + half) * shape.rows
    return at_rows(start, shape.rows, shape.rows)


def kv_target(shape, meta, block, order):
    start = block * shape.block + (meta[1] ^ shape.offsets[order]) * shape.rows
    return at_rows(start, shape.rows, shape.rows)


def query_bounds(shape, meta, slot, tile):
    lane = lax.broadcasted_iota(jnp.int32, (1, LANE_ROWS), 1)
    row = lane % shape.head_rows
    pos = (tile * shape.q_blocks + row // shape.rows) * shape.block + meta[1] * shape.rows + row % shape.rows
    first_end = meta[2 + 2 * slot]
    second_end = first_end + meta[3 + 2 * slot]

    def start_of(at):
        return jnp.where(at < first_end, 0, jnp.where(at < second_end, first_end, second_end))

    first_pos = tile * shape.q_blocks * shape.block + meta[1] * shape.rows
    last_pos = first_pos + (shape.q_blocks - 1) * shape.block + shape.rows - 1
    return pos, start_of(pos), start_of(first_pos) // KEY_TILE, last_pos // KEY_TILE + 1


def visible(pos, start, tile):
    key_pos = tile * KEY_TILE + lax.broadcasted_iota(jnp.int32, (KEY_TILE, LANE_ROWS), 0)
    return (key_pos <= pos) & (key_pos >= start)


def device_rows(shape, meta, parity, chip, slot, half):
    device = meta[0] ^ (2 * chip + parity)
    return at_rows(device * shape.tokens + (slot * 2 + half) * shape.rows, shape.rows, shape.rows)


def attend_kernel(shape, meta, q_even, q_odd, kv_even, kv_odd, o_out, q_all, kv_all, o_t, lse, o_rows):
    queries, keys = (q_even, q_odd), (kv_even, kv_odd)

    def place(parity, chip, slot, half, block):
        for head in range(shape.heads):
            q_all[slot, q_target(shape, block, head), :] = queries[parity][
                q_source(shape, chip, slot, half), head * HD : (head + 1) * HD
            ]
        for order in range(shape.fsdp_count):
            kv_all[slot, kv_target(shape, meta, block, order), :] = keys[parity][
                kv_source(shape, chip, order, slot, half), :
            ]

    for_blocks(shape, meta, place)

    def tile_step(item, carry):
        slot, tile = item // shape.q_tiles, item % shape.q_tiles
        pos, start, low, high = query_bounds(shape, meta, slot, tile)
        q_tile = q_all[slot, at_rows(tile * LANE_ROWS, LANE_ROWS, LANE_ROWS), :]

        def key_step(at, state):
            peak, total, acc = state
            part = at_rows(at * KEY_TILE, KEY_TILE, KEY_TILE)
            scores = mm_t(kv_all[slot, part, :HD], q_tile) * SCALE
            scores = jnp.where(visible(pos, start, at), scores, MASKED)
            new_peak = jnp.maximum(peak, jnp.max(scores, axis=0, keepdims=True))
            fade = jnp.exp(peak - new_peak)
            weights = jnp.exp(scores - new_peak)
            total = total * fade + jnp.sum(weights, axis=0, keepdims=True)
            acc = acc * fade + mm_rows(kv_all[slot, part, HD:], weights.astype(BF16))
            return new_peak, total, acc

        begin = (
            jnp.full((1, LANE_ROWS), MASKED, F32),
            jnp.zeros((1, LANE_ROWS), F32),
            jnp.zeros((HD, LANE_ROWS), F32),
        )
        peak, total, acc = lax.fori_loop(low, high, key_step, begin)
        acc = acc / total
        o_t[item] = acc
        lse[item] = peak + jnp.log(total)
        o_rows[slot, at_rows(tile * LANE_ROWS, LANE_ROWS, LANE_ROWS), :] = acc.T.astype(BF16)
        return carry

    lax.fori_loop(0, shape.slots * shape.q_tiles, tile_step, 0)

    def put_back(parity, chip, slot, half, block):
        for head in range(shape.heads):
            o_out[device_rows(shape, meta, parity, chip, slot, half), head * HD : (head + 1) * HD] = o_rows[
                slot, q_target(shape, block, head), :
            ]

    for_blocks(shape, meta, put_back)


def attend_grad_kernel(
    shape, meta, q_all, kv_all, o_t, lse, grads, gq_even, gq_odd, gkv_even, gkv_odd, ga_even, ga_odd, go_all, gq_all, gkv_all
):
    g_queries, g_keys, g_branch = (gq_even, gq_odd), (gkv_even, gkv_odd), (ga_even, ga_odd)

    def place(parity, chip, slot, half, block):
        source = device_rows(shape, meta, parity, chip, slot, half)
        for head in range(shape.heads):
            go_all[slot, q_target(shape, block, head), :] = grads[source, head * HD : (head + 1) * HD]
        g_branch[parity][q_source(shape, chip, slot, half), :] = grads[source, shape.heads * HD :]

    for_blocks(shape, meta, place)
    gkv_all[...] = jnp.zeros_like(gkv_all)

    def tile_step(item, carry):
        slot, tile = item // shape.q_tiles, item % shape.q_tiles
        pos, start, low, high = query_bounds(shape, meta, slot, tile)
        rows = at_rows(tile * LANE_ROWS, LANE_ROWS, LANE_ROWS)
        q_tile = q_all[slot, rows, :]
        go_tile = go_all[slot, rows, :]
        delta = jnp.sum(go_tile.astype(F32).T * o_t[item], axis=0, keepdims=True)
        lse_row = lse[item]

        def key_step(at, acc):
            part = at_rows(at * KEY_TILE, KEY_TILE, KEY_TILE)
            key_part, value_part = kv_all[slot, part, :HD], kv_all[slot, part, HD:]
            scores = mm_t(key_part, q_tile) * SCALE
            probs = jnp.where(visible(pos, start, at), jnp.exp(scores - lse_row), 0.0)
            g_scores = (probs * (mm_t(value_part, go_tile) - delta)).astype(BF16)
            gkv_all[slot, part, :HD] += mm(g_scores, q_tile)
            gkv_all[slot, part, HD:] += mm(probs.astype(BF16), go_tile)
            return acc + mm_rows(key_part, g_scores)

        acc = lax.fori_loop(low, high, key_step, jnp.zeros((HD, LANE_ROWS), F32))
        gq_all[slot, rows, :] = (acc * SCALE).T.astype(BF16)
        return carry

    lax.fori_loop(0, shape.slots * shape.q_tiles, tile_step, 0)

    def put_back(parity, chip, slot, half, block):
        for head in range(shape.heads):
            g_queries[parity][q_source(shape, chip, slot, half), head * HD : (head + 1) * HD] = gq_all[
                slot, q_target(shape, block, head), :
            ]
        for order in range(shape.fsdp_count):
            target = kv_target(shape, meta, block, order)
            source = kv_source(shape, chip, order, slot, half)
            g_keys[parity][source, :HD] = (gkv_all[slot, target, :HD] * SCALE).astype(BF16)
            g_keys[parity][source, HD:] = gkv_all[slot, target, HD:].astype(BF16)

    for_blocks(shape, meta, put_back)


def attend(shape, meta, q_even, q_odd, kv_even, kv_odd):
    items = shape.slots * shape.q_tiles
    pairs = items * LANE_ROWS * shape.keys // 2
    return pl.pallas_call(
        functools.partial(attend_kernel, shape),
        grid_spec=pltpu.PrefetchScalarGridSpec(
            num_scalar_prefetch=1,
            grid=(1,),
            in_specs=[pl.BlockSpec(memory_space=pltpu.VMEM)] * 4,
            out_specs=[pl.BlockSpec(memory_space=pltpu.VMEM)] * 5,
            scratch_shapes=[pltpu.VMEM((shape.slots, shape.q_rows, HD), BF16)],
        ),
        out_shape=[
            jax.ShapeDtypeStruct((shape.ctx_count * shape.tokens, shape.heads * HD), BF16),
            jax.ShapeDtypeStruct((shape.slots, shape.q_rows, HD), BF16),
            jax.ShapeDtypeStruct((shape.slots, shape.keys, 2 * HD), BF16),
            jax.ShapeDtypeStruct((items, HD, LANE_ROWS), F32),
            jax.ShapeDtypeStruct((items, 1, LANE_ROWS), F32),
        ],
        compiler_params=pltpu.CompilerParams(vmem_limit_bytes=56 * 2**20),
        cost_estimate=pl.CostEstimate(flops=pairs * HD * 4, transcendentals=pairs, bytes_accessed=8 * 2**20),
        name="attend",
    )(meta, q_even, q_odd, kv_even, kv_odd)


def attend_grad(shape, meta, q_all, kv_all, o_t, lse, grads):
    items = shape.slots * shape.q_tiles
    q_like = jax.ShapeDtypeStruct((shape.chips * shape.tokens, shape.heads * HD), BF16)
    kv_like = jax.ShapeDtypeStruct((shape.chips * shape.fsdp_count * shape.tokens, 2 * HD), BF16)
    pairs = items * LANE_ROWS * shape.keys // 2
    return pl.pallas_call(
        functools.partial(attend_grad_kernel, shape),
        grid_spec=pltpu.PrefetchScalarGridSpec(
            num_scalar_prefetch=1,
            grid=(1,),
            in_specs=[pl.BlockSpec(memory_space=pltpu.VMEM)] * 5,
            out_specs=[pl.BlockSpec(memory_space=pltpu.VMEM)] * 6,
            scratch_shapes=[
                pltpu.VMEM((shape.slots, shape.q_rows, HD), BF16),
                pltpu.VMEM((shape.slots, shape.q_rows, HD), BF16),
                pltpu.VMEM((shape.slots, shape.keys, 2 * HD), F32),
            ],
        ),
        out_shape=[q_like, q_like, kv_like, kv_like, q_like, q_like],
        compiler_params=pltpu.CompilerParams(vmem_limit_bytes=56 * 2**20),
        cost_estimate=pl.CostEstimate(flops=pairs * HD * 10, transcendentals=pairs, bytes_accessed=10 * 2**20),
        name="attend_grad",
    )(meta, q_all, kv_all, o_t, lse, grads)


def block_of(shape, parts, at):
    part, block = shape.part_of(at, len(parts))
    return parts[part][block]


def gelu_parts(values):
    root = math.sqrt(2.0 / math.pi)
    return jnp.tanh(root * (values + 0.044715 * (values * values * values)))


def hidden_kernel(shape, meta, rows_ref, bias_ref, *refs):
    parts, (hidden_ref, act_ref) = refs[:-2], refs[-2:]
    depth = parts[0].shape[1]
    total = bias_ref[...]
    for at, offset in enumerate(shape.offsets):
        part = pl.ds(pl.multiple_of((meta[1] ^ offset) * depth, depth), depth)
        total = total + mm(rows_ref[:, part], block_of(shape, parts, at))
    hidden_ref[...] = total
    act_ref[...] = (0.5 * total * (1.0 + gelu_parts(total))).astype(BF16)


def feed_hidden(shape, meta, rows, parts, bias):
    count, width = rows.shape
    _, depth, columns = parts[0].shape
    tile = 256
    weights = [
        pl.BlockSpec((part.shape[0], depth, tile), lambda i, m: (0, 0, i)) for part in parts
    ]
    out = pl.BlockSpec((count, tile), lambda i, m: (0, i))
    return pl.pallas_call(
        functools.partial(hidden_kernel, shape),
        grid_spec=pltpu.PrefetchScalarGridSpec(
            num_scalar_prefetch=1,
            grid=(columns // tile,),
            in_specs=[
                pl.BlockSpec((count, width), lambda i, m: (0, 0)),
                pl.BlockSpec((1, tile), lambda i, m: (0, i)),
                *weights,
            ],
            out_specs=[out, out],
        ),
        out_shape=[
            jax.ShapeDtypeStruct((count, columns), F32),
            jax.ShapeDtypeStruct((count, columns), BF16),
        ],
        compiler_params=pltpu.CompilerParams(vmem_limit_bytes=56 * 2**20),
        cost_estimate=pl.CostEstimate(
            flops=2 * count * width * columns,
            transcendentals=count * columns,
            bytes_accessed=2 * (count * width + width * columns) + 6 * count * columns,
        ),
        name="feed_hidden",
    )(meta, rows, bias, *parts)


def hidden_grad_kernel(shape, meta, grads_ref, hidden_ref, *refs):
    parts, (out_ref, sum_ref) = refs[:-2], refs[-2:]
    at = pl.program_id(0)
    weights = parts[0][0]
    for part, start in zip(parts[1:], shape.part_starts(len(parts))[1:]):
        weights = jnp.where(at < start, weights, part[0])
    values = hidden_ref[...]
    tanh = gelu_parts(values)
    root = math.sqrt(2.0 / math.pi)
    slope = 0.5 * (1.0 + tanh) + (0.5 * root) * values * (1.0 - tanh * tanh) * (
        1.0 + (3.0 * 0.044715) * (values * values)
    )
    low = (mm_t(grads_ref[...], weights) * slope).astype(BF16)
    out_ref[...] = low
    sum_ref[...] = jnp.sum(low.astype(F32), axis=0, keepdims=True)


def relative(shape, meta, at):
    place = shape.offsets[0]
    for index, offset in enumerate(shape.offsets):
        place = jnp.where(at == index, offset, place)
    return meta[1] ^ place


def feed_hidden_grad(shape, meta, grads, hidden, parts):
    count, width = grads.shape
    half, unit, _ = parts[0].shape
    if unit % 128:
        weights = jnp.zeros((2 * half, unit, width), BF16)
        for at, offset in enumerate(shape.offsets):
            weights = lax.dynamic_update_index_in_dim(
                weights, block_of(shape, parts, at), meta[1] ^ offset, 0
            )
        pull = jax.vjp(gelu_tanh, hidden)[1]
        out = pull(mm_t(grads, weights.reshape(-1, width)))[0].astype(BF16)
        return out, jnp.sum(out, axis=0, dtype=F32, keepdims=True)
    columns = 2 * half * unit
    place = lambda i, m: (0, relative(shape, m, i))
    return pl.pallas_call(
        functools.partial(hidden_grad_kernel, shape),
        grid_spec=pltpu.PrefetchScalarGridSpec(
            num_scalar_prefetch=1,
            grid=(2 * half,),
            in_specs=[
                pl.BlockSpec((count, width), lambda i, m: (0, 0)),
                pl.BlockSpec((count, unit), place),
                *[
                    pl.BlockSpec(
                        (1, unit, width),
                        lambda i, m, start=start, last=part.shape[0] - 1: (
                            jnp.clip(i - start, 0, last),
                            0,
                            0,
                        ),
                    )
                    for part, start in zip(parts, shape.part_starts(len(parts)))
                ],
            ],
            out_specs=[pl.BlockSpec((count, unit), place), pl.BlockSpec((1, unit), place)],
        ),
        out_shape=[
            jax.ShapeDtypeStruct((count, columns), BF16),
            jax.ShapeDtypeStruct((1, columns), F32),
        ],
        compiler_params=pltpu.CompilerParams(vmem_limit_bytes=56 * 2**20),
        cost_estimate=pl.CostEstimate(
            flops=2 * count * width * columns,
            transcendentals=count * columns,
            bytes_accessed=2 * (count * width + width * columns) + 6 * count * columns,
        ),
        name="feed_hidden_grad",
    )(meta, grads, hidden, *parts)


def feed_blocks_kernel(shape, grad, meta, rows_ref, *refs):
    parts, out_ref = refs[:-1], refs[-1]
    for at, offset in enumerate(shape.offsets):
        block = block_of(shape, parts, at)
        size = block.shape[0]
        part = pl.ds(pl.multiple_of((meta[1] ^ offset) * size, size), size)
        if grad:
            out_ref[:, part] = mm_t(rows_ref[...], block).astype(BF16)
        elif at == 0:
            total = mm(rows_ref[:, part], block)
        else:
            total = total + mm(rows_ref[:, part], block)
    if not grad:
        out_ref[...] = total.astype(BF16)


def feed_blocks(shape, meta, rows, parts, side, count, grad):
    half, size, columns = parts[0].shape
    width = 2 * half * size if grad else columns
    tile = 256
    if not grad and size % 128:
        weights = jnp.zeros((2 * half, size, columns), BF16)
        for at, offset in enumerate(shape.offsets):
            weights = lax.dynamic_update_index_in_dim(
                weights, block_of(shape, parts, at), meta[1] ^ offset, 0
            )
        rows = rows[side * count : (side + 1) * count]
        return mm(rows, weights.reshape(-1, columns)).astype(BF16)
    steps = count // tile
    weights = [pl.BlockSpec(part.shape, lambda i, m: (0, 0, 0)) for part in parts]
    return pl.pallas_call(
        functools.partial(feed_blocks_kernel, shape, grad),
        grid_spec=pltpu.PrefetchScalarGridSpec(
            num_scalar_prefetch=1,
            grid=(steps,),
            in_specs=[
                pl.BlockSpec((tile, rows.shape[1]), lambda i, m: (side * steps + i, 0)),
                *weights,
            ],
            out_specs=pl.BlockSpec((tile, width), lambda i, m: (i, 0)),
        ),
        out_shape=jax.ShapeDtypeStruct((count, width), BF16),
        compiler_params=pltpu.CompilerParams(vmem_limit_bytes=56 * 2**20),
        cost_estimate=pl.CostEstimate(
            flops=2 * count * rows.shape[1] * width,
            transcendentals=0,
            bytes_accessed=2 * (count + width) * rows.shape[1] + 2 * count * width,
        ),
        name="feed_grad_rows" if grad else "feed_rows",
    )(meta, rows, *parts)


def branch_kernel(layout, grad, meta, rows_ref, *refs):
    parts, out_ref = refs[:-1], refs[-1]
    out_ref[...] = jnp.zeros_like(out_ref)
    for part, (ctx_order, z_order) in zip(parts, layout):
        depth, columns = part.shape[2], part.shape[3]
        for at, ctx_offset in enumerate(ctx_order):
            column = pl.ds(pl.multiple_of((meta[0] ^ ctx_offset) * columns, columns), columns)
            for order, z_offset in enumerate(z_order):
                row = pl.ds(pl.multiple_of((meta[1] ^ z_offset) * depth, depth), depth)
                if grad:
                    out_ref[:, row] += mm_t(rows_ref[:, column], part[at, order])
                else:
                    out_ref[:, column] += mm(rows_ref[:, row], part[at, order])


def times_blocks(meta, rows, parts, layout, grad):
    return pl.pallas_call(
        functools.partial(branch_kernel, layout, grad),
        grid_spec=pltpu.PrefetchScalarGridSpec(
            num_scalar_prefetch=1,
            grid=(1,),
            in_specs=[pl.BlockSpec(memory_space=pltpu.VMEM)] * (1 + len(parts)),
            out_specs=pl.BlockSpec(memory_space=pltpu.VMEM),
        ),
        out_shape=jax.ShapeDtypeStruct(rows.shape, F32),
        compiler_params=pltpu.CompilerParams(vmem_limit_bytes=56 * 2**20),
        cost_estimate=pl.CostEstimate(
            flops=2 * rows.shape[0] * rows.shape[1] ** 2,
            transcendentals=0,
            bytes_accessed=2 * rows.shape[1] ** 2,
        ),
        name="branch_grad" if grad else "branch",
    )(meta, rows, *parts)


def spread_rows_kernel(pieces, steps, meta, *refs):
    out_ref = refs[-1]
    for piece, blocks in enumerate(pieces):

        @pl.when(pl.program_id(0) // steps == piece)
        def _(blocks=blocks):
            for source, block, offset in blocks:
                rows = refs[source].shape[1]
                start = pl.multiple_of((meta[0] ^ offset) * rows, rows)
                out_ref[pl.ds(start, rows), :] = refs[source][block].astype(F32)


def spread_rows(meta, gathered):
    tile = 256
    members, specs, pieces = [], [], []
    for piece, parts in enumerate(gathered):
        blocks = []
        for values, order in parts:
            count, rows, columns = values.shape
            steps = columns // tile
            blocks += [(len(members), at, offset) for at, offset in enumerate(order)]
            members.append(values)

            def place(i, m, piece=piece, steps=steps):
                return (0, 0, jnp.clip(i - piece * steps, 0, steps - 1))

            specs.append(pl.BlockSpec((count, rows, tile), place))
        pieces.append(blocks)
    total = len(pieces[0]) * rows
    return pl.pallas_call(
        functools.partial(spread_rows_kernel, pieces, steps),
        grid_spec=pltpu.PrefetchScalarGridSpec(
            num_scalar_prefetch=1,
            grid=(len(pieces) * steps,),
            in_specs=specs,
            out_specs=pl.BlockSpec((total, tile), lambda i, m: (0, i)),
        ),
        out_shape=jax.ShapeDtypeStruct((total, len(pieces) * columns), F32),
        compiler_params=pltpu.CompilerParams(vmem_limit_bytes=48 * 2**20),
        name="spread_rows",
    )(meta, *members)


def spread_kernel(moves, extras, outs, meta, *refs):
    outs = refs[len(refs) - outs :]
    for source, block, columns, offset, out, start, step, size in moves:
        target = pl.multiple_of(start + (meta[0] ^ offset) * step, size)
        outs[out][:, pl.ds(target, size)] = refs[source][block, :, columns].astype(F32)
    for source, out in extras:
        width = refs[source].shape[1]
        outs[out][:, outs[out].shape[1] - width :] = refs[source][...]


def spread_columns(meta, gathered, groups, joined, extra=None):
    pieces = len(gathered)
    rows = gathered[0][0][0].shape[1]
    width = gathered[0][0][0].shape[2] // groups
    count = sum(len(order) for _, order in gathered[0])
    if width % 128:
        results = []
        for parts in gathered:
            out = jnp.zeros((count, rows, groups, width), F32)
            for values, order in parts:
                for at, offset in enumerate(order):
                    block = values[at].reshape(rows, groups, width).astype(F32)
                    out = lax.dynamic_update_index_in_dim(out, block, meta[0] ^ offset, 0)
            results.append(jnp.transpose(out, (1, 2, 0, 3)).reshape(rows, -1))
        return [jnp.concatenate(results, axis=1)]
    members, moves = [], []
    for piece, parts in enumerate(gathered):
        for values, order in parts:
            for at, offset in enumerate(order):
                for group in range(groups):
                    start = ((piece if joined else 0) * groups + group) * count * width
                    columns = slice(group * width, (group + 1) * width)
                    out = 0 if joined else piece
                    moves.append((len(members), at, columns, offset, out, start, width, width))
            members.append(values)
    sizes = [groups * count * width * pieces] if joined else [groups * count * width] * pieces
    tile = min(rows, 64)
    in_specs = [
        pl.BlockSpec((member.shape[0], tile, groups * width), lambda i, m: (0, i, 0))
        for member in members
    ]
    extras = []
    if extra is not None:
        extras = [(len(members), 0)]
        members.append(extra)
        in_specs.append(pl.BlockSpec((tile, extra.shape[1]), lambda i, m: (i, 0)))
        sizes[0] += extra.shape[1]
    return pl.pallas_call(
        functools.partial(spread_kernel, moves, extras, len(sizes)),
        grid_spec=pltpu.PrefetchScalarGridSpec(
            num_scalar_prefetch=1,
            grid=(rows // tile,),
            in_specs=in_specs,
            out_specs=[pl.BlockSpec((tile, size), lambda i, m: (i, 0)) for size in sizes],
        ),
        out_shape=[jax.ShapeDtypeStruct((rows, size), F32) for size in sizes],
        compiler_params=pltpu.CompilerParams(vmem_limit_bytes=48 * 2**20),
        name="spread_columns",
    )(meta, *members)


def pick_block(pair_table, ctx_at, half_bit):
    ctx_total = pair_table.shape[0]
    chosen = jnp.sum(jnp.where(jnp.arange(ctx_total, dtype=jnp.int32) == ctx_at, pair_table, 0))
    return jnp.where(half_bit == 0, chosen, 2 * ctx_total - 1 - chosen)


def body(
    inputs,
    w_qkv,
    w_out,
    w_fc,
    w_proj,
    ln1_gain,
    ln1_bias,
    bias_q,
    bias_v,
    bias_out,
    ln2_gain,
    ln2_bias,
    bias_fc,
    bias_proj,
    cotangent,
    lengths,
    pair_table,
):
    slots, _, _, rows, width = inputs.shape
    ctx_count, fsdp_count = lax.axis_size("ctx"), lax.axis_size("fsdp")
    c_at, z_at = lax.axis_index("ctx"), lax.axis_index("fsdp")
    shape = Shape(ctx_count, fsdp_count, slots, rows)
    tokens, chips = shape.tokens, shape.chips
    q_width = width // ctx_count
    shard = width // fsdp_count
    hidden_width = w_fc.shape[1]
    unit = hidden_width // (fsdp_count * ctx_count)
    meta = jnp.concatenate(
        [jnp.stack([c_at, z_at]).astype(jnp.int32), lengths.reshape(-1), pair_table]
    ).astype(jnp.int32)

    offsets = jnp.arange(2 * rows, dtype=jnp.int32)
    pos = (
        pick_block(pair_table, c_at, offsets // rows) * shape.block + z_at * rows + offsets % rows
    )
    live = (pos[None, :] < lengths[:, 0:1] + lengths[:, 1:2]).reshape(tokens, 1).astype(F32)

    x_low = inputs.reshape(tokens, width)
    grad_out = cotangent.reshape(tokens, width).astype(F32) * live
    grad_mlp = grad_out.astype(BF16)
    pack_width = q_width + 2 * HD
    w_first = jnp.concatenate(
        [lax.dynamic_slice_in_dim(w_qkv, c_at * q_width, q_width, axis=1), w_qkv[:, width:]], axis=1
    ).astype(BF16)
    vectors = [ln1_gain, ln1_bias, bias_q, bias_v, bias_out, ln2_gain, ln2_bias, bias_fc, bias_proj]
    sizes = [member.shape[0] for member in vectors]
    vector_rows = 16 * math.ceil(sum(sizes) / (16 * HD))
    packed = jnp.concatenate(
        [member.astype(BF16) for member in vectors]
        + [jnp.zeros((vector_rows * HD - sum(sizes),), BF16)]
    ).reshape(vector_rows, HD)
    x_even, x_odd = ctx_gather(after(x_low, w_first))
    half = fsdp_count // 2
    first_held, first_own = z_gather_steps(w_first)
    first_blocks = z_gather_finish(first_held, first_own)
    vector_held = z_gather_held(after(packed, first_held))
    vector_blocks = [vector_held, z_swap(vector_held, 1)]

    def first_plan(ref):
        moves = []
        for at, offset in enumerate(shape.offsets):
            owner, (part, block) = ref[1] ^ offset, shape.part_of(at, len(first_blocks))
            weight_rows = pl.ds(pl.multiple_of(owner * shard, shard), shard)
            q_part, kv_part = pl.ds(0, q_width), pl.ds(q_width, 2 * HD)
            moves += [
                (part, (block, slice(None), q_part), 0, (weight_rows, slice(None))),
                (part, (block, slice(None), kv_part), 1, (weight_rows, slice(None))),
                (len(first_blocks) + at // half, (at % half,), 2, (owner,)),
            ]
        return moves

    w_q, w_kv, packed = place_blocks(
        meta,
        [*first_blocks, *vector_blocks],
        [(width, q_width), (width, 2 * HD), (fsdp_count, vector_rows, HD)],
        first_plan,
        "place_first",
    )
    packed = packed.reshape(fsdp_count, -1)
    full, start = [], 0
    for size in sizes:
        full.append(packed[:, start : start + size].reshape(-1).astype(F32))
        start += size
    gain_one, shift_one, q_bias, v_bias, out_bias, gain_two, shift_two, fc_bias, proj_bias = full
    q_bias = lax.dynamic_slice_in_dim(q_bias, c_at * q_width, q_width)
    fc_bias = lax.dynamic_index_in_dim(
        fc_bias.reshape(fsdp_count, ctx_count, unit), c_at, 1, keepdims=False
    )

    x_own = x_low.astype(F32)
    first_norm, normed_one, inverse_one = layer_norm(x_own, gain_one, shift_one)
    kv_own = mm(first_norm.astype(BF16), w_kv)
    kv_own = jnp.concatenate([kv_own[:, :HD], kv_own[:, HD:] + v_bias], axis=1).astype(BF16)
    kv_z = jnp.concatenate(z_gather_parts(kv_own), axis=0).reshape(fsdp_count * tokens, 2 * HD)
    kv_even, kv_odd = ctx_gather(kv_z)

    out_parts = z_gather_parts(
        after(lax.dynamic_slice_in_dim(w_out, c_at * q_width, q_width, axis=1).astype(BF16), kv_z)
    )

    fc_own = jnp.concatenate(
        [
            lax.dynamic_slice_in_dim(
                w_fc, group * (hidden_width // fsdp_count) + c_at * unit, unit, axis=1
            )
            for group in range(fsdp_count)
        ],
        axis=1,
    ).astype(BF16)
    proj_own = lax.dynamic_slice_in_dim(w_proj, c_at * unit, unit, axis=0).astype(BF16)
    out_halves = out_parts[0], jnp.concatenate(out_parts[1:], axis=0)
    fc_steps = z_gather_steps(after(fc_own, *out_parts))

    a_even = layer_norm(x_even.astype(F32), gain_one, shift_one)[0].astype(BF16)
    a_odd = layer_norm(x_odd.astype(F32), gain_one, shift_one)[0].astype(BF16)
    q_even = (mm(a_even, w_q) + q_bias).astype(BF16)
    q_odd = (mm(a_odd, w_q) + q_bias).astype(BF16)
    o_heads, q_all, kv_all, o_t, lse = attend(shape, meta, q_even, q_odd, kv_even, kv_odd)
    out_gathered = ctx_gather_halves(
        *[after(side, kv_even) for side in out_halves],
        wait=lambda part: after(part, kv_odd),
        last=lambda part: after(part, o_heads),
    )
    out_blocks, out_layout = [], []
    for side, parts in enumerate(out_gathered):
        z_order = shape.offsets[side * half : (side + 1) * half]
        for values, order in parts:
            out_blocks.append(values)
            out_layout.append((order, z_order))
    o_own = ctx_exchange(o_heads.reshape(ctx_count, tokens, q_width))
    o_own = jnp.transpose(o_own, (1, 0, 2)).reshape(tokens, width)
    fc_parts = z_gather_finish(*fc_steps)
    proj_held = z_gather_held(after(proj_own, fc_parts[-1]))
    o_own = after(o_own, *fc_steps)
    middle = x_own + (times_blocks(meta, o_own, out_blocks, out_layout, False) + out_bias)
    second_norm, normed_two, inverse_two = layer_norm(middle, gain_two, shift_two)

    cn_even, cn_odd = ctx_gather(after(second_norm.astype(BF16), fc_parts[-1]))
    o_parts, gm_parts = ctx_gather_halves(
        after(o_own, cn_even), after(grad_mlp, cn_even), wait=lambda part: after(part, cn_odd)
    )
    o_even, o_odd = in_order(o_parts, 0), in_order(o_parts, 1)
    gm_all = jnp.concatenate([in_order(gm_parts, 0), in_order(gm_parts, 1)], axis=0)
    gm_all, o_even, o_odd = lax.optimization_barrier((gm_all, o_even, o_odd))
    cn_all = after(jnp.concatenate([cn_even, cn_odd], axis=0), proj_held)
    proj_parts = [proj_held, z_swap(proj_held, 1)]
    half_rows = chips * tokens
    hidden, act = feed_hidden(shape, meta, cn_all, fc_parts, fc_bias.reshape(1, -1))
    act_ready = after(act, *proj_parts)
    parts = [slice(at * width // 2, (at + 1) * width // 2) for at in range(2)]
    d_proj = [z_scatter_queued(mm_rows(act_ready, gm_all[:, part]).astype(BF16)) for part in parts]
    g_hidden, g_bias_fc = feed_hidden_grad(
        shape, meta, gm_all, hidden, proj_parts
    )
    g_odd = feed_blocks(shape, meta, g_hidden, fc_parts, 1, half_rows, True)
    g_even = feed_blocks(shape, meta, after(g_hidden, g_odd), fc_parts, 0, half_rows, True)
    grad_second = ctx_scatter(g_even, g_odd)
    cn_late, act_late = after(cn_all, g_even), after(act, g_even)
    own_width = fsdp_count * unit
    parts = [slice(at * own_width // 2, (at + 1) * own_width // 2) for at in range(2)]
    d_fc = [z_scatter_queued(mm_rows(cn_late, g_hidden[:, part]).astype(BF16)) for part in parts]
    mlp = [feed_blocks(shape, meta, act_late, proj_parts, side, half_rows, False) for side in range(2)]

    grad_mid_norm, grad_gain_two, grad_shift_two = norm_backward(
        grad_second, normed_two, inverse_two, gain_two
    )
    grad_middle = grad_out + grad_mid_norm
    grad_branch = grad_middle.astype(BF16)
    go_own = times_blocks(meta, grad_branch, out_blocks, out_layout, True).astype(BF16)
    grads = jnp.concatenate(
        [
            go_own.reshape(tokens, ctx_count, q_width),
            grad_branch.reshape(tokens, ctx_count, q_width),
        ],
        axis=2,
    )
    grads = ctx_exchange(jnp.transpose(grads, (1, 0, 2))).reshape(ctx_count * tokens, 2 * q_width)

    gq_even, gq_odd, gkv_even, gkv_odd, ga_even, ga_odd = attend_grad(
        shape, meta, q_all, kv_all, o_t, lse, grads
    )
    result = ctx_scatter(*mlp, [grad_second], [gq_even])
    result = (middle + (result + proj_bias)).astype(BF16)
    gkv_plane = ctx_scatter(gkv_even, gkv_odd).reshape(fsdp_count, tokens, 2 * HD)
    gkv_low = z_scatter_stacked(gkv_plane).astype(BF16)
    gkv_even, gkv_odd = ctx_gather_small(gkv_low)
    grad_first = ctx_scatter(
        mm_t(gq_even, w_q), mm_t(gq_odd, w_q), [gkv_plane, result], [gkv_even, gkv_odd]
    )
    grad_in_norm, grad_gain_one, grad_shift_one = norm_backward(
        grad_first + mm_t(gkv_low, w_kv), normed_one, inverse_one, gain_one
    )
    grad_inputs = grad_middle + grad_in_norm

    d_proj = ctx_gather_halves(
        *[after(part, grads) for part in d_proj], wait=lambda part: after(part, gkv_plane)
    )
    grad_w_proj = spread_rows(meta, d_proj)
    d_fc = ctx_gather_halves(
        *[after(part, gkv_low) for part in d_fc], wait=lambda part: after(part, grad_first)
    )
    (grad_w_fc,) = spread_columns(meta, d_fc, fsdp_count // 2, True)
    d_q = mm_rows(a_even, gq_even) + mm_rows(a_odd, gq_odd)
    d_out = mm_rows(o_even, ga_even) + mm_rows(o_odd, ga_odd)
    d_pair = z_scatter_queued(jnp.concatenate([d_q, d_out], axis=1).astype(BF16))
    d_kv = (mm_rows(a_even, gkv_even) + mm_rows(a_odd, gkv_odd)).astype(BF16)
    d_kv = z_scatter_queued(d_kv).astype(F32)
    d_pair = ctx_gather_halves(
        d_pair[:, :q_width], d_pair[:, q_width:], wait=lambda part: after(part, grad_w_proj)
    )
    grad_w_qkv, grad_w_out = spread_columns(meta, d_pair, 1, False, d_kv)

    def column_sum(*parts):
        return sum(jnp.sum(part, axis=0, dtype=F32) for part in parts)

    g_bias_q = lax.dynamic_update_index_in_dim(
        jnp.zeros((ctx_count, q_width), F32), column_sum(gq_even, gq_odd), c_at, 0
    ).reshape(-1)
    g_bias_fc = lax.dynamic_update_index_in_dim(
        jnp.zeros((fsdp_count, ctx_count, unit), F32), g_bias_fc.reshape(fsdp_count, unit), c_at, 1
    ).reshape(-1)
    g_vectors = [
        grad_gain_one,
        grad_shift_one,
        g_bias_q,
        column_sum(gkv_low[:, HD:]),
        column_sum(grad_branch),
        grad_gain_two,
        grad_shift_two,
        g_bias_fc,
        column_sum(grad_mlp),
    ]
    stacked = jnp.concatenate(
        [member.reshape(fsdp_count, -1) for member in g_vectors], axis=1
    ).astype(BF16)
    stacked = jnp.stack(
        [lax.dynamic_index_in_dim(stacked, z_at ^ at, 0, keepdims=True) for at in shape.offsets]
    )
    own = z_scatter_stacked(stacked).astype(BF16)
    summed = column_sum(*ctx_gather_small(own))
    vector_grads, start = [], 0
    for size in sizes:
        vector_grads.append(summed[start : start + size].astype(BF16).astype(F32))
        start += size
    return (
        result.reshape(inputs.shape),
        grad_inputs.reshape(inputs.shape),
        grad_w_qkv,
        grad_w_out,
        grad_w_fc,
        grad_w_proj,
        *vector_grads,
    )


def solution(mesh):
    rows_placed = P(None, "ctx", None, "fsdp", None)
    matrix, vector = P("fsdp", None), P("fsdp")
    return jax.shard_map(
        body,
        mesh=mesh,
        in_specs=(rows_placed,) + (matrix,) * 4 + (vector,) * 9 + (rows_placed, P(), P()),
        out_specs=(rows_placed, rows_placed) + (matrix,) * 4 + (vector,) * 9,
        check_vma=False,
    )
```

```python
import functools
import math

import jax
import jax.numpy as jnp
from jax import lax
from jax.experimental.layout import Layout, with_layout_constraint
from jax.experimental import pallas as pl
from jax.experimental.pallas import tpu as pltpu
from jax.sharding import PartitionSpec as P

HEADS = 16
HD = 128
NORM_EPS = 1e-05
MASKED = -1e30
KEY_TILE = 512
LANE_ROWS = 256
SCALE = 1.0 / math.sqrt(HD)
F32 = jnp.float32
BF16 = jnp.bfloat16


def layer_norm(values, gain_vec, shift_vec):
    centred = values - jnp.mean(values, axis=-1, keepdims=True)
    inverse = lax.rsqrt(jnp.mean(centred * centred, axis=-1, keepdims=True) + NORM_EPS)
    normed = centred * inverse
    return (normed * gain_vec + shift_vec, normed, inverse)


def norm_backward(grad_norm, normed, inverse, gain_vec):
    scaled = grad_norm * gain_vec
    centred = scaled - jnp.mean(scaled, axis=-1, keepdims=True)
    centred = centred - normed * jnp.mean(scaled * normed, axis=-1, keepdims=True)
    return (centred * inverse, jnp.sum(grad_norm * normed, axis=0), jnp.sum(grad_norm, axis=0))


def gelu_tanh(values):
    return jax.nn.gelu(values, approximate=True)


def mm(left, right):
    return jnp.dot(left, right, preferred_element_type=F32)


def mm_t(left, right):
    return lax.dot_general(left, right, (((1,), (1,)), ((), ())), preferred_element_type=F32)


def mm_rows(left, right):
    return lax.dot_general(left, right, (((0,), (0,)), ((), ())), preferred_element_type=F32)


def after(values, *ready):
    return lax.optimization_barrier((values, *ready))[0] if ready else values


def ctx_swap(values, mask):
    count = lax.axis_size("ctx")
    return lax.ppermute(values, "ctx", [(at, at ^ mask) for at in range(count)])


def ctx_gather(values, ready=()):
    chips = lax.axis_size("ctx") // 2
    mine = jnp.concatenate([values] + [ctx_swap(values, 2 * at) for at in range(1, chips)], axis=0)
    mine = after(mine, *ready)
    return mine, ctx_swap(mine, 1)


def ctx_gather_all(values):
    return jnp.concatenate(ctx_gather(values), axis=0)


def ctx_scatter(even, odd, ready=(), finish=()):
    return ctx_scatter_chips(*ctx_scatter_cores(even, odd), ready, finish)


def ctx_scatter_cores(even, odd):
    rows = even.shape[0] // (lax.axis_size("ctx") // 2)
    both = even.astype(F32) + ctx_swap(odd.astype(BF16), 1).astype(F32)
    return both[:rows], both[rows:].astype(BF16)


def ctx_scatter_chips(total, low, ready=(), finish=()):
    return ctx_scatter_sum(total, ctx_scatter_sent(low, total.shape[0], ready), finish)


def ctx_scatter_sent(low, rows, ready=()):
    low = after(low, *ready)
    return [
        ctx_swap(low[(at - 1) * rows : at * rows], 2 * at)
        for at in range(1, lax.axis_size("ctx") // 2)
    ]


def ctx_scatter_sum(total, parts, finish=()):
    for part in parts:
        total = total + after(part, *finish).astype(F32)
    return total


def chip_masks(side):
    masks, mask = [], lax.axis_size("ctx") // 2
    while mask > 1:
        masks.append(mask)
        mask //= 2
    return masks[1:] + masks[:1] if side else masks


def ctx_gather_halves(
    first, second, wait=lambda values: values, last=lambda values: values, begun=None
):
    held, offsets = [first[None], second[None]], [[0], [0]]
    steps = len(chip_masks(0))
    for step in range(steps):
        sent = []
        for side in range(2):
            mask = chip_masks(side)[step]
            got = begun[side] if begun and step == 0 else ctx_swap(held[side], mask)
            sent.append((got, [at ^ mask for at in offsets[side]]))
        if step < steps - 1:
            for side in range(2):
                held[side] = jnp.concatenate([held[side], wait(sent[side][0])], axis=0)
                offsets[side] = offsets[side] + sent[side][1]
    gathered = []
    for side in range(2):
        parts = [(held[side], offsets[side]), (last(sent[side][0]), sent[side][1])]
        gathered.append(
            parts + [(ctx_swap(block, 1), [at ^ 1 for at in order]) for block, order in parts]
        )
    return gathered


def ctx_scatter_halves(even, odd, ready=(), finish=()):
    chips = lax.axis_size("ctx") // 2
    rows = even.shape[0] // chips
    both = even.astype(F32) + ctx_swap(odd.astype(BF16), 1).astype(F32)
    both = both.reshape(chips, 2, rows // 2, -1)
    totals = []
    for side in range(2):
        blocks = {2 * at: both[at, side] for at in range(chips)}
        for step, mask in enumerate(reversed(chip_masks(side))):
            kept = [offset for offset in sorted(blocks) if not offset & mask]
            sent = jnp.stack([blocks[offset ^ mask].astype(BF16) for offset in kept])
            got = ctx_swap(after(sent, *ready) if step == 0 else sent, mask)
            if len(kept) == 1:
                got = after(got, *finish)
            blocks = {offset: blocks[offset] + got[at].astype(F32) for at, offset in enumerate(kept)}
        totals.append(blocks[0])
    return jnp.concatenate(totals, axis=0)


def in_order(parts, parity):
    blocks = {
        offset: values[at]
        for values, order in parts
        for at, offset in enumerate(order)
        if offset % 2 == parity
    }
    return jnp.concatenate([blocks[offset] for offset in sorted(blocks)], axis=0)


def ctx_exchange(values):
    return lax.all_to_all(values, "ctx", 0, 0, tiled=True)


def z_masks(count):
    masks = []
    while count > 1:
        masks.append(count - 1)
        count //= 2
    return masks


def z_offsets(count):
    offsets = [0]
    for mask in z_masks(count):
        offsets = offsets + [at ^ mask for at in offsets]
    return offsets


def z_swap(values, mask):
    count = lax.axis_size("fsdp")
    return lax.ppermute(values, "fsdp", [(at, at ^ mask) for at in range(count)])


def z_gather_steps(values):
    held = values[None]
    own = z_swap(held, 1)
    for mask in z_masks(lax.axis_size("fsdp"))[:-1]:
        held = jnp.concatenate([held, z_swap(held, mask)], axis=0)
    return held, own


def z_gather_finish(held, own):
    if held.shape[0] == 1:
        return [held, own]
    return [held, own, z_swap(held[1:], 1)]


def z_gather_parts(values):
    return z_gather_finish(*z_gather_steps(values))


def z_gather_held(values):
    held = values[None]
    for mask in z_masks(lax.axis_size("fsdp"))[:-1]:
        held = jnp.concatenate([held, z_swap(held, mask)], axis=0)
    return held


def z_sum_exchange(values):
    return jnp.sum(lax.all_to_all(values, "fsdp", 0, 0, tiled=True), axis=0, dtype=F32)


def z_gather_queued(values):
    return lax.all_gather(values, "fsdp", axis=0, tiled=True)


def z_scatter_queued(values):
    return lax.psum_scatter(values, "fsdp", scatter_dimension=0, tiled=True)


def place_kernel(plan, n_in, meta, *refs):
    ins, outs = refs[:n_in], refs[n_in:]
    for source, rows_in, target, rows_out in plan(meta):
        outs[target][rows_out] = ins[source][rows_in]


def place_blocks(meta, sources, outs, plan, name):
    return pl.pallas_call(
        functools.partial(place_kernel, plan, len(sources)),
        grid_spec=pltpu.PrefetchScalarGridSpec(
            num_scalar_prefetch=1,
            grid=(1,),
            in_specs=[pl.BlockSpec(memory_space=pltpu.VMEM)] * len(sources),
            out_specs=[pl.BlockSpec(memory_space=pltpu.VMEM)] * len(outs),
        ),
        out_shape=[jax.ShapeDtypeStruct(out, sources[0].dtype) for out in outs],
        compiler_params=pltpu.CompilerParams(vmem_limit_bytes=56 * 2**20),
        name=name,
    )(meta, *sources)


class Shape:
    def __init__(self, ctx_count, fsdp_count, slots, rows):
        self.ctx_count, self.fsdp_count, self.slots, self.rows = ctx_count, fsdp_count, slots, rows
        self.heads = HEADS // ctx_count
        self.block = rows * fsdp_count
        self.blocks = 2 * ctx_count
        self.keys = self.block * self.blocks
        self.tokens = slots * 2 * rows
        self.q_blocks = LANE_ROWS // (self.heads * rows)
        self.head_rows = self.q_blocks * rows
        self.q_tiles = self.blocks // self.q_blocks
        self.q_rows = self.q_tiles * LANE_ROWS
        self.chips = ctx_count // 2
        self.offsets = z_offsets(fsdp_count)


    def part_starts(self, count):
        half = self.fsdp_count // 2
        return [0, half, half + 1][:count]

    def part_of(self, at, count):
        starts = self.part_starts(count)
        part = max(index for index, start in enumerate(starts) if at >= start)
        return part, at - starts[part]


def for_blocks(shape, meta, act):
    me = meta[0]

    def step(chip, carry):
        for parity in range(2):
            first = meta[6 + (me ^ (2 * chip + parity))]
            for slot in range(shape.slots):
                for half in range(2):
                    block = first if half == 0 else shape.blocks - 1 - first
                    act(parity, chip, slot, half, block)
        return carry

    lax.fori_loop(0, shape.chips, step, 0)


def at_rows(start, size, unit):
    return pl.ds(pl.multiple_of(start, unit), size)


def q_source(shape, chip, slot, half):
    return at_rows(chip * shape.tokens + (slot * 2 + half) * shape.rows, shape.rows, shape.rows)


def q_target(shape, block, head):
    start = (block // shape.q_blocks) * LANE_ROWS + (block % shape.q_blocks) * shape.rows
    return at_rows(start + head * shape.head_rows, shape.rows, shape.rows)


def kv_source(shape, chip, order, slot, half):
    start = (chip * shape.fsdp_count + order) * shape.tokens + (slot * 2 + half) * shape.rows
    return at_rows(start, shape.rows, shape.rows)


def kv_target(shape, meta, block, order):
    start = block * shape.block + (meta[1] ^ shape.offsets[order]) * shape.rows
    return at_rows(start, shape.rows, shape.rows)


def query_bounds(shape, meta, slot, tile):
    lane = lax.broadcasted_iota(jnp.int32, (1, LANE_ROWS), 1)
    row = lane % shape.head_rows
    pos = (tile * shape.q_blocks + row // shape.rows) * shape.block + meta[1] * shape.rows + row % shape.rows
    first_end = meta[2 + 2 * slot]
    second_end = first_end + meta[3 + 2 * slot]

    def start_of(at):
        return jnp.where(at < first_end, 0, jnp.where(at < second_end, first_end, second_end))

    first_pos = tile * shape.q_blocks * shape.block + meta[1] * shape.rows
    last_pos = first_pos + (shape.q_blocks - 1) * shape.block + shape.rows - 1
    return pos, start_of(pos), start_of(first_pos) // KEY_TILE, last_pos // KEY_TILE + 1


def visible(pos, start, tile):
    key_pos = tile * KEY_TILE + lax.broadcasted_iota(jnp.int32, (KEY_TILE, LANE_ROWS), 0)
    return (key_pos <= pos) & (key_pos >= start)


def device_rows(shape, meta, parity, chip, slot, half):
    device = meta[0] ^ (2 * chip + parity)
    return at_rows(device * shape.tokens + (slot * 2 + half) * shape.rows, shape.rows, shape.rows)


def attend_kernel(shape, meta, q_even, q_odd, kv_even, kv_odd, o_out, q_all, kv_all, o_t, lse, o_rows):
    queries, keys = (q_even, q_odd), (kv_even, kv_odd)

    def place(parity, chip, slot, half, block):
        for head in range(shape.heads):
            q_all[slot, q_target(shape, block, head), :] = queries[parity][
                q_source(shape, chip, slot, half), head * HD : (head + 1) * HD
            ]
        for order in range(shape.fsdp_count):
            kv_all[slot, kv_target(shape, meta, block, order), :] = keys[parity][
                kv_source(shape, chip, order, slot, half), :
            ]

    for_blocks(shape, meta, place)

    def tile_step(item, carry):
        slot, tile = item // shape.q_tiles, item % shape.q_tiles
        pos, start, low, high = query_bounds(shape, meta, slot, tile)
        q_tile = q_all[slot, at_rows(tile * LANE_ROWS, LANE_ROWS, LANE_ROWS), :]

        def key_step(at, state):
            peak, total, acc = state
            part = at_rows(at * KEY_TILE, KEY_TILE, KEY_TILE)
            scores = mm_t(kv_all[slot, part, :HD], q_tile) * SCALE
            scores = jnp.where(visible(pos, start, at), scores, MASKED)
            new_peak = jnp.maximum(peak, jnp.max(scores, axis=0, keepdims=True))
            fade = jnp.exp(peak - new_peak)
            weights = jnp.exp(scores - new_peak)
            total = total * fade + jnp.sum(weights, axis=0, keepdims=True)
            acc = acc * fade + mm_rows(kv_all[slot, part, HD:], weights.astype(BF16))
            return new_peak, total, acc

        begin = (
            jnp.full((1, LANE_ROWS), MASKED, F32),
            jnp.zeros((1, LANE_ROWS), F32),
            jnp.zeros((HD, LANE_ROWS), F32),
        )
        peak, total, acc = lax.fori_loop(low, high, key_step, begin)
        acc = acc / total
        o_t[item] = acc
        lse[item] = peak + jnp.log(total)
        o_rows[slot, at_rows(tile * LANE_ROWS, LANE_ROWS, LANE_ROWS), :] = acc.T.astype(BF16)
        return carry

    lax.fori_loop(0, shape.slots * shape.q_tiles, tile_step, 0)

    def put_back(parity, chip, slot, half, block):
        for head in range(shape.heads):
            o_out[device_rows(shape, meta, parity, chip, slot, half), head * HD : (head + 1) * HD] = o_rows[
                slot, q_target(shape, block, head), :
            ]

    for_blocks(shape, meta, put_back)


def attend_grad_kernel(
    shape, meta, q_all, kv_all, o_t, lse, grads, gq_even, gq_odd, gkv_even, gkv_odd, ga_even, ga_odd, go_all, gq_all, gkv_all
):
    g_queries, g_keys, g_branch = (gq_even, gq_odd), (gkv_even, gkv_odd), (ga_even, ga_odd)

    def place(parity, chip, slot, half, block):
        source = device_rows(shape, meta, parity, chip, slot, half)
        for head in range(shape.heads):
            go_all[slot, q_target(shape, block, head), :] = grads[source, head * HD : (head + 1) * HD]
        g_branch[parity][q_source(shape, chip, slot, half), :] = grads[source, shape.heads * HD :]

    for_blocks(shape, meta, place)
    gkv_all[...] = jnp.zeros_like(gkv_all)

    def tile_step(item, carry):
        slot, tile = item // shape.q_tiles, item % shape.q_tiles
        pos, start, low, high = query_bounds(shape, meta, slot, tile)
        rows = at_rows(tile * LANE_ROWS, LANE_ROWS, LANE_ROWS)
        q_tile = q_all[slot, rows, :]
        go_tile = go_all[slot, rows, :]
        delta = jnp.sum(go_tile.astype(F32).T * o_t[item], axis=0, keepdims=True)
        lse_row = lse[item]

        def key_step(at, acc):
            part = at_rows(at * KEY_TILE, KEY_TILE, KEY_TILE)
            key_part, value_part = kv_all[slot, part, :HD], kv_all[slot, part, HD:]
            scores = mm_t(key_part, q_tile) * SCALE
            probs = jnp.where(visible(pos, start, at), jnp.exp(scores - lse_row), 0.0)
            g_scores = (probs * (mm_t(value_part, go_tile) - delta)).astype(BF16)
            gkv_all[slot, part, :HD] += mm(g_scores, q_tile)
            gkv_all[slot, part, HD:] += mm(probs.astype(BF16), go_tile)
            return acc + mm_rows(key_part, g_scores)

        acc = lax.fori_loop(low, high, key_step, jnp.zeros((HD, LANE_ROWS), F32))
        gq_all[slot, rows, :] = (acc * SCALE).T.astype(BF16)
        return carry

    lax.fori_loop(0, shape.slots * shape.q_tiles, tile_step, 0)

    def put_back(parity, chip, slot, half, block):
        for head in range(shape.heads):
            g_queries[parity][q_source(shape, chip, slot, half), head * HD : (head + 1) * HD] = gq_all[
                slot, q_target(shape, block, head), :
            ]
        for order in range(shape.fsdp_count):
            target = kv_target(shape, meta, block, order)
            source = kv_source(shape, chip, meta[1] ^ shape.offsets[order], slot, half)
            g_keys[parity][source, :HD] = (gkv_all[slot, target, :HD] * SCALE).astype(BF16)
            g_keys[parity][source, HD:] = gkv_all[slot, target, HD:].astype(BF16)

    for_blocks(shape, meta, put_back)


def attend(shape, meta, q_even, q_odd, kv_even, kv_odd):
    items = shape.slots * shape.q_tiles
    pairs = items * LANE_ROWS * shape.keys // 2
    return pl.pallas_call(
        functools.partial(attend_kernel, shape),
        grid_spec=pltpu.PrefetchScalarGridSpec(
            num_scalar_prefetch=1,
            grid=(1,),
            in_specs=[pl.BlockSpec(memory_space=pltpu.VMEM)] * 4,
            out_specs=[pl.BlockSpec(memory_space=pltpu.VMEM)] * 5,
            scratch_shapes=[pltpu.VMEM((shape.slots, shape.q_rows, HD), BF16)],
        ),
        out_shape=[
            jax.ShapeDtypeStruct((shape.ctx_count * shape.tokens, shape.heads * HD), BF16),
            jax.ShapeDtypeStruct((shape.slots, shape.q_rows, HD), BF16),
            jax.ShapeDtypeStruct((shape.slots, shape.keys, 2 * HD), BF16),
            jax.ShapeDtypeStruct((items, HD, LANE_ROWS), F32),
            jax.ShapeDtypeStruct((items, 1, LANE_ROWS), F32),
        ],
        compiler_params=pltpu.CompilerParams(vmem_limit_bytes=56 * 2**20),
        cost_estimate=pl.CostEstimate(flops=pairs * HD * 4, transcendentals=pairs, bytes_accessed=8 * 2**20),
        name="attend",
    )(meta, q_even, q_odd, kv_even, kv_odd)


def attend_grad(shape, meta, q_all, kv_all, o_t, lse, grads):
    items = shape.slots * shape.q_tiles
    q_like = jax.ShapeDtypeStruct((shape.chips * shape.tokens, shape.heads * HD), BF16)
    kv_like = jax.ShapeDtypeStruct((shape.chips * shape.fsdp_count * shape.tokens, 2 * HD), BF16)
    pairs = items * LANE_ROWS * shape.keys // 2
    return pl.pallas_call(
        functools.partial(attend_grad_kernel, shape),
        grid_spec=pltpu.PrefetchScalarGridSpec(
            num_scalar_prefetch=1,
            grid=(1,),
            in_specs=[pl.BlockSpec(memory_space=pltpu.VMEM)] * 5,
            out_specs=[pl.BlockSpec(memory_space=pltpu.VMEM)] * 6,
            scratch_shapes=[
                pltpu.VMEM((shape.slots, shape.q_rows, HD), BF16),
                pltpu.VMEM((shape.slots, shape.q_rows, HD), BF16),
                pltpu.VMEM((shape.slots, shape.keys, 2 * HD), F32),
            ],
        ),
        out_shape=[q_like, q_like, kv_like, kv_like, q_like, q_like],
        compiler_params=pltpu.CompilerParams(vmem_limit_bytes=56 * 2**20),
        cost_estimate=pl.CostEstimate(flops=pairs * HD * 10, transcendentals=pairs, bytes_accessed=10 * 2**20),
        name="attend_grad",
    )(meta, q_all, kv_all, o_t, lse, grads)


def block_of(shape, parts, at):
    part, block = shape.part_of(at, len(parts))
    return parts[part][block]


def gelu_parts(values):
    root = math.sqrt(2.0 / math.pi)
    return jnp.tanh(root * (values + 0.044715 * (values * values * values)))


def hidden_kernel(shape, meta, rows_ref, bias_ref, *refs):
    parts, (hidden_ref, act_ref) = refs[:-2], refs[-2:]
    depth = parts[0].shape[1]
    total = bias_ref[...]
    for at, offset in enumerate(shape.offsets):
        part = pl.ds(pl.multiple_of((meta[1] ^ offset) * depth, depth), depth)
        total = total + mm(rows_ref[:, part], block_of(shape, parts, at))
    hidden_ref[...] = total
    act_ref[...] = (0.5 * total * (1.0 + gelu_parts(total))).astype(BF16)


def feed_hidden(shape, meta, rows, parts, bias):
    count, width = rows.shape
    _, depth, columns = parts[0].shape
    tile = 256
    weights = [
        pl.BlockSpec((part.shape[0], depth, tile), lambda i, m: (0, 0, i)) for part in parts
    ]
    out = pl.BlockSpec((count, tile), lambda i, m: (0, i))
    return pl.pallas_call(
        functools.partial(hidden_kernel, shape),
        grid_spec=pltpu.PrefetchScalarGridSpec(
            num_scalar_prefetch=1,
            grid=(columns // tile,),
            in_specs=[
                pl.BlockSpec((count, width), lambda i, m: (0, 0)),
                pl.BlockSpec((1, tile), lambda i, m: (0, i)),
                *weights,
            ],
            out_specs=[out, out],
        ),
        out_shape=[
            jax.ShapeDtypeStruct((count, columns), F32),
            jax.ShapeDtypeStruct((count, columns), BF16),
        ],
        compiler_params=pltpu.CompilerParams(vmem_limit_bytes=56 * 2**20),
        cost_estimate=pl.CostEstimate(
            flops=2 * count * width * columns,
            transcendentals=count * columns,
            bytes_accessed=2 * (count * width + width * columns) + 6 * count * columns,
        ),
        name="feed_hidden",
    )(meta, rows, bias, *parts)


def hidden_grad_kernel(grads_ref, hidden_ref, first, second, out_ref, sum_ref):
    values = hidden_ref[...]
    tanh = gelu_parts(values)
    root = math.sqrt(2.0 / math.pi)
    slope = 0.5 * (1.0 + tanh) + (0.5 * root) * values * (1.0 - tanh * tanh) * (
        1.0 + (3.0 * 0.044715) * (values * values)
    )
    width = first.shape[1]
    grads = mm_t(grads_ref[:, :width], first[...]) + mm_t(grads_ref[:, width:], second[...])
    low = (grads * slope).astype(BF16)
    out_ref[...] = low
    sum_ref[...] = jnp.sum(low.astype(F32), axis=0, keepdims=True)


def feed_hidden_grad(grads, hidden, weights):
    count, width = grads.shape
    columns = hidden.shape[1]
    tile = 256
    place = pl.BlockSpec((count, tile), lambda i: (0, i))
    return pl.pallas_call(
        hidden_grad_kernel,
        grid=(columns // tile,),
        in_specs=[pl.BlockSpec((count, width), lambda i: (0, 0)), place]
        + [pl.BlockSpec((tile, width // 2), lambda i: (i, 0))] * 2,
        out_specs=[place, pl.BlockSpec((1, tile), lambda i: (0, i))],
        out_shape=[
            jax.ShapeDtypeStruct((count, columns), BF16),
            jax.ShapeDtypeStruct((1, columns), F32),
        ],
        compiler_params=pltpu.CompilerParams(vmem_limit_bytes=56 * 2**20),
        cost_estimate=pl.CostEstimate(
            flops=2 * count * width * columns,
            transcendentals=count * columns,
            bytes_accessed=2 * (count * width + width * columns) + 6 * count * columns,
        ),
        name="feed_hidden_grad",
    )(grads, hidden, *weights)


def feed_late_kernel(steps, rows_ref, first, second, norm_ref, grads_ref, even_ref, odd_ref, *d_refs):
    at = pl.program_id(0)
    width = first.shape[1]
    for side, out_ref in enumerate((even_ref, odd_ref)):

        @pl.when(at // steps == side)
        def _(out_ref=out_ref):
            out_ref[:, :width] = mm(rows_ref[...], first[...]).astype(BF16)
            out_ref[:, width:] = mm(rows_ref[...], second[...]).astype(BF16)

    @pl.when(at >= 2 * steps)
    def _():
        columns = d_refs[0].shape[1]
        for part, out_ref in enumerate(d_refs):
            out_ref[...] = mm_rows(
                norm_ref[...], grads_ref[:, part * columns : (part + 1) * columns]
            ).astype(BF16)


def feed_late(rows, weights, norm, grads):
    depth, half_width = weights[0].shape
    count, tile = rows.shape[0] // 2, 256
    steps = count // tile
    width, columns = norm.shape[1], grads.shape[1]
    last = 2 * steps - 1
    d_block = pl.BlockSpec((tile, columns // 2), lambda i: (jnp.maximum(i - last - 1, 0), 0))
    return pl.pallas_call(
        functools.partial(feed_late_kernel, steps),
        grid=(2 * steps + width // tile,),
        in_specs=[
            pl.BlockSpec((tile, depth), lambda i: (jnp.minimum(i, last), 0)),
            pl.BlockSpec((depth, half_width), lambda i: (0, 0)),
            pl.BlockSpec((depth, half_width), lambda i: (0, 0)),
            pl.BlockSpec((2 * count, tile), lambda i: (0, jnp.maximum(i - last - 1, 0))),
            pl.BlockSpec((2 * count, columns), lambda i: (0, 0)),
        ],
        out_specs=[
            pl.BlockSpec((tile, 2 * half_width), lambda i: (jnp.minimum(i, steps - 1), 0)),
            pl.BlockSpec((tile, 2 * half_width), lambda i: (jnp.clip(i - steps, 0, steps - 1), 0)),
            d_block,
            d_block,
        ],
        out_shape=[jax.ShapeDtypeStruct((count, 2 * half_width), BF16)] * 2
        + [jax.ShapeDtypeStruct((width, columns // 2), BF16)] * 2,
        compiler_params=pltpu.CompilerParams(vmem_limit_bytes=56 * 2**20),
        cost_estimate=pl.CostEstimate(
            flops=8 * count * depth * half_width + 4 * count * width * columns,
            transcendentals=0,
            bytes_accessed=2 * (6 * count * half_width + 2 * depth * half_width + 4 * count * width),
        ),
        name="feed_late",
    )(rows, *weights, norm, grads)


def feed_grad_kernel(shape, meta, rows_ref, *refs):
    parts, out_ref = refs[:-1], refs[-1]
    for at, offset in enumerate(shape.offsets):
        block = block_of(shape, parts, at)
        size = block.shape[0]
        part = pl.ds(pl.multiple_of((meta[1] ^ offset) * size, size), size)
        out_ref[:, part] = mm_t(rows_ref[...], block).astype(BF16)


def feed_grad(shape, meta, rows, parts, side, count):
    width = shape.fsdp_count * parts[0].shape[1]
    tile = 256
    steps = count // tile
    return pl.pallas_call(
        functools.partial(feed_grad_kernel, shape),
        grid_spec=pltpu.PrefetchScalarGridSpec(
            num_scalar_prefetch=1,
            grid=(steps,),
            in_specs=[
                pl.BlockSpec((tile, rows.shape[1]), lambda i, m: (side * steps + i, 0)),
                *[pl.BlockSpec(part.shape, lambda i, m: (0, 0, 0)) for part in parts],
            ],
            out_specs=pl.BlockSpec((tile, width), lambda i, m: (i, 0)),
        ),
        out_shape=jax.ShapeDtypeStruct((count, width), BF16),
        compiler_params=pltpu.CompilerParams(vmem_limit_bytes=56 * 2**20),
        cost_estimate=pl.CostEstimate(
            flops=2 * count * rows.shape[1] * width,
            transcendentals=0,
            bytes_accessed=2 * (count + width) * rows.shape[1] + 2 * count * width,
        ),
        name="feed_grad",
    )(meta, rows, *parts)


def branch_kernel(layout, grad, meta, rows_ref, *refs):
    parts, out_ref = refs[:-1], refs[-1]
    out_ref[...] = jnp.zeros_like(out_ref)
    for part, (ctx_order, z_order) in zip(parts, layout):
        depth, columns = part.shape[2], part.shape[3]
        for at, ctx_offset in enumerate(ctx_order):
            column = pl.ds(pl.multiple_of((meta[0] ^ ctx_offset) * columns, columns), columns)
            for order, z_offset in enumerate(z_order):
                row = pl.ds(pl.multiple_of((meta[1] ^ z_offset) * depth, depth), depth)
                if grad:
                    out_ref[:, row] += mm_t(rows_ref[:, column], part[at, order])
                else:
                    out_ref[:, column] += mm(rows_ref[:, row], part[at, order])


def times_blocks(meta, rows, parts, layout, grad):
    return pl.pallas_call(
        functools.partial(branch_kernel, layout, grad),
        grid_spec=pltpu.PrefetchScalarGridSpec(
            num_scalar_prefetch=1,
            grid=(1,),
            in_specs=[pl.BlockSpec(memory_space=pltpu.VMEM)] * (1 + len(parts)),
            out_specs=pl.BlockSpec(memory_space=pltpu.VMEM),
        ),
        out_shape=jax.ShapeDtypeStruct(rows.shape, F32),
        compiler_params=pltpu.CompilerParams(vmem_limit_bytes=56 * 2**20),
        cost_estimate=pl.CostEstimate(
            flops=2 * rows.shape[0] * rows.shape[1] ** 2,
            transcendentals=0,
            bytes_accessed=2 * rows.shape[1] ** 2,
        ),
        name="branch_grad" if grad else "branch",
    )(meta, rows, *parts)


def spread_rows_kernel(pieces, steps, meta, *refs):
    out_ref = refs[-1]
    for piece, blocks in enumerate(pieces):

        @pl.when(pl.program_id(0) // steps == piece)
        def _(blocks=blocks):
            for source, block, offset in blocks:
                rows = refs[source].shape[1]
                start = pl.multiple_of((meta[0] ^ offset) * rows, rows)
                out_ref[pl.ds(start, rows), :] = refs[source][block].astype(F32)


def spread_rows(meta, gathered):
    tile = 256
    members, specs, pieces = [], [], []
    for piece, parts in enumerate(gathered):
        blocks = []
        for values, order in parts:
            count, rows, columns = values.shape
            steps = columns // tile
            blocks += [(len(members), at, offset) for at, offset in enumerate(order)]
            members.append(values)

            def place(i, m, piece=piece, steps=steps):
                return (0, 0, jnp.clip(i - piece * steps, 0, steps - 1))

            specs.append(pl.BlockSpec((count, rows, tile), place))
        pieces.append(blocks)
    total = len(pieces[0]) * rows
    return pl.pallas_call(
        functools.partial(spread_rows_kernel, pieces, steps),
        grid_spec=pltpu.PrefetchScalarGridSpec(
            num_scalar_prefetch=1,
            grid=(len(pieces) * steps,),
            in_specs=specs,
            out_specs=pl.BlockSpec((total, tile), lambda i, m: (0, i)),
        ),
        out_shape=jax.ShapeDtypeStruct((total, len(pieces) * columns), F32),
        compiler_params=pltpu.CompilerParams(vmem_limit_bytes=48 * 2**20),
        name="spread_rows",
    )(meta, *members)


def spread_kernel(moves, extras, outs, meta, *refs):
    outs = refs[len(refs) - outs :]
    for source, block, columns, offset, out, start, step, size in moves:
        target = pl.multiple_of(start + (meta[0] ^ offset) * step, size)
        outs[out][:, pl.ds(target, size)] = refs[source][block, :, columns].astype(F32)
    for source, out in extras:
        width = refs[source].shape[1]
        outs[out][:, outs[out].shape[1] - width :] = refs[source][...]


def spread_columns(meta, gathered, groups, joined, extra=None):
    pieces = len(gathered)
    rows, columns = gathered[0][0][0].shape[1:]
    width = columns // groups if joined else columns // pieces
    count = sum(len(order) for _, order in gathered[0])
    if width % 128:
        results = []
        for parts in gathered:
            out = jnp.zeros((count, rows, groups, width), F32)
            for values, order in parts:
                for at, offset in enumerate(order):
                    block = values[at].reshape(rows, groups, width).astype(F32)
                    out = lax.dynamic_update_index_in_dim(out, block, meta[0] ^ offset, 0)
            results.append(jnp.transpose(out, (1, 2, 0, 3)).reshape(rows, -1))
        return [jnp.concatenate(results, axis=1)]
    members, moves = [], []
    for piece, parts in enumerate(gathered):
        if not joined:
            members = []
        for values, order in parts:
            for at, offset in enumerate(order):
                for group in range(groups):
                    start = ((piece if joined else 0) * groups + group) * count * width
                    source = (group if joined else piece) * width
                    moves.append(
                        (
                            len(members),
                            at,
                            slice(source, source + width),
                            offset,
                            0 if joined else piece,
                            start,
                            width,
                            width,
                        )
                    )
            members.append(values)
    sizes = [groups * count * width * pieces] if joined else [count * width] * pieces
    tile = min(rows, 64)
    in_specs = [
        pl.BlockSpec((member.shape[0], tile, columns), lambda i, m: (0, i, 0)) for member in members
    ]
    extras = []
    if extra is not None:
        extras = [(len(members), 0)]
        members.append(extra)
        in_specs.append(pl.BlockSpec((tile, extra.shape[1]), lambda i, m: (i, 0)))
        sizes[0] += extra.shape[1]
    return pl.pallas_call(
        functools.partial(spread_kernel, moves, extras, len(sizes)),
        grid_spec=pltpu.PrefetchScalarGridSpec(
            num_scalar_prefetch=1,
            grid=(rows // tile,),
            in_specs=in_specs,
            out_specs=[pl.BlockSpec((tile, size), lambda i, m: (i, 0)) for size in sizes],
        ),
        out_shape=[jax.ShapeDtypeStruct((rows, size), F32) for size in sizes],
        compiler_params=pltpu.CompilerParams(vmem_limit_bytes=48 * 2**20),
        name="spread_columns",
    )(meta, *members)


def pick_block(pair_table, ctx_at, half_bit):
    ctx_total = pair_table.shape[0]
    chosen = jnp.sum(jnp.where(jnp.arange(ctx_total, dtype=jnp.int32) == ctx_at, pair_table, 0))
    return jnp.where(half_bit == 0, chosen, 2 * ctx_total - 1 - chosen)


def body(
    inputs,
    w_qkv,
    w_out,
    w_fc,
    w_proj,
    ln1_gain,
    ln1_bias,
    bias_q,
    bias_v,
    bias_out,
    ln2_gain,
    ln2_bias,
    bias_fc,
    bias_proj,
    cotangent,
    lengths,
    pair_table,
):
    slots, _, _, rows, width = inputs.shape
    ctx_count, fsdp_count = lax.axis_size("ctx"), lax.axis_size("fsdp")
    c_at, z_at = lax.axis_index("ctx"), lax.axis_index("fsdp")
    shape = Shape(ctx_count, fsdp_count, slots, rows)
    tokens, chips = shape.tokens, shape.chips
    q_width = width // ctx_count
    shard = width // fsdp_count
    hidden_width = w_fc.shape[1]
    unit = hidden_width // (fsdp_count * ctx_count)
    meta = jnp.concatenate(
        [jnp.stack([c_at, z_at]).astype(jnp.int32), lengths.reshape(-1), pair_table]
    ).astype(jnp.int32)

    offsets = jnp.arange(2 * rows, dtype=jnp.int32)
    pos = (
        pick_block(pair_table, c_at, offsets // rows) * shape.block + z_at * rows + offsets % rows
    )
    live = (pos[None, :] < lengths[:, 0:1] + lengths[:, 1:2]).reshape(tokens, 1).astype(F32)

    x_low = inputs.reshape(tokens, width)
    grad_out = cotangent.reshape(tokens, width).astype(F32) * live
    grad_mlp = grad_out.astype(BF16)
    pack_width = q_width + 2 * HD
    w_first = jnp.concatenate(
        [lax.dynamic_slice_in_dim(w_qkv, c_at * q_width, q_width, axis=1), w_qkv[:, width:]], axis=1
    ).astype(BF16)
    vectors = [ln1_gain, ln1_bias, bias_q, bias_v, bias_out, ln2_gain, ln2_bias, bias_fc, bias_proj]
    sizes = [member.shape[0] for member in vectors]
    vector_rows = 16 * math.ceil(sum(sizes) / (16 * HD))
    packed = jnp.concatenate(
        [member.astype(BF16) for member in vectors]
        + [jnp.zeros((vector_rows * HD - sum(sizes),), BF16)]
    ).reshape(vector_rows, HD)
    x_even, x_odd = ctx_gather(after(x_low, w_first))
    half = fsdp_count // 2
    first_held, first_own = z_gather_steps(w_first)
    first_blocks = z_gather_finish(first_held, first_own)
    vector_held = z_gather_held(after(packed, first_held))
    vector_blocks = [vector_held, z_swap(vector_held, 1)]

    def first_plan(ref):
        moves = []
        for at, offset in enumerate(shape.offsets):
            owner, (part, block) = ref[1] ^ offset, shape.part_of(at, len(first_blocks))
            weight_rows = pl.ds(pl.multiple_of(owner * shard, shard), shard)
            q_part, kv_part = pl.ds(0, q_width), pl.ds(q_width, 2 * HD)
            moves += [
                (part, (block, slice(None), q_part), 0, (weight_rows, slice(None))),
                (part, (block, slice(None), kv_part), 1, (weight_rows, slice(None))),
                (len(first_blocks) + at // half, (at % half,), 2, (owner,)),
            ]
        return moves

    w_q, w_kv, packed = place_blocks(
        meta,
        [*first_blocks, *vector_blocks],
        [(width, q_width), (width, 2 * HD), (fsdp_count, vector_rows, HD)],
        first_plan,
        "place_first",
    )
    packed = packed.reshape(fsdp_count, -1)
    full, start = [], 0
    for size in sizes:
        full.append(packed[:, start : start + size].reshape(-1).astype(F32))
        start += size
    gain_one, shift_one, q_bias, v_bias, out_bias, gain_two, shift_two, fc_bias, proj_bias = full
    q_bias = lax.dynamic_slice_in_dim(q_bias, c_at * q_width, q_width)
    fc_bias = lax.dynamic_index_in_dim(
        fc_bias.reshape(fsdp_count, ctx_count, unit), c_at, 1, keepdims=False
    )

    x_own = x_low.astype(F32)
    first_norm, normed_one, inverse_one = layer_norm(x_own, gain_one, shift_one)
    kv_own = mm(first_norm.astype(BF16), w_kv)
    kv_own = jnp.concatenate([kv_own[:, :HD], kv_own[:, HD:] + v_bias], axis=1).astype(BF16)
    kv_z = jnp.concatenate(z_gather_parts(kv_own), axis=0).reshape(fsdp_count * tokens, 2 * HD)
    kv_even, kv_odd = ctx_gather(kv_z)

    out_parts = z_gather_parts(
        after(lax.dynamic_slice_in_dim(w_out, c_at * q_width, q_width, axis=1).astype(BF16), kv_z)
    )

    fc_own = jnp.concatenate(
        [
            lax.dynamic_slice_in_dim(
                w_fc, group * (hidden_width // fsdp_count) + c_at * unit, unit, axis=1
            )
            for group in range(fsdp_count)
        ],
        axis=1,
    ).astype(BF16)
    proj_own = lax.dynamic_slice_in_dim(w_proj, c_at * unit, unit, axis=0).astype(BF16)
    out_halves = out_parts[0], jnp.concatenate(out_parts[1:], axis=0)
    fc_steps = z_gather_steps(after(fc_own, out_parts[0]))

    a_even = layer_norm(x_even.astype(F32), gain_one, shift_one)[0].astype(BF16)
    a_odd = layer_norm(x_odd.astype(F32), gain_one, shift_one)[0].astype(BF16)
    q_even = (mm(a_even, w_q) + q_bias).astype(BF16)
    q_odd = (mm(a_odd, w_q) + q_bias).astype(BF16)
    o_heads, q_all, kv_all, o_t, lse = attend(shape, meta, q_even, q_odd, kv_even, kv_odd)
    out_gathered = ctx_gather_halves(
        *[after(side, kv_even) for side in out_halves],
        wait=lambda part: after(part, kv_odd),
        last=lambda part: after(part, o_heads),
    )
    out_blocks, out_layout = [], []
    for side, parts in enumerate(out_gathered):
        z_order = shape.offsets[side * half : (side + 1) * half]
        for values, order in parts:
            out_blocks.append(values)
            out_layout.append((order, z_order))
    o_own = ctx_exchange(o_heads.reshape(ctx_count, tokens, q_width))
    o_own = jnp.transpose(o_own, (1, 0, 2)).reshape(tokens, width)
    fc_parts = z_gather_finish(*fc_steps)
    proj_own = after(proj_own, fc_parts[-1])
    w_p = [
        z_gather_queued(proj_own[:, at * width // 2 : (at + 1) * width // 2]) for at in range(2)
    ]
    o_own = after(o_own, *fc_steps)
    middle = x_own + (times_blocks(meta, o_own, out_blocks, out_layout, False) + out_bias)
    second_norm, normed_two, inverse_two = layer_norm(middle, gain_two, shift_two)

    cn_even, cn_odd = ctx_gather(after(second_norm.astype(BF16), fc_parts[-1]))
    o_parts, gm_parts = ctx_gather_halves(
        after(o_own, cn_even), after(grad_mlp, cn_even), wait=lambda part: after(part, cn_odd)
    )
    o_even, o_odd = in_order(o_parts, 0), in_order(o_parts, 1)
    gm_all = jnp.concatenate([in_order(gm_parts, 0), in_order(gm_parts, 1)], axis=0)
    gm_all, o_even, o_odd = lax.optimization_barrier((gm_all, o_even, o_odd))
    cn_all = jnp.concatenate([cn_even, cn_odd], axis=0)
    half_rows = chips * tokens
    hidden, act = feed_hidden(shape, meta, cn_all, fc_parts, fc_bias.reshape(1, -1))
    d_proj = mm_rows(act, gm_all).astype(BF16)
    g_hidden, g_bias_fc = feed_hidden_grad(gm_all, hidden, w_p)
    g_odd = feed_grad(shape, meta, g_hidden, fc_parts, 1, half_rows)
    g_even = feed_grad(shape, meta, after(g_hidden, g_odd), fc_parts, 0, half_rows)
    g_total, g_low = ctx_scatter_cores(g_even, g_odd)
    cn_late, act_late, g_low = lax.optimization_barrier((cn_all, act, g_low))
    g_parts = ctx_scatter_sent(g_low, tokens)
    late = feed_late(act_late, w_p, cn_late, g_hidden)
    g_parts, late = lax.optimization_barrier((g_parts, late))
    grad_second = ctx_scatter_sum(g_total, g_parts)
    d_proj = [
        z_scatter_queued(after(part, *w_p)) for part in (d_proj[:, : width // 2], d_proj[:, width // 2 :])
    ]
    d_fc = [z_scatter_queued(part) for part in late[2:]]
    r_total, r_low = ctx_scatter_cores(*late[:2])

    grad_mid_norm, grad_gain_two, grad_shift_two = norm_backward(
        grad_second, normed_two, inverse_two, gain_two
    )
    grad_middle = grad_out + grad_mid_norm
    grad_branch = grad_middle.astype(BF16)
    go_own = times_blocks(meta, grad_branch, out_blocks, out_layout, True).astype(BF16)
    grads = jnp.concatenate(
        [
            go_own.reshape(tokens, ctx_count, q_width),
            grad_branch.reshape(tokens, ctx_count, q_width),
        ],
        axis=2,
    )
    grads_sent = jnp.transpose(grads, (1, 0, 2))
    grads = ctx_exchange(grads_sent).reshape(ctx_count * tokens, 2 * q_width)
    grads, r_total = lax.optimization_barrier((grads, r_total))

    gq_even, gq_odd, gkv_even, gkv_odd, ga_even, ga_odd = attend_grad(
        shape, meta, q_all, kv_all, o_t, lse, grads
    )
    first_sent = [ctx_swap(part[None], chip_masks(side)[0]) for side, part in enumerate(d_proj)]
    r_parts = ctx_scatter_sent(r_low, tokens, [grads_sent])
    gkv_odd, first_sent, r_parts = lax.optimization_barrier((gkv_odd, first_sent, r_parts))
    result = (middle + (ctx_scatter_sum(r_total, r_parts) + proj_bias)).astype(BF16)
    gkv_plane = ctx_scatter(gkv_even, gkv_odd)
    d_proj = ctx_gather_halves(
        *d_proj, wait=lambda part: after(part, gkv_plane), begun=first_sent
    )
    gkv_low = z_sum_exchange(gkv_plane.astype(BF16).reshape(fsdp_count, tokens, 2 * HD)).astype(BF16)
    gkv_all = ctx_exchange(jnp.broadcast_to(gkv_low[None], (ctx_count,) + gkv_low.shape))
    gl_total, gl_low = ctx_scatter_cores(mm_t(gq_even, w_q), mm_t(gq_odd, w_q))
    gl_parts = ctx_scatter_sent(gl_low, tokens, [gkv_plane])
    gkv_all, gl_parts = lax.optimization_barrier((gkv_all, gl_parts))
    (gkv_all,) = place_blocks(
        meta,
        [gkv_all],
        [(ctx_count * tokens, 2 * HD)],
        lambda ref: [
            (
                0,
                (ref[0] ^ (2 * chip + parity),),
                0,
                (pl.ds((parity * chips + chip) * tokens, tokens),),
            )
            for parity in range(2)
            for chip in range(chips)
        ],
        "place_keys",
    )
    gkv_even, gkv_odd = gkv_all[: chips * tokens], gkv_all[chips * tokens :]
    grad_first = ctx_scatter_sum(gl_total, gl_parts)
    grad_in_norm, grad_gain_one, grad_shift_one = norm_backward(
        grad_first + mm_t(gkv_low, w_kv), normed_one, inverse_one, gain_one
    )
    grad_inputs = grad_middle + grad_in_norm

    grad_w_proj = spread_rows(meta, d_proj)
    d_fc = ctx_gather_halves(
        *[after(part, gkv_low) for part in d_fc], last=lambda part: after(part, grad_w_proj)
    )
    (grad_w_fc,) = spread_columns(meta, d_fc, fsdp_count // 2, True)
    d_q = mm_rows(a_even, gq_even) + mm_rows(a_odd, gq_odd)
    d_out = mm_rows(o_even, ga_even) + mm_rows(o_odd, ga_odd)
    d_pair = with_layout_constraint(
        jnp.concatenate([d_q, d_out], axis=1).astype(BF16), Layout(major_to_minor=(0, 1))
    )
    d_pair = z_scatter_queued(d_pair)
    d_kv = (mm_rows(a_even, gkv_even) + mm_rows(a_odd, gkv_odd)).astype(BF16)
    d_kv = z_scatter_queued(d_kv).astype(F32)
    d_pair = [
        (values.reshape(chips, shard, 2 * q_width), [2 * at + parity for at in range(chips)])
        for parity, values in enumerate(ctx_gather(d_pair))
    ]
    grad_w_qkv, grad_w_out = spread_columns(meta, [d_pair] * 2, 1, False, d_kv)

    def column_sum(*parts):
        return sum(jnp.sum(part, axis=0, dtype=F32) for part in parts)

    g_bias_q = lax.dynamic_update_index_in_dim(
        jnp.zeros((ctx_count, q_width), F32), column_sum(gq_even, gq_odd), c_at, 0
    ).reshape(-1)
    g_bias_fc = lax.dynamic_update_index_in_dim(
        jnp.zeros((fsdp_count, ctx_count, unit), F32), g_bias_fc.reshape(fsdp_count, unit), c_at, 1
    ).reshape(-1)
    g_vectors = [
        grad_gain_one,
        grad_shift_one,
        g_bias_q,
        column_sum(gkv_low[:, HD:]),
        column_sum(grad_branch),
        grad_gain_two,
        grad_shift_two,
        g_bias_fc,
        column_sum(grad_mlp),
    ]
    stacked = jnp.concatenate(
        [member.reshape(fsdp_count, -1) for member in g_vectors], axis=1
    ).astype(BF16)
    own = z_sum_exchange(stacked).astype(BF16)
    own = ctx_exchange(jnp.broadcast_to(own[None], (ctx_count,) + own.shape))
    summed = jnp.sum(own, axis=0, dtype=F32)
    vector_grads, start = [], 0
    for size in sizes:
        vector_grads.append(summed[start : start + size].astype(BF16).astype(F32))
        start += size
    return (
        result.reshape(inputs.shape),
        grad_inputs.reshape(inputs.shape),
        grad_w_qkv,
        grad_w_out,
        grad_w_fc,
        grad_w_proj,
        *vector_grads,
    )


def solution(mesh):
    rows_placed = P(None, "ctx", None, "fsdp", None)
    matrix, vector = P("fsdp", None), P("fsdp")
    return jax.shard_map(
        body,
        mesh=mesh,
        in_specs=(rows_placed,) + (matrix,) * 4 + (vector,) * 9 + (rows_placed, P(), P()),
        out_specs=(rows_placed, rows_placed) + (matrix,) * 4 + (vector,) * 9,
        check_vma=False,
    )
```

```python
import functools
import math

import jax
import jax.numpy as jnp
from jax import lax
from jax.experimental.layout import Layout, with_layout_constraint
from jax.experimental import pallas as pl
from jax.experimental.pallas import tpu as pltpu
from jax.sharding import PartitionSpec as P

HEADS = 16
HD = 128
NORM_EPS = 1e-05
MASKED = -1e30
KEY_TILE = 512
LANE_ROWS = 256
SCALE = 1.0 / math.sqrt(HD)
F32 = jnp.float32
BF16 = jnp.bfloat16


def layer_norm(values, gain_vec, shift_vec):
    centred = values - jnp.mean(values, axis=-1, keepdims=True)
    inverse = lax.rsqrt(jnp.mean(centred * centred, axis=-1, keepdims=True) + NORM_EPS)
    normed = centred * inverse
    return (normed * gain_vec + shift_vec, normed, inverse)


def norm_backward(grad_norm, normed, inverse, gain_vec):
    scaled = grad_norm * gain_vec
    centred = scaled - jnp.mean(scaled, axis=-1, keepdims=True)
    centred = centred - normed * jnp.mean(scaled * normed, axis=-1, keepdims=True)
    return (centred * inverse, jnp.sum(grad_norm * normed, axis=0), jnp.sum(grad_norm, axis=0))


def gelu_tanh(values):
    return jax.nn.gelu(values, approximate=True)


def mm(left, right):
    return jnp.dot(left, right, preferred_element_type=F32)


def mm_t(left, right):
    return lax.dot_general(left, right, (((1,), (1,)), ((), ())), preferred_element_type=F32)


def mm_rows(left, right):
    return lax.dot_general(left, right, (((0,), (0,)), ((), ())), preferred_element_type=F32)


def after(values, *ready):
    return lax.optimization_barrier((values, *ready))[0] if ready else values


def ctx_swap(values, mask):
    count = lax.axis_size("ctx")
    return lax.ppermute(values, "ctx", [(at, at ^ mask) for at in range(count)])


def ctx_gather(values, ready=()):
    chips = lax.axis_size("ctx") // 2
    mine = jnp.concatenate([values] + [ctx_swap(values, 2 * at) for at in range(1, chips)], axis=0)
    mine = after(mine, *ready)
    return mine, ctx_swap(mine, 1)


def ctx_gather_all(values):
    return jnp.concatenate(ctx_gather(values), axis=0)


def ctx_scatter(even, odd, ready=(), finish=()):
    return ctx_scatter_chips(*ctx_scatter_cores(even, odd), ready, finish)


def ctx_scatter_cores(even, odd):
    rows = even.shape[0] // (lax.axis_size("ctx") // 2)
    both = even.astype(F32) + ctx_swap(odd.astype(BF16), 1).astype(F32)
    return both[:rows], both[rows:].astype(BF16)


def ctx_scatter_chips(total, low, ready=(), finish=()):
    return ctx_scatter_sum(total, ctx_scatter_sent(low, total.shape[0], ready), finish)


def ctx_scatter_sent(low, rows, ready=()):
    low = after(low, *ready)
    return [
        ctx_swap(low[(at - 1) * rows : at * rows], 2 * at)
        for at in range(1, lax.axis_size("ctx") // 2)
    ]


def ctx_scatter_sum(total, parts, finish=()):
    for part in parts:
        total = total + after(part, *finish).astype(F32)
    return total


def chip_masks(side):
    masks, mask = [], lax.axis_size("ctx") // 2
    while mask > 1:
        masks.append(mask)
        mask //= 2
    return masks[1:] + masks[:1] if side else masks


def ctx_gather_halves(
    first, second, wait=lambda values: values, last=lambda values: values, begun=None
):
    held, offsets = [first[None], second[None]], [[0], [0]]
    steps = len(chip_masks(0))
    for step in range(steps):
        sent = []
        for side in range(2):
            mask = chip_masks(side)[step]
            got = begun[side] if begun and step == 0 else ctx_swap(held[side], mask)
            sent.append((got, [at ^ mask for at in offsets[side]]))
        if step < steps - 1:
            for side in range(2):
                held[side] = jnp.concatenate([held[side], wait(sent[side][0])], axis=0)
                offsets[side] = offsets[side] + sent[side][1]
    gathered = []
    for side in range(2):
        parts = [(held[side], offsets[side]), (last(sent[side][0]), sent[side][1])]
        gathered.append(
            parts + [(ctx_swap(block, 1), [at ^ 1 for at in order]) for block, order in parts]
        )
    return gathered


def ctx_scatter_halves(even, odd, ready=(), finish=()):
    chips = lax.axis_size("ctx") // 2
    rows = even.shape[0] // chips
    both = even.astype(F32) + ctx_swap(odd.astype(BF16), 1).astype(F32)
    both = both.reshape(chips, 2, rows // 2, -1)
    totals = []
    for side in range(2):
        blocks = {2 * at: both[at, side] for at in range(chips)}
        for step, mask in enumerate(reversed(chip_masks(side))):
            kept = [offset for offset in sorted(blocks) if not offset & mask]
            sent = jnp.stack([blocks[offset ^ mask].astype(BF16) for offset in kept])
            got = ctx_swap(after(sent, *ready) if step == 0 else sent, mask)
            if len(kept) == 1:
                got = after(got, *finish)
            blocks = {offset: blocks[offset] + got[at].astype(F32) for at, offset in enumerate(kept)}
        totals.append(blocks[0])
    return jnp.concatenate(totals, axis=0)


def in_order(parts, parity):
    blocks = {
        offset: values[at]
        for values, order in parts
        for at, offset in enumerate(order)
        if offset % 2 == parity
    }
    return jnp.concatenate([blocks[offset] for offset in sorted(blocks)], axis=0)


def ctx_exchange(values):
    return lax.all_to_all(values, "ctx", 0, 0, tiled=True)


def z_masks(count):
    masks = []
    while count > 1:
        masks.append(count - 1)
        count //= 2
    return masks


def z_offsets(count):
    offsets = [0]
    for mask in z_masks(count):
        offsets = offsets + [at ^ mask for at in offsets]
    return offsets


def z_swap(values, mask):
    count = lax.axis_size("fsdp")
    return lax.ppermute(values, "fsdp", [(at, at ^ mask) for at in range(count)])


def z_gather_steps(values):
    held = values[None]
    own = z_swap(held, 1)
    for mask in z_masks(lax.axis_size("fsdp"))[:-1]:
        held = jnp.concatenate([held, z_swap(held, mask)], axis=0)
    return held, own


def z_gather_finish(held, own):
    if held.shape[0] == 1:
        return [held, own]
    return [held, own, z_swap(held[1:], 1)]


def z_gather_parts(values):
    return z_gather_finish(*z_gather_steps(values))


def z_gather_held(values):
    held = values[None]
    for mask in z_masks(lax.axis_size("fsdp"))[:-1]:
        held = jnp.concatenate([held, z_swap(held, mask)], axis=0)
    return held


def z_sum_exchange(values):
    return jnp.sum(lax.all_to_all(values, "fsdp", 0, 0, tiled=True), axis=0, dtype=F32)


def z_gather_queued(values):
    return lax.all_gather(values, "fsdp", axis=0, tiled=True)


def z_scatter_queued(values):
    return lax.psum_scatter(values, "fsdp", scatter_dimension=0, tiled=True)


def place_kernel(plan, n_in, meta, *refs):
    ins, outs = refs[:n_in], refs[n_in:]
    for source, rows_in, target, rows_out in plan(meta):
        outs[target][rows_out] = ins[source][rows_in]


def place_blocks(meta, sources, outs, plan, name):
    return pl.pallas_call(
        functools.partial(place_kernel, plan, len(sources)),
        grid_spec=pltpu.PrefetchScalarGridSpec(
            num_scalar_prefetch=1,
            grid=(1,),
            in_specs=[pl.BlockSpec(memory_space=pltpu.VMEM)] * len(sources),
            out_specs=[pl.BlockSpec(memory_space=pltpu.VMEM)] * len(outs),
        ),
        out_shape=[jax.ShapeDtypeStruct(out, sources[0].dtype) for out in outs],
        compiler_params=pltpu.CompilerParams(vmem_limit_bytes=56 * 2**20),
        name=name,
    )(meta, *sources)


class Shape:
    def __init__(self, ctx_count, fsdp_count, slots, rows):
        self.ctx_count, self.fsdp_count, self.slots, self.rows = ctx_count, fsdp_count, slots, rows
        self.heads = HEADS // ctx_count
        self.block = rows * fsdp_count
        self.blocks = 2 * ctx_count
        self.keys = self.block * self.blocks
        self.tokens = slots * 2 * rows
        self.q_blocks = LANE_ROWS // (self.heads * rows)
        self.head_rows = self.q_blocks * rows
        self.q_tiles = self.blocks // self.q_blocks
        self.q_rows = self.q_tiles * LANE_ROWS
        self.chips = ctx_count // 2
        self.offsets = z_offsets(fsdp_count)


    def part_starts(self, count):
        half = self.fsdp_count // 2
        return [0, half, half + 1][:count]

    def part_of(self, at, count):
        starts = self.part_starts(count)
        part = max(index for index, start in enumerate(starts) if at >= start)
        return part, at - starts[part]


def for_blocks(shape, meta, act):
    me = meta[0]

    def step(chip, carry):
        for parity in range(2):
            first = meta[6 + (me ^ (2 * chip + parity))]
            for slot in range(shape.slots):
                for half in range(2):
                    block = first if half == 0 else shape.blocks - 1 - first
                    act(parity, chip, slot, half, block)
        return carry

    lax.fori_loop(0, shape.chips, step, 0)


def at_rows(start, size, unit):
    return pl.ds(pl.multiple_of(start, unit), size)


def q_source(shape, chip, slot, half):
    return at_rows(chip * shape.tokens + (slot * 2 + half) * shape.rows, shape.rows, shape.rows)


def q_target(shape, block, head):
    start = (block // shape.q_blocks) * LANE_ROWS + (block % shape.q_blocks) * shape.rows
    return at_rows(start + head * shape.head_rows, shape.rows, shape.rows)


def kv_source(shape, chip, order, slot, half):
    start = (chip * shape.fsdp_count + order) * shape.tokens + (slot * 2 + half) * shape.rows
    return at_rows(start, shape.rows, shape.rows)


def kv_target(shape, meta, block, order):
    start = block * shape.block + (meta[1] ^ shape.offsets[order]) * shape.rows
    return at_rows(start, shape.rows, shape.rows)


def query_bounds(shape, meta, slot, tile):
    lane = lax.broadcasted_iota(jnp.int32, (1, LANE_ROWS), 1)
    row = lane % shape.head_rows
    pos = (tile * shape.q_blocks + row // shape.rows) * shape.block + meta[1] * shape.rows + row % shape.rows
    first_end = meta[2 + 2 * slot]
    second_end = first_end + meta[3 + 2 * slot]

    def start_of(at):
        return jnp.where(at < first_end, 0, jnp.where(at < second_end, first_end, second_end))

    first_pos = tile * shape.q_blocks * shape.block + meta[1] * shape.rows
    last_pos = first_pos + (shape.q_blocks - 1) * shape.block + shape.rows - 1
    return pos, start_of(pos), start_of(first_pos) // KEY_TILE, last_pos // KEY_TILE + 1


def visible(pos, start, tile):
    key_pos = tile * KEY_TILE + lax.broadcasted_iota(jnp.int32, (KEY_TILE, LANE_ROWS), 0)
    return (key_pos <= pos) & (key_pos >= start)


def device_rows(shape, meta, parity, chip, slot, half):
    device = meta[0] ^ (2 * chip + parity)
    return at_rows(device * shape.tokens + (slot * 2 + half) * shape.rows, shape.rows, shape.rows)


def attend_kernel(shape, meta, q_even, q_odd, kv_even, kv_odd, o_out, q_all, kv_all, o_t, lse, o_rows):
    queries, keys = (q_even, q_odd), (kv_even, kv_odd)

    def place(parity, chip, slot, half, block):
        for head in range(shape.heads):
            q_all[slot, q_target(shape, block, head), :] = queries[parity][
                q_source(shape, chip, slot, half), head * HD : (head + 1) * HD
            ]
        for order in range(shape.fsdp_count):
            kv_all[slot, kv_target(shape, meta, block, order), :] = keys[parity][
                kv_source(shape, chip, order, slot, half), :
            ]

    for_blocks(shape, meta, place)

    def tile_step(item, carry):
        slot, tile = item // shape.q_tiles, item % shape.q_tiles
        pos, start, low, high = query_bounds(shape, meta, slot, tile)
        q_tile = q_all[slot, at_rows(tile * LANE_ROWS, LANE_ROWS, LANE_ROWS), :]

        def key_step(at, state):
            peak, total, acc = state
            part = at_rows(at * KEY_TILE, KEY_TILE, KEY_TILE)
            scores = mm_t(kv_all[slot, part, :HD], q_tile) * SCALE
            scores = jnp.where(visible(pos, start, at), scores, MASKED)
            new_peak = jnp.maximum(peak, jnp.max(scores, axis=0, keepdims=True))
            fade = jnp.exp(peak - new_peak)
            weights = jnp.exp(scores - new_peak)
            total = total * fade + jnp.sum(weights, axis=0, keepdims=True)
            acc = acc * fade + mm_rows(kv_all[slot, part, HD:], weights.astype(BF16))
            return new_peak, total, acc

        begin = (
            jnp.full((1, LANE_ROWS), MASKED, F32),
            jnp.zeros((1, LANE_ROWS), F32),
            jnp.zeros((HD, LANE_ROWS), F32),
        )
        peak, total, acc = lax.fori_loop(low, high, key_step, begin)
        acc = acc / total
        o_t[item] = acc
        lse[item] = peak + jnp.log(total)
        o_rows[slot, at_rows(tile * LANE_ROWS, LANE_ROWS, LANE_ROWS), :] = acc.T.astype(BF16)
        return carry

    lax.fori_loop(0, shape.slots * shape.q_tiles, tile_step, 0)

    def put_back(parity, chip, slot, half, block):
        for head in range(shape.heads):
            o_out[device_rows(shape, meta, parity, chip, slot, half), head * HD : (head + 1) * HD] = o_rows[
                slot, q_target(shape, block, head), :
            ]

    for_blocks(shape, meta, put_back)


def attend_grad_kernel(
    shape, meta, q_all, kv_all, o_t, lse, grads, gq_even, gq_odd, gkv_even, gkv_odd, ga_even, ga_odd, go_all, gq_all, gkv_all
):
    g_queries, g_keys, g_branch = (gq_even, gq_odd), (gkv_even, gkv_odd), (ga_even, ga_odd)

    def place(parity, chip, slot, half, block):
        source = device_rows(shape, meta, parity, chip, slot, half)
        for head in range(shape.heads):
            go_all[slot, q_target(shape, block, head), :] = grads[source, head * HD : (head + 1) * HD]
        g_branch[parity][q_source(shape, chip, slot, half), :] = grads[source, shape.heads * HD :]

    for_blocks(shape, meta, place)
    gkv_all[...] = jnp.zeros_like(gkv_all)

    def tile_step(item, carry):
        slot, tile = item // shape.q_tiles, item % shape.q_tiles
        pos, start, low, high = query_bounds(shape, meta, slot, tile)
        rows = at_rows(tile * LANE_ROWS, LANE_ROWS, LANE_ROWS)
        q_tile = q_all[slot, rows, :]
        go_tile = go_all[slot, rows, :]
        delta = jnp.sum(go_tile.astype(F32).T * o_t[item], axis=0, keepdims=True)
        lse_row = lse[item]

        def key_step(at, acc):
            part = at_rows(at * KEY_TILE, KEY_TILE, KEY_TILE)
            key_part, value_part = kv_all[slot, part, :HD], kv_all[slot, part, HD:]
            scores = mm_t(key_part, q_tile) * SCALE
            probs = jnp.where(visible(pos, start, at), jnp.exp(scores - lse_row), 0.0)
            g_scores = (probs * (mm_t(value_part, go_tile) - delta)).astype(BF16)
            gkv_all[slot, part, :HD] += mm(g_scores, q_tile)
            gkv_all[slot, part, HD:] += mm(probs.astype(BF16), go_tile)
            return acc + mm_rows(key_part, g_scores)

        acc = lax.fori_loop(low, high, key_step, jnp.zeros((HD, LANE_ROWS), F32))
        gq_all[slot, rows, :] = (acc * SCALE).T.astype(BF16)
        return carry

    lax.fori_loop(0, shape.slots * shape.q_tiles, tile_step, 0)

    def put_back(parity, chip, slot, half, block):
        for head in range(shape.heads):
            g_queries[parity][q_source(shape, chip, slot, half), head * HD : (head + 1) * HD] = gq_all[
                slot, q_target(shape, block, head), :
            ]
        for order in range(shape.fsdp_count):
            target = kv_target(shape, meta, block, order)
            source = kv_source(shape, chip, meta[1] ^ shape.offsets[order], slot, half)
            g_keys[parity][source, :HD] = (gkv_all[slot, target, :HD] * SCALE).astype(BF16)
            g_keys[parity][source, HD:] = gkv_all[slot, target, HD:].astype(BF16)

    for_blocks(shape, meta, put_back)


def attend(shape, meta, q_even, q_odd, kv_even, kv_odd):
    items = shape.slots * shape.q_tiles
    pairs = items * LANE_ROWS * shape.keys // 2
    return pl.pallas_call(
        functools.partial(attend_kernel, shape),
        grid_spec=pltpu.PrefetchScalarGridSpec(
            num_scalar_prefetch=1,
            grid=(1,),
            in_specs=[pl.BlockSpec(memory_space=pltpu.VMEM)] * 4,
            out_specs=[pl.BlockSpec(memory_space=pltpu.VMEM)] * 5,
            scratch_shapes=[pltpu.VMEM((shape.slots, shape.q_rows, HD), BF16)],
        ),
        out_shape=[
            jax.ShapeDtypeStruct((shape.ctx_count * shape.tokens, shape.heads * HD), BF16),
            jax.ShapeDtypeStruct((shape.slots, shape.q_rows, HD), BF16),
            jax.ShapeDtypeStruct((shape.slots, shape.keys, 2 * HD), BF16),
            jax.ShapeDtypeStruct((items, HD, LANE_ROWS), F32),
            jax.ShapeDtypeStruct((items, 1, LANE_ROWS), F32),
        ],
        compiler_params=pltpu.CompilerParams(vmem_limit_bytes=56 * 2**20),
        cost_estimate=pl.CostEstimate(flops=pairs * HD * 4, transcendentals=pairs, bytes_accessed=8 * 2**20),
        name="attend",
    )(meta, q_even, q_odd, kv_even, kv_odd)


def attend_grad(shape, meta, q_all, kv_all, o_t, lse, grads):
    items = shape.slots * shape.q_tiles
    q_like = jax.ShapeDtypeStruct((shape.chips * shape.tokens, shape.heads * HD), BF16)
    kv_like = jax.ShapeDtypeStruct((shape.chips * shape.fsdp_count * shape.tokens, 2 * HD), BF16)
    pairs = items * LANE_ROWS * shape.keys // 2
    return pl.pallas_call(
        functools.partial(attend_grad_kernel, shape),
        grid_spec=pltpu.PrefetchScalarGridSpec(
            num_scalar_prefetch=1,
            grid=(1,),
            in_specs=[pl.BlockSpec(memory_space=pltpu.VMEM)] * 5,
            out_specs=[pl.BlockSpec(memory_space=pltpu.VMEM)] * 6,
            scratch_shapes=[
                pltpu.VMEM((shape.slots, shape.q_rows, HD), BF16),
                pltpu.VMEM((shape.slots, shape.q_rows, HD), BF16),
                pltpu.VMEM((shape.slots, shape.keys, 2 * HD), F32),
            ],
        ),
        out_shape=[q_like, q_like, kv_like, kv_like, q_like, q_like],
        compiler_params=pltpu.CompilerParams(vmem_limit_bytes=56 * 2**20),
        cost_estimate=pl.CostEstimate(flops=pairs * HD * 10, transcendentals=pairs, bytes_accessed=10 * 2**20),
        name="attend_grad",
    )(meta, q_all, kv_all, o_t, lse, grads)


def block_of(shape, parts, at):
    part, block = shape.part_of(at, len(parts))
    return parts[part][block]


def gelu_parts(values):
    root = math.sqrt(2.0 / math.pi)
    return jnp.tanh(root * (values + 0.044715 * (values * values * values)))


def hidden_kernel(shape, meta, rows_ref, bias_ref, *refs):
    parts, (hidden_ref, act_ref) = refs[:-2], refs[-2:]
    depth = parts[0].shape[1]
    total = bias_ref[...]
    for at, offset in enumerate(shape.offsets):
        part = pl.ds(pl.multiple_of((meta[1] ^ offset) * depth, depth), depth)
        total = total + mm(rows_ref[:, part], block_of(shape, parts, at))
    hidden_ref[...] = total
    act_ref[...] = (0.5 * total * (1.0 + gelu_parts(total))).astype(BF16)


def feed_hidden(shape, meta, rows, parts, bias):
    count, width = rows.shape
    _, depth, columns = parts[0].shape
    tile = 256
    weights = [
        pl.BlockSpec((part.shape[0], depth, tile), lambda i, m: (0, 0, i)) for part in parts
    ]
    out = pl.BlockSpec((count, tile), lambda i, m: (0, i))
    return pl.pallas_call(
        functools.partial(hidden_kernel, shape),
        grid_spec=pltpu.PrefetchScalarGridSpec(
            num_scalar_prefetch=1,
            grid=(columns // tile,),
            in_specs=[
                pl.BlockSpec((count, width), lambda i, m: (0, 0)),
                pl.BlockSpec((1, tile), lambda i, m: (0, i)),
                *weights,
            ],
            out_specs=[out, out],
        ),
        out_shape=[
            jax.ShapeDtypeStruct((count, columns), F32),
            jax.ShapeDtypeStruct((count, columns), BF16),
        ],
        compiler_params=pltpu.CompilerParams(vmem_limit_bytes=56 * 2**20),
        cost_estimate=pl.CostEstimate(
            flops=2 * count * width * columns,
            transcendentals=count * columns,
            bytes_accessed=2 * (count * width + width * columns) + 6 * count * columns,
        ),
        name="feed_hidden",
    )(meta, rows, bias, *parts)


def hidden_grad_kernel(grads_ref, hidden_ref, first, second, out_ref, sum_ref):
    values = hidden_ref[...]
    tanh = gelu_parts(values)
    root = math.sqrt(2.0 / math.pi)
    slope = 0.5 * (1.0 + tanh) + (0.5 * root) * values * (1.0 - tanh * tanh) * (
        1.0 + (3.0 * 0.044715) * (values * values)
    )
    width = first.shape[1]
    grads = mm_t(grads_ref[:, :width], first[...]) + mm_t(grads_ref[:, width:], second[...])
    low = (grads * slope).astype(BF16)
    out_ref[...] = low
    sum_ref[...] = jnp.sum(low.astype(F32), axis=0, keepdims=True)


def feed_hidden_grad(grads, hidden, weights):
    count, width = grads.shape
    columns = hidden.shape[1]
    tile = 256
    place = pl.BlockSpec((count, tile), lambda i: (0, i))
    return pl.pallas_call(
        hidden_grad_kernel,
        grid=(columns // tile,),
        in_specs=[pl.BlockSpec((count, width), lambda i: (0, 0)), place]
        + [pl.BlockSpec((tile, width // 2), lambda i: (i, 0))] * 2,
        out_specs=[place, pl.BlockSpec((1, tile), lambda i: (0, i))],
        out_shape=[
            jax.ShapeDtypeStruct((count, columns), BF16),
            jax.ShapeDtypeStruct((1, columns), F32),
        ],
        compiler_params=pltpu.CompilerParams(vmem_limit_bytes=56 * 2**20),
        cost_estimate=pl.CostEstimate(
            flops=2 * count * width * columns,
            transcendentals=count * columns,
            bytes_accessed=2 * (count * width + width * columns) + 6 * count * columns,
        ),
        name="feed_hidden_grad",
    )(grads, hidden, *weights)


def feed_late_kernel(steps, rows_ref, first, second, norm_ref, grads_ref, even_ref, odd_ref, *d_refs):
    at = pl.program_id(0)
    width = first.shape[1]
    for side, out_ref in enumerate((even_ref, odd_ref)):

        @pl.when(at // steps == side)
        def _(out_ref=out_ref):
            out_ref[:, :width] = mm(rows_ref[...], first[...]).astype(BF16)
            out_ref[:, width:] = mm(rows_ref[...], second[...]).astype(BF16)

    @pl.when(at >= 2 * steps)
    def _():
        columns = d_refs[0].shape[1]
        for part, out_ref in enumerate(d_refs):
            out_ref[...] = mm_rows(
                norm_ref[...], grads_ref[:, part * columns : (part + 1) * columns]
            ).astype(BF16)


def feed_late(rows, weights, norm, grads):
    depth, half_width = weights[0].shape
    count, tile = rows.shape[0] // 2, 256
    steps = count // tile
    width, columns = norm.shape[1], grads.shape[1]
    last = 2 * steps - 1
    d_block = pl.BlockSpec((tile, columns // 2), lambda i: (jnp.maximum(i - last - 1, 0), 0))
    return pl.pallas_call(
        functools.partial(feed_late_kernel, steps),
        grid=(2 * steps + width // tile,),
        in_specs=[
            pl.BlockSpec((tile, depth), lambda i: (jnp.minimum(i, last), 0)),
            pl.BlockSpec((depth, half_width), lambda i: (0, 0)),
            pl.BlockSpec((depth, half_width), lambda i: (0, 0)),
            pl.BlockSpec((2 * count, tile), lambda i: (0, jnp.maximum(i - last - 1, 0))),
            pl.BlockSpec((2 * count, columns), lambda i: (0, 0)),
        ],
        out_specs=[
            pl.BlockSpec((tile, 2 * half_width), lambda i: (jnp.minimum(i, steps - 1), 0)),
            pl.BlockSpec((tile, 2 * half_width), lambda i: (jnp.clip(i - steps, 0, steps - 1), 0)),
            d_block,
            d_block,
        ],
        out_shape=[jax.ShapeDtypeStruct((count, 2 * half_width), BF16)] * 2
        + [jax.ShapeDtypeStruct((width, columns // 2), BF16)] * 2,
        compiler_params=pltpu.CompilerParams(vmem_limit_bytes=56 * 2**20),
        cost_estimate=pl.CostEstimate(
            flops=8 * count * depth * half_width + 4 * count * width * columns,
            transcendentals=0,
            bytes_accessed=2 * (6 * count * half_width + 2 * depth * half_width + 4 * count * width),
        ),
        name="feed_late",
    )(rows, *weights, norm, grads)


def feed_grad_kernel(shape, meta, rows_ref, *refs):
    parts, out_ref = refs[:-1], refs[-1]
    for at, offset in enumerate(shape.offsets):
        block = block_of(shape, parts, at)
        size = block.shape[0]
        part = pl.ds(pl.multiple_of((meta[1] ^ offset) * size, size), size)
        out_ref[:, part] = mm_t(rows_ref[...], block).astype(BF16)


def feed_grad(shape, meta, rows, parts, side, count):
    width = shape.fsdp_count * parts[0].shape[1]
    tile = 256
    steps = count // tile
    return pl.pallas_call(
        functools.partial(feed_grad_kernel, shape),
        grid_spec=pltpu.PrefetchScalarGridSpec(
            num_scalar_prefetch=1,
            grid=(steps,),
            in_specs=[
                pl.BlockSpec((tile, rows.shape[1]), lambda i, m: (side * steps + i, 0)),
                *[pl.BlockSpec(part.shape, lambda i, m: (0, 0, 0)) for part in parts],
            ],
            out_specs=pl.BlockSpec((tile, width), lambda i, m: (i, 0)),
        ),
        out_shape=jax.ShapeDtypeStruct((count, width), BF16),
        compiler_params=pltpu.CompilerParams(vmem_limit_bytes=56 * 2**20),
        cost_estimate=pl.CostEstimate(
            flops=2 * count * rows.shape[1] * width,
            transcendentals=0,
            bytes_accessed=2 * (count + width) * rows.shape[1] + 2 * count * width,
        ),
        name="feed_grad",
    )(meta, rows, *parts)


def branch_kernel(layout, grad, meta, rows_ref, *refs):
    parts, out_ref = refs[:-1], refs[-1]
    out_ref[...] = jnp.zeros_like(out_ref)
    for part, (ctx_order, z_order) in zip(parts, layout):
        depth, columns = part.shape[2], part.shape[3]
        for at, ctx_offset in enumerate(ctx_order):
            column = pl.ds(pl.multiple_of((meta[0] ^ ctx_offset) * columns, columns), columns)
            for order, z_offset in enumerate(z_order):
                row = pl.ds(pl.multiple_of((meta[1] ^ z_offset) * depth, depth), depth)
                if grad:
                    out_ref[:, row] += mm_t(rows_ref[:, column], part[at, order])
                else:
                    out_ref[:, column] += mm(rows_ref[:, row], part[at, order])


def times_blocks(meta, rows, parts, layout, grad):
    return pl.pallas_call(
        functools.partial(branch_kernel, layout, grad),
        grid_spec=pltpu.PrefetchScalarGridSpec(
            num_scalar_prefetch=1,
            grid=(1,),
            in_specs=[pl.BlockSpec(memory_space=pltpu.VMEM)] * (1 + len(parts)),
            out_specs=pl.BlockSpec(memory_space=pltpu.VMEM),
        ),
        out_shape=jax.ShapeDtypeStruct(rows.shape, F32),
        compiler_params=pltpu.CompilerParams(vmem_limit_bytes=56 * 2**20),
        cost_estimate=pl.CostEstimate(
            flops=2 * rows.shape[0] * rows.shape[1] ** 2,
            transcendentals=0,
            bytes_accessed=2 * rows.shape[1] ** 2,
        ),
        name="branch_grad" if grad else "branch",
    )(meta, rows, *parts)


def spread_rows_kernel(pieces, steps, meta, *refs):
    out_ref = refs[-1]
    for piece, blocks in enumerate(pieces):

        @pl.when(pl.program_id(0) // steps == piece)
        def _(blocks=blocks):
            for source, block, offset in blocks:
                rows = refs[source].shape[1]
                start = pl.multiple_of((meta[0] ^ offset) * rows, rows)
                out_ref[pl.ds(start, rows), :] = refs[source][block].astype(F32)


def spread_rows(meta, gathered):
    tile = 256
    members, specs, pieces = [], [], []
    for piece, parts in enumerate(gathered):
        blocks = []
        for values, order in parts:
            count, rows, columns = values.shape
            steps = columns // tile
            blocks += [(len(members), at, offset) for at, offset in enumerate(order)]
            members.append(values)

            def place(i, m, piece=piece, steps=steps):
                return (0, 0, jnp.clip(i - piece * steps, 0, steps - 1))

            specs.append(pl.BlockSpec((count, rows, tile), place))
        pieces.append(blocks)
    total = len(pieces[0]) * rows
    return pl.pallas_call(
        functools.partial(spread_rows_kernel, pieces, steps),
        grid_spec=pltpu.PrefetchScalarGridSpec(
            num_scalar_prefetch=1,
            grid=(len(pieces) * steps,),
            in_specs=specs,
            out_specs=pl.BlockSpec((total, tile), lambda i, m: (0, i)),
        ),
        out_shape=jax.ShapeDtypeStruct((total, len(pieces) * columns), F32),
        compiler_params=pltpu.CompilerParams(vmem_limit_bytes=48 * 2**20),
        name="spread_rows",
    )(meta, *members)


def spread_kernel(moves, extras, outs, meta, *refs):
    outs = refs[len(refs) - outs :]
    for source, block, columns, offset, out, start, step, size in moves:
        target = pl.multiple_of(start + (meta[0] ^ offset) * step, size)
        outs[out][:, pl.ds(target, size)] = refs[source][block, :, columns].astype(F32)
    for source, out in extras:
        width = refs[source].shape[1]
        outs[out][:, outs[out].shape[1] - width :] = refs[source][...]


def spread_columns(meta, gathered, groups, joined, extra=None):
    pieces = len(gathered)
    rows, columns = gathered[0][0][0].shape[1:]
    width = columns // groups if joined else columns // pieces
    count = sum(len(order) for _, order in gathered[0])
    if width % 128:
        results = []
        for parts in gathered:
            out = jnp.zeros((count, rows, groups, width), F32)
            for values, order in parts:
                for at, offset in enumerate(order):
                    block = values[at].reshape(rows, groups, width).astype(F32)
                    out = lax.dynamic_update_index_in_dim(out, block, meta[0] ^ offset, 0)
            results.append(jnp.transpose(out, (1, 2, 0, 3)).reshape(rows, -1))
        return [jnp.concatenate(results, axis=1)]
    members, moves = [], []
    for piece, parts in enumerate(gathered):
        if not joined:
            members = []
        for values, order in parts:
            for at, offset in enumerate(order):
                for group in range(groups):
                    start = ((piece if joined else 0) * groups + group) * count * width
                    source = (group if joined else piece) * width
                    moves.append(
                        (
                            len(members),
                            at,
                            slice(source, source + width),
                            offset,
                            0 if joined else piece,
                            start,
                            width,
                            width,
                        )
                    )
            members.append(values)
    sizes = [groups * count * width * pieces] if joined else [count * width] * pieces
    tile = min(rows, 64)
    in_specs = [
        pl.BlockSpec((member.shape[0], tile, columns), lambda i, m: (0, i, 0)) for member in members
    ]
    extras = []
    if extra is not None:
        extras = [(len(members), 0)]
        members.append(extra)
        in_specs.append(pl.BlockSpec((tile, extra.shape[1]), lambda i, m: (i, 0)))
        sizes[0] += extra.shape[1]
    return pl.pallas_call(
        functools.partial(spread_kernel, moves, extras, len(sizes)),
        grid_spec=pltpu.PrefetchScalarGridSpec(
            num_scalar_prefetch=1,
            grid=(rows // tile,),
            in_specs=in_specs,
            out_specs=[pl.BlockSpec((tile, size), lambda i, m: (i, 0)) for size in sizes],
        ),
        out_shape=[jax.ShapeDtypeStruct((rows, size), F32) for size in sizes],
        compiler_params=pltpu.CompilerParams(vmem_limit_bytes=48 * 2**20),
        name="spread_columns",
    )(meta, *members)


def pick_block(pair_table, ctx_at, half_bit):
    ctx_total = pair_table.shape[0]
    chosen = jnp.sum(jnp.where(jnp.arange(ctx_total, dtype=jnp.int32) == ctx_at, pair_table, 0))
    return jnp.where(half_bit == 0, chosen, 2 * ctx_total - 1 - chosen)


def body(
    inputs,
    w_qkv,
    w_out,
    w_fc,
    w_proj,
    ln1_gain,
    ln1_bias,
    bias_q,
    bias_v,
    bias_out,
    ln2_gain,
    ln2_bias,
    bias_fc,
    bias_proj,
    cotangent,
    lengths,
    pair_table,
):
    slots, _, _, rows, width = inputs.shape
    ctx_count, fsdp_count = lax.axis_size("ctx"), lax.axis_size("fsdp")
    c_at, z_at = lax.axis_index("ctx"), lax.axis_index("fsdp")
    shape = Shape(ctx_count, fsdp_count, slots, rows)
    tokens, chips = shape.tokens, shape.chips
    q_width = width // ctx_count
    shard = width // fsdp_count
    hidden_width = w_fc.shape[1]
    unit = hidden_width // (fsdp_count * ctx_count)
    meta = jnp.concatenate(
        [jnp.stack([c_at, z_at]).astype(jnp.int32), lengths.reshape(-1), pair_table]
    ).astype(jnp.int32)

    offsets = jnp.arange(2 * rows, dtype=jnp.int32)
    pos = (
        pick_block(pair_table, c_at, offsets // rows) * shape.block + z_at * rows + offsets % rows
    )
    live = (pos[None, :] < lengths[:, 0:1] + lengths[:, 1:2]).reshape(tokens, 1).astype(F32)

    x_low = inputs.reshape(tokens, width)
    grad_out = cotangent.reshape(tokens, width).astype(F32) * live
    grad_mlp = grad_out.astype(BF16)
    pack_width = q_width + 2 * HD
    w_first = jnp.concatenate(
        [lax.dynamic_slice_in_dim(w_qkv, c_at * q_width, q_width, axis=1), w_qkv[:, width:]], axis=1
    ).astype(BF16)
    vectors = [ln1_gain, ln1_bias, bias_q, bias_v, bias_out, ln2_gain, ln2_bias, bias_fc, bias_proj]
    sizes = [member.shape[0] for member in vectors]
    vector_rows = 16 * math.ceil(sum(sizes) / (16 * HD))
    packed = jnp.concatenate(
        [member.astype(BF16) for member in vectors]
        + [jnp.zeros((vector_rows * HD - sum(sizes),), BF16)]
    ).reshape(vector_rows, HD)
    x_even, x_odd = ctx_gather(after(x_low, w_first))
    half = fsdp_count // 2
    first_held, first_own = z_gather_steps(w_first)
    first_blocks = z_gather_finish(first_held, first_own)
    vector_held = z_gather_held(after(packed, first_held))
    vector_blocks = [vector_held, z_swap(vector_held, 1)]

    def first_plan(ref):
        moves = []
        for at, offset in enumerate(shape.offsets):
            owner, (part, block) = ref[1] ^ offset, shape.part_of(at, len(first_blocks))
            weight_rows = pl.ds(pl.multiple_of(owner * shard, shard), shard)
            q_part, kv_part = pl.ds(0, q_width), pl.ds(q_width, 2 * HD)
            moves += [
                (part, (block, slice(None), q_part), 0, (weight_rows, slice(None))),
                (part, (block, slice(None), kv_part), 1, (weight_rows, slice(None))),
                (len(first_blocks) + at // half, (at % half,), 2, (owner,)),
            ]
        return moves

    w_q, w_kv, packed = place_blocks(
        meta,
        [*first_blocks, *vector_blocks],
        [(width, q_width), (width, 2 * HD), (fsdp_count, vector_rows, HD)],
        first_plan,
        "place_first",
    )
    packed = packed.reshape(fsdp_count, -1)
    full, start = [], 0
    for size in sizes:
        full.append(packed[:, start : start + size].reshape(-1).astype(F32))
        start += size
    gain_one, shift_one, q_bias, v_bias, out_bias, gain_two, shift_two, fc_bias, proj_bias = full
    q_bias = lax.dynamic_slice_in_dim(q_bias, c_at * q_width, q_width)
    fc_bias = lax.dynamic_index_in_dim(
        fc_bias.reshape(fsdp_count, ctx_count, unit), c_at, 1, keepdims=False
    )

    def relative_plan(ref):
        return [
            (
                0,
                (ref[0] ^ (2 * chip + parity),),
                0,
                (pl.ds((parity * chips + chip) * tokens, tokens),),
            )
            for parity in range(2)
            for chip in range(chips)
        ]

    x_own = x_low.astype(F32)
    first_norm, normed_one, inverse_one = layer_norm(x_own, gain_one, shift_one)
    kv_own = mm(first_norm.astype(BF16), w_kv)
    kv_own = jnp.concatenate([kv_own[:, :HD], kv_own[:, HD:] + v_bias], axis=1).astype(BF16)
    kv_z = jnp.concatenate(z_gather_parts(kv_own), axis=0).reshape(fsdp_count * tokens, 2 * HD)
    kv_even, kv_odd = ctx_gather(kv_z)

    out_parts = z_gather_parts(
        after(lax.dynamic_slice_in_dim(w_out, c_at * q_width, q_width, axis=1).astype(BF16), kv_z)
    )

    fc_own = jnp.concatenate(
        [
            lax.dynamic_slice_in_dim(
                w_fc, group * (hidden_width // fsdp_count) + c_at * unit, unit, axis=1
            )
            for group in range(fsdp_count)
        ],
        axis=1,
    ).astype(BF16)
    proj_own = lax.dynamic_slice_in_dim(w_proj, c_at * unit, unit, axis=0).astype(BF16)
    out_halves = out_parts[0], jnp.concatenate(out_parts[1:], axis=0)
    fc_steps = z_gather_steps(after(fc_own, out_parts[0]))

    a_even = layer_norm(x_even.astype(F32), gain_one, shift_one)[0].astype(BF16)
    a_odd = layer_norm(x_odd.astype(F32), gain_one, shift_one)[0].astype(BF16)
    q_even = (mm(a_even, w_q) + q_bias).astype(BF16)
    q_odd = (mm(a_odd, w_q) + q_bias).astype(BF16)
    o_heads, q_all, kv_all, o_t, lse = attend(shape, meta, q_even, q_odd, kv_even, kv_odd)
    out_gathered = ctx_gather_halves(
        *[after(side, kv_even) for side in out_halves],
        wait=lambda part: after(part, kv_odd),
        last=lambda part: after(part, o_heads),
    )
    out_blocks, out_layout = [], []
    for side, parts in enumerate(out_gathered):
        z_order = shape.offsets[side * half : (side + 1) * half]
        for values, order in parts:
            out_blocks.append(values)
            out_layout.append((order, z_order))
    o_own = ctx_exchange(o_heads.reshape(ctx_count, tokens, q_width))
    o_own = jnp.transpose(o_own, (1, 0, 2)).reshape(tokens, width)
    fc_parts = z_gather_finish(*fc_steps)
    proj_own = after(proj_own, fc_parts[-1])
    w_p = [
        z_gather_queued(proj_own[:, at * width // 2 : (at + 1) * width // 2]) for at in range(2)
    ]
    o_own = after(o_own, *fc_steps)
    middle = x_own + (times_blocks(meta, o_own, out_blocks, out_layout, False) + out_bias)
    second_norm, normed_two, inverse_two = layer_norm(middle, gain_two, shift_two)

    o_parts = [ctx_swap(o_own, 2 * at) for at in range(1, chips)]
    cn_own, o_parts = lax.optimization_barrier((second_norm.astype(BF16), o_parts))
    cn_even, cn_odd = ctx_gather(cn_own)
    o_even = jnp.concatenate([o_own, *o_parts], axis=0)
    o_odd = ctx_swap(o_even, 1)
    gm_all = lax.all_gather(grad_mlp, "ctx", axis=0, tiled=False)
    (gm_all,) = place_blocks(
        meta, [gm_all], [(ctx_count * tokens, width)], relative_plan, "place_rows"
    )
    cn_all = jnp.concatenate([cn_even, cn_odd], axis=0)
    half_rows = chips * tokens
    hidden, act = feed_hidden(shape, meta, cn_all, fc_parts, fc_bias.reshape(1, -1))
    d_proj = mm_rows(act, gm_all).astype(BF16)
    g_hidden, g_bias_fc = feed_hidden_grad(gm_all, hidden, w_p)
    g_odd = feed_grad(shape, meta, g_hidden, fc_parts, 1, half_rows)
    g_even = feed_grad(shape, meta, after(g_hidden, g_odd), fc_parts, 0, half_rows)
    g_total, g_low = ctx_scatter_cores(g_even, g_odd)
    cn_late, act_late, g_low = lax.optimization_barrier((cn_all, act, g_low))
    g_parts = ctx_scatter_sent(g_low, tokens)
    late = feed_late(act_late, w_p, cn_late, g_hidden)
    g_parts, late = lax.optimization_barrier((g_parts, late))
    grad_second = ctx_scatter_sum(g_total, g_parts)
    d_proj = [
        z_scatter_queued(after(part, *w_p)) for part in (d_proj[:, : width // 2], d_proj[:, width // 2 :])
    ]
    d_fc = [z_scatter_queued(part) for part in late[2:]]
    r_total, r_low = ctx_scatter_cores(*late[:2])

    grad_mid_norm, grad_gain_two, grad_shift_two = norm_backward(
        grad_second, normed_two, inverse_two, gain_two
    )
    grad_middle = grad_out + grad_mid_norm
    grad_branch = grad_middle.astype(BF16)
    go_own = times_blocks(meta, grad_branch, out_blocks, out_layout, True).astype(BF16)
    grads = jnp.concatenate(
        [
            go_own.reshape(tokens, ctx_count, q_width),
            grad_branch.reshape(tokens, ctx_count, q_width),
        ],
        axis=2,
    )
    grads_sent = jnp.transpose(grads, (1, 0, 2))
    grads = ctx_exchange(grads_sent).reshape(ctx_count * tokens, 2 * q_width)
    grads, r_total = lax.optimization_barrier((grads, r_total))

    gq_even, gq_odd, gkv_even, gkv_odd, ga_even, ga_odd = attend_grad(
        shape, meta, q_all, kv_all, o_t, lse, grads
    )
    first_sent = [ctx_swap(part[None], chip_masks(side)[0]) for side, part in enumerate(d_proj)]
    r_parts = ctx_scatter_sent(r_low, tokens, [grads_sent])
    gkv_odd, first_sent, r_parts = lax.optimization_barrier((gkv_odd, first_sent, r_parts))
    result = (middle + (ctx_scatter_sum(r_total, r_parts) + proj_bias)).astype(BF16)
    gkv_plane = ctx_scatter(gkv_even, gkv_odd)
    d_proj = ctx_gather_halves(
        *d_proj, wait=lambda part: after(part, gkv_plane), begun=first_sent
    )
    gkv_low = z_sum_exchange(gkv_plane.astype(BF16).reshape(fsdp_count, tokens, 2 * HD)).astype(BF16)
    gkv_all = ctx_exchange(jnp.broadcast_to(gkv_low[None], (ctx_count,) + gkv_low.shape))
    gl_total, gl_low = ctx_scatter_cores(mm_t(gq_even, w_q), mm_t(gq_odd, w_q))
    gl_parts = ctx_scatter_sent(gl_low, tokens, [gkv_plane])
    gkv_all, gl_parts = lax.optimization_barrier((gkv_all, gl_parts))
    (gkv_all,) = place_blocks(
        meta,
        [gkv_all],
        [(ctx_count * tokens, 2 * HD)],
        relative_plan,
        "place_keys",
    )
    gkv_even, gkv_odd = gkv_all[: chips * tokens], gkv_all[chips * tokens :]
    grad_first = ctx_scatter_sum(gl_total, gl_parts)
    grad_in_norm, grad_gain_one, grad_shift_one = norm_backward(
        grad_first + mm_t(gkv_low, w_kv), normed_one, inverse_one, gain_one
    )
    grad_inputs = grad_middle + grad_in_norm

    grad_w_proj = spread_rows(meta, d_proj)
    d_fc = ctx_gather_halves(
        *[after(part, gkv_low) for part in d_fc], last=lambda part: after(part, grad_w_proj)
    )
    (grad_w_fc,) = spread_columns(meta, d_fc, fsdp_count // 2, True)
    d_q = mm_rows(a_even, gq_even) + mm_rows(a_odd, gq_odd)
    d_out = mm_rows(o_even, ga_even) + mm_rows(o_odd, ga_odd)
    d_pair = with_layout_constraint(
        jnp.concatenate([d_q, d_out], axis=1).astype(BF16), Layout(major_to_minor=(0, 1))
    )
    d_pair = z_scatter_queued(d_pair)
    d_kv = (mm_rows(a_even, gkv_even) + mm_rows(a_odd, gkv_odd)).astype(BF16)
    d_kv = z_scatter_queued(d_kv).astype(F32)
    d_pair = [
        (values.reshape(chips, shard, 2 * q_width), [2 * at + parity for at in range(chips)])
        for parity, values in enumerate(ctx_gather(d_pair))
    ]
    grad_w_qkv, grad_w_out = spread_columns(meta, [d_pair] * 2, 1, False, d_kv)

    def column_sum(*parts):
        return sum(jnp.sum(part, axis=0, dtype=F32) for part in parts)

    g_bias_q = lax.dynamic_update_index_in_dim(
        jnp.zeros((ctx_count, q_width), F32), column_sum(gq_even, gq_odd), c_at, 0
    ).reshape(-1)
    g_bias_fc = lax.dynamic_update_index_in_dim(
        jnp.zeros((fsdp_count, ctx_count, unit), F32), g_bias_fc.reshape(fsdp_count, unit), c_at, 1
    ).reshape(-1)
    g_vectors = [
        grad_gain_one,
        grad_shift_one,
        g_bias_q,
        column_sum(gkv_low[:, HD:]),
        column_sum(grad_branch),
        grad_gain_two,
        grad_shift_two,
        g_bias_fc,
        column_sum(grad_mlp),
    ]
    stacked = jnp.concatenate(
        [member.reshape(fsdp_count, -1) for member in g_vectors], axis=1
    ).astype(BF16)
    own = z_sum_exchange(stacked).astype(BF16)
    own = ctx_exchange(jnp.broadcast_to(own[None], (ctx_count,) + own.shape))
    summed = jnp.sum(own, axis=0, dtype=F32)
    vector_grads, start = [], 0
    for size in sizes:
        vector_grads.append(summed[start : start + size].astype(BF16).astype(F32))
        start += size
    return (
        result.reshape(inputs.shape),
        grad_inputs.reshape(inputs.shape),
        grad_w_qkv,
        grad_w_out,
        grad_w_fc,
        grad_w_proj,
        *vector_grads,
    )


def solution(mesh):
    rows_placed = P(None, "ctx", None, "fsdp", None)
    matrix, vector = P("fsdp", None), P("fsdp")
    return jax.shard_map(
        body,
        mesh=mesh,
        in_specs=(rows_placed,) + (matrix,) * 4 + (vector,) * 9 + (rows_placed, P(), P()),
        out_specs=(rows_placed, rows_placed) + (matrix,) * 4 + (vector,) * 9,
        check_vma=False,
    )
```

```python
import functools
import math

import jax
import jax.numpy as jnp
from jax import lax
from jax.experimental.layout import Layout, with_layout_constraint
from jax.experimental import pallas as pl
from jax.experimental.pallas import tpu as pltpu
from jax.sharding import PartitionSpec as P

HEADS = 16
HD = 128
NORM_EPS = 1e-05
MASKED = -1e30
KEY_TILE = 512
LANE_ROWS = 256
SCALE = 1.0 / math.sqrt(HD)
F32 = jnp.float32
BF16 = jnp.bfloat16


def layer_norm(values, gain_vec, shift_vec):
    centred = values - jnp.mean(values, axis=-1, keepdims=True)
    inverse = lax.rsqrt(jnp.mean(centred * centred, axis=-1, keepdims=True) + NORM_EPS)
    normed = centred * inverse
    return (normed * gain_vec + shift_vec, normed, inverse)


def norm_backward(grad_norm, normed, inverse, gain_vec):
    scaled = grad_norm * gain_vec
    centred = scaled - jnp.mean(scaled, axis=-1, keepdims=True)
    centred = centred - normed * jnp.mean(scaled * normed, axis=-1, keepdims=True)
    return (centred * inverse, jnp.sum(grad_norm * normed, axis=0), jnp.sum(grad_norm, axis=0))


def gelu_tanh(values):
    return jax.nn.gelu(values, approximate=True)


def mm(left, right):
    return jnp.dot(left, right, preferred_element_type=F32)


def mm_t(left, right):
    return lax.dot_general(left, right, (((1,), (1,)), ((), ())), preferred_element_type=F32)


def mm_rows(left, right):
    return lax.dot_general(left, right, (((0,), (0,)), ((), ())), preferred_element_type=F32)


def after(values, *ready):
    return lax.optimization_barrier((values, *ready))[0] if ready else values


def ctx_swap(values, mask):
    count = lax.axis_size("ctx")
    return lax.ppermute(values, "ctx", [(at, at ^ mask) for at in range(count)])


def ctx_gather(values, ready=()):
    chips = lax.axis_size("ctx") // 2
    mine = jnp.concatenate([values] + [ctx_swap(values, 2 * at) for at in range(1, chips)], axis=0)
    mine = after(mine, *ready)
    return mine, ctx_swap(mine, 1)


def ctx_gather_all(values):
    return jnp.concatenate(ctx_gather(values), axis=0)


def ctx_scatter(even, odd, ready=(), finish=()):
    return ctx_scatter_chips(*ctx_scatter_cores(even, odd), ready, finish)


def ctx_scatter_cores(even, odd):
    rows = even.shape[0] // (lax.axis_size("ctx") // 2)
    both = even.astype(F32) + ctx_swap(odd.astype(BF16), 1).astype(F32)
    return both[:rows], both[rows:].astype(BF16)


def ctx_scatter_chips(total, low, ready=(), finish=()):
    return ctx_scatter_sum(total, ctx_scatter_sent(low, total.shape[0], ready), finish)


def ctx_scatter_sent(low, rows, ready=()):
    low = after(low, *ready)
    return [
        ctx_swap(low[(at - 1) * rows : at * rows], 2 * at)
        for at in range(1, lax.axis_size("ctx") // 2)
    ]


def ctx_scatter_sum(total, parts, finish=()):
    for part in parts:
        total = total + after(part, *finish).astype(F32)
    return total


def chip_masks(side):
    masks, mask = [], lax.axis_size("ctx") // 2
    while mask > 1:
        masks.append(mask)
        mask //= 2
    return masks[1:] + masks[:1] if side else masks


def ctx_gather_halves(
    first, second, wait=lambda values: values, last=lambda values: values, begun=None, finish=None
):
    held, offsets = [first[None], second[None]], [[0], [0]]
    steps = len(chip_masks(0))
    for step in range(steps):
        sent = []
        for side in range(2):
            mask = chip_masks(side)[step]
            got = begun[side] if begun and step == 0 else ctx_swap(held[side], mask)
            sent.append((got, [at ^ mask for at in offsets[side]]))
        if step < steps - 1:
            for side in range(2):
                held[side] = jnp.concatenate([held[side], wait(sent[side][0])], axis=0)
                offsets[side] = offsets[side] + sent[side][1]
    if finish:
        came = finish([got for got, _ in sent])
        sent = [(got, order) for got, (_, order) in zip(came, sent)]
    gathered = []
    for side in range(2):
        parts = [(held[side], offsets[side]), (last(sent[side][0]), sent[side][1])]
        gathered.append(
            parts + [(ctx_swap(block, 1), [at ^ 1 for at in order]) for block, order in parts]
        )
    return gathered


def ctx_scatter_halves(even, odd, ready=(), finish=()):
    chips = lax.axis_size("ctx") // 2
    rows = even.shape[0] // chips
    both = even.astype(F32) + ctx_swap(odd.astype(BF16), 1).astype(F32)
    both = both.reshape(chips, 2, rows // 2, -1)
    totals = []
    for side in range(2):
        blocks = {2 * at: both[at, side] for at in range(chips)}
        for step, mask in enumerate(reversed(chip_masks(side))):
            kept = [offset for offset in sorted(blocks) if not offset & mask]
            sent = jnp.stack([blocks[offset ^ mask].astype(BF16) for offset in kept])
            got = ctx_swap(after(sent, *ready) if step == 0 else sent, mask)
            if len(kept) == 1:
                got = after(got, *finish)
            blocks = {offset: blocks[offset] + got[at].astype(F32) for at, offset in enumerate(kept)}
        totals.append(blocks[0])
    return jnp.concatenate(totals, axis=0)


def in_order(parts, parity):
    blocks = {
        offset: values[at]
        for values, order in parts
        for at, offset in enumerate(order)
        if offset % 2 == parity
    }
    return jnp.concatenate([blocks[offset] for offset in sorted(blocks)], axis=0)


def ctx_exchange(values):
    return lax.all_to_all(values, "ctx", 0, 0, tiled=True)


def z_masks(count):
    masks = []
    while count > 1:
        masks.append(count - 1)
        count //= 2
    return masks


def z_offsets(count):
    offsets = [0]
    for mask in z_masks(count):
        offsets = offsets + [at ^ mask for at in offsets]
    return offsets


def z_swap(values, mask):
    count = lax.axis_size("fsdp")
    return lax.ppermute(values, "fsdp", [(at, at ^ mask) for at in range(count)])


def z_gather_steps(values):
    held = values[None]
    own = z_swap(held, 1)
    for mask in z_masks(lax.axis_size("fsdp"))[:-1]:
        held = jnp.concatenate([held, z_swap(held, mask)], axis=0)
    return held, own


def z_gather_finish(held, own):
    if held.shape[0] == 1:
        return [held, own]
    return [held, own, z_swap(held[1:], 1)]


def z_gather_parts(values):
    return z_gather_finish(*z_gather_steps(values))


def z_gather_held(values):
    held = values[None]
    for mask in z_masks(lax.axis_size("fsdp"))[:-1]:
        held = jnp.concatenate([held, z_swap(held, mask)], axis=0)
    return held


def z_sum_exchange(values):
    return jnp.sum(lax.all_to_all(values, "fsdp", 0, 0, tiled=True), axis=0, dtype=F32)


def z_gather_queued(values):
    return lax.all_gather(values, "fsdp", axis=0, tiled=True)


def z_scatter_queued(values):
    return lax.psum_scatter(values, "fsdp", scatter_dimension=0, tiled=True)


def place_kernel(plan, n_in, meta, *refs):
    ins, outs = refs[:n_in], refs[n_in:]
    for source, rows_in, target, rows_out in plan(meta):
        outs[target][rows_out] = ins[source][rows_in]


def place_blocks(meta, sources, outs, plan, name):
    return pl.pallas_call(
        functools.partial(place_kernel, plan, len(sources)),
        grid_spec=pltpu.PrefetchScalarGridSpec(
            num_scalar_prefetch=1,
            grid=(1,),
            in_specs=[pl.BlockSpec(memory_space=pltpu.VMEM)] * len(sources),
            out_specs=[pl.BlockSpec(memory_space=pltpu.VMEM)] * len(outs),
        ),
        out_shape=[jax.ShapeDtypeStruct(out, sources[0].dtype) for out in outs],
        compiler_params=pltpu.CompilerParams(vmem_limit_bytes=56 * 2**20),
        name=name,
    )(meta, *sources)


class Shape:
    def __init__(self, ctx_count, fsdp_count, slots, rows):
        self.ctx_count, self.fsdp_count, self.slots, self.rows = ctx_count, fsdp_count, slots, rows
        self.heads = HEADS // ctx_count
        self.block = rows * fsdp_count
        self.blocks = 2 * ctx_count
        self.keys = self.block * self.blocks
        self.tokens = slots * 2 * rows
        self.q_blocks = LANE_ROWS // (self.heads * rows)
        self.head_rows = self.q_blocks * rows
        self.q_tiles = self.blocks // self.q_blocks
        self.q_rows = self.q_tiles * LANE_ROWS
        self.chips = ctx_count // 2
        self.offsets = z_offsets(fsdp_count)


    def part_starts(self, count):
        half = self.fsdp_count // 2
        return [0, half, half + 1][:count]

    def part_of(self, at, count):
        starts = self.part_starts(count)
        part = max(index for index, start in enumerate(starts) if at >= start)
        return part, at - starts[part]


def for_blocks(shape, meta, act):
    me = meta[0]

    def step(chip, carry):
        for parity in range(2):
            first = meta[6 + (me ^ (2 * chip + parity))]
            for slot in range(shape.slots):
                for half in range(2):
                    block = first if half == 0 else shape.blocks - 1 - first
                    act(parity, chip, slot, half, block)
        return carry

    lax.fori_loop(0, shape.chips, step, 0)


def at_rows(start, size, unit):
    return pl.ds(pl.multiple_of(start, unit), size)


def q_source(shape, chip, slot, half):
    return at_rows(chip * shape.tokens + (slot * 2 + half) * shape.rows, shape.rows, shape.rows)


def q_target(shape, block, head):
    start = (block // shape.q_blocks) * LANE_ROWS + (block % shape.q_blocks) * shape.rows
    return at_rows(start + head * shape.head_rows, shape.rows, shape.rows)


def kv_source(shape, chip, order, slot, half):
    start = (chip * shape.fsdp_count + order) * shape.tokens + (slot * 2 + half) * shape.rows
    return at_rows(start, shape.rows, shape.rows)


def kv_target(shape, meta, block, order):
    start = block * shape.block + (meta[1] ^ shape.offsets[order]) * shape.rows
    return at_rows(start, shape.rows, shape.rows)


def query_bounds(shape, meta, slot, tile):
    lane = lax.broadcasted_iota(jnp.int32, (1, LANE_ROWS), 1)
    row = lane % shape.head_rows
    pos = (tile * shape.q_blocks + row // shape.rows) * shape.block + meta[1] * shape.rows + row % shape.rows
    first_end = meta[2 + 2 * slot]
    second_end = first_end + meta[3 + 2 * slot]

    def start_of(at):
        return jnp.where(at < first_end, 0, jnp.where(at < second_end, first_end, second_end))

    first_pos = tile * shape.q_blocks * shape.block + meta[1] * shape.rows
    last_pos = first_pos + (shape.q_blocks - 1) * shape.block + shape.rows - 1
    return pos, start_of(pos), start_of(first_pos) // KEY_TILE, last_pos // KEY_TILE + 1


def visible(pos, start, tile):
    key_pos = tile * KEY_TILE + lax.broadcasted_iota(jnp.int32, (KEY_TILE, LANE_ROWS), 0)
    return (key_pos <= pos) & (key_pos >= start)


def device_rows(shape, meta, parity, chip, slot, half):
    device = meta[0] ^ (2 * chip + parity)
    return at_rows(device * shape.tokens + (slot * 2 + half) * shape.rows, shape.rows, shape.rows)


def attend_kernel(shape, meta, q_even, q_odd, kv_even, kv_odd, o_out, q_all, kv_all, o_t, lse, o_rows):
    queries, keys = (q_even, q_odd), (kv_even, kv_odd)

    def place(parity, chip, slot, half, block):
        for head in range(shape.heads):
            q_all[slot, q_target(shape, block, head), :] = queries[parity][
                q_source(shape, chip, slot, half), head * HD : (head + 1) * HD
            ]
        for order in range(shape.fsdp_count):
            kv_all[slot, kv_target(shape, meta, block, order), :] = keys[parity][
                kv_source(shape, chip, order, slot, half), :
            ]

    for_blocks(shape, meta, place)

    def tile_step(item, carry):
        slot, tile = item // shape.q_tiles, item % shape.q_tiles
        pos, start, low, high = query_bounds(shape, meta, slot, tile)
        q_tile = q_all[slot, at_rows(tile * LANE_ROWS, LANE_ROWS, LANE_ROWS), :]

        def key_step(at, state):
            peak, total, acc = state
            part = at_rows(at * KEY_TILE, KEY_TILE, KEY_TILE)
            scores = mm_t(kv_all[slot, part, :HD], q_tile) * SCALE
            scores = jnp.where(visible(pos, start, at), scores, MASKED)
            new_peak = jnp.maximum(peak, jnp.max(scores, axis=0, keepdims=True))
            fade = jnp.exp(peak - new_peak)
            weights = jnp.exp(scores - new_peak)
            total = total * fade + jnp.sum(weights, axis=0, keepdims=True)
            acc = acc * fade + mm_rows(kv_all[slot, part, HD:], weights.astype(BF16))
            return new_peak, total, acc

        begin = (
            jnp.full((1, LANE_ROWS), MASKED, F32),
            jnp.zeros((1, LANE_ROWS), F32),
            jnp.zeros((HD, LANE_ROWS), F32),
        )
        peak, total, acc = lax.fori_loop(low, high, key_step, begin)
        acc = acc / total
        o_t[item] = acc
        lse[item] = peak + jnp.log(total)
        o_rows[slot, at_rows(tile * LANE_ROWS, LANE_ROWS, LANE_ROWS), :] = acc.T.astype(BF16)
        return carry

    lax.fori_loop(0, shape.slots * shape.q_tiles, tile_step, 0)

    def put_back(parity, chip, slot, half, block):
        for head in range(shape.heads):
            o_out[device_rows(shape, meta, parity, chip, slot, half), head * HD : (head + 1) * HD] = o_rows[
                slot, q_target(shape, block, head), :
            ]

    for_blocks(shape, meta, put_back)


def attend_grad_kernel(
    shape, meta, q_all, kv_all, o_t, lse, grads, gq_even, gq_odd, gkv_even, gkv_odd, ga_even, ga_odd, go_all, gq_all, gkv_all
):
    g_queries, g_keys, g_branch = (gq_even, gq_odd), (gkv_even, gkv_odd), (ga_even, ga_odd)

    def place(parity, chip, slot, half, block):
        source = device_rows(shape, meta, parity, chip, slot, half)
        for head in range(shape.heads):
            go_all[slot, q_target(shape, block, head), :] = grads[source, head * HD : (head + 1) * HD]
        g_branch[parity][q_source(shape, chip, slot, half), :] = grads[source, shape.heads * HD :]

    for_blocks(shape, meta, place)
    gkv_all[...] = jnp.zeros_like(gkv_all)

    def tile_step(item, carry):
        slot, tile = item // shape.q_tiles, item % shape.q_tiles
        pos, start, low, high = query_bounds(shape, meta, slot, tile)
        rows = at_rows(tile * LANE_ROWS, LANE_ROWS, LANE_ROWS)
        q_tile = q_all[slot, rows, :]
        go_tile = go_all[slot, rows, :]
        delta = jnp.sum(go_tile.astype(F32).T * o_t[item], axis=0, keepdims=True)
        lse_row = lse[item]

        def key_step(at, acc):
            part = at_rows(at * KEY_TILE, KEY_TILE, KEY_TILE)
            key_part, value_part = kv_all[slot, part, :HD], kv_all[slot, part, HD:]
            scores = mm_t(key_part, q_tile) * SCALE
            probs = jnp.where(visible(pos, start, at), jnp.exp(scores - lse_row), 0.0)
            g_scores = (probs * (mm_t(value_part, go_tile) - delta)).astype(BF16)
            gkv_all[slot, part, :HD] += mm(g_scores, q_tile)
            gkv_all[slot, part, HD:] += mm(probs.astype(BF16), go_tile)
            return acc + mm_rows(key_part, g_scores)

        acc = lax.fori_loop(low, high, key_step, jnp.zeros((HD, LANE_ROWS), F32))
        gq_all[slot, rows, :] = (acc * SCALE).T.astype(BF16)
        return carry

    lax.fori_loop(0, shape.slots * shape.q_tiles, tile_step, 0)

    def put_back(parity, chip, slot, half, block):
        for head in range(shape.heads):
            g_queries[parity][q_source(shape, chip, slot, half), head * HD : (head + 1) * HD] = gq_all[
                slot, q_target(shape, block, head), :
            ]
        for order in range(shape.fsdp_count):
            target = kv_target(shape, meta, block, order)
            source = kv_source(shape, chip, meta[1] ^ shape.offsets[order], slot, half)
            g_keys[parity][source, :HD] = (gkv_all[slot, target, :HD] * SCALE).astype(BF16)
            g_keys[parity][source, HD:] = gkv_all[slot, target, HD:].astype(BF16)

    for_blocks(shape, meta, put_back)


def attend(shape, meta, q_even, q_odd, kv_even, kv_odd):
    items = shape.slots * shape.q_tiles
    pairs = items * LANE_ROWS * shape.keys // 2
    return pl.pallas_call(
        functools.partial(attend_kernel, shape),
        grid_spec=pltpu.PrefetchScalarGridSpec(
            num_scalar_prefetch=1,
            grid=(1,),
            in_specs=[pl.BlockSpec(memory_space=pltpu.VMEM)] * 4,
            out_specs=[pl.BlockSpec(memory_space=pltpu.VMEM)] * 5,
            scratch_shapes=[pltpu.VMEM((shape.slots, shape.q_rows, HD), BF16)],
        ),
        out_shape=[
            jax.ShapeDtypeStruct((shape.ctx_count * shape.tokens, shape.heads * HD), BF16),
            jax.ShapeDtypeStruct((shape.slots, shape.q_rows, HD), BF16),
            jax.ShapeDtypeStruct((shape.slots, shape.keys, 2 * HD), BF16),
            jax.ShapeDtypeStruct((items, HD, LANE_ROWS), F32),
            jax.ShapeDtypeStruct((items, 1, LANE_ROWS), F32),
        ],
        compiler_params=pltpu.CompilerParams(vmem_limit_bytes=56 * 2**20),
        cost_estimate=pl.CostEstimate(flops=pairs * HD * 4, transcendentals=pairs, bytes_accessed=8 * 2**20),
        name="attend",
    )(meta, q_even, q_odd, kv_even, kv_odd)


def attend_grad(shape, meta, q_all, kv_all, o_t, lse, grads):
    items = shape.slots * shape.q_tiles
    q_like = jax.ShapeDtypeStruct((shape.chips * shape.tokens, shape.heads * HD), BF16)
    kv_like = jax.ShapeDtypeStruct((shape.chips * shape.fsdp_count * shape.tokens, 2 * HD), BF16)
    pairs = items * LANE_ROWS * shape.keys // 2
    return pl.pallas_call(
        functools.partial(attend_grad_kernel, shape),
        grid_spec=pltpu.PrefetchScalarGridSpec(
            num_scalar_prefetch=1,
            grid=(1,),
            in_specs=[pl.BlockSpec(memory_space=pltpu.VMEM)] * 5,
            out_specs=[pl.BlockSpec(memory_space=pltpu.VMEM)] * 6,
            scratch_shapes=[
                pltpu.VMEM((shape.slots, shape.q_rows, HD), BF16),
                pltpu.VMEM((shape.slots, shape.q_rows, HD), BF16),
                pltpu.VMEM((shape.slots, shape.keys, 2 * HD), F32),
            ],
        ),
        out_shape=[q_like, q_like, kv_like, kv_like, q_like, q_like],
        compiler_params=pltpu.CompilerParams(vmem_limit_bytes=56 * 2**20),
        cost_estimate=pl.CostEstimate(flops=pairs * HD * 10, transcendentals=pairs, bytes_accessed=10 * 2**20),
        name="attend_grad",
    )(meta, q_all, kv_all, o_t, lse, grads)


def block_of(shape, parts, at):
    part, block = shape.part_of(at, len(parts))
    return parts[part][block]


def gelu_parts(values):
    root = math.sqrt(2.0 / math.pi)
    return jnp.tanh(root * (values + 0.044715 * (values * values * values)))


def hidden_kernel(shape, meta, rows_ref, bias_ref, *refs):
    parts, (hidden_ref, act_ref) = refs[:-2], refs[-2:]
    depth = parts[0].shape[1]
    total = bias_ref[...]
    for at, offset in enumerate(shape.offsets):
        part = pl.ds(pl.multiple_of((meta[1] ^ offset) * depth, depth), depth)
        total = total + mm(rows_ref[:, part], block_of(shape, parts, at))
    hidden_ref[...] = total
    act_ref[...] = (0.5 * total * (1.0 + gelu_parts(total))).astype(BF16)


def feed_hidden(shape, meta, rows, parts, bias):
    count, width = rows.shape
    _, depth, columns = parts[0].shape
    tile = 256
    weights = [
        pl.BlockSpec((part.shape[0], depth, tile), lambda i, m: (0, 0, i)) for part in parts
    ]
    out = pl.BlockSpec((count, tile), lambda i, m: (0, i))
    return pl.pallas_call(
        functools.partial(hidden_kernel, shape),
        grid_spec=pltpu.PrefetchScalarGridSpec(
            num_scalar_prefetch=1,
            grid=(columns // tile,),
            in_specs=[
                pl.BlockSpec((count, width), lambda i, m: (0, 0)),
                pl.BlockSpec((1, tile), lambda i, m: (0, i)),
                *weights,
            ],
            out_specs=[out, out],
        ),
        out_shape=[
            jax.ShapeDtypeStruct((count, columns), F32),
            jax.ShapeDtypeStruct((count, columns), BF16),
        ],
        compiler_params=pltpu.CompilerParams(vmem_limit_bytes=56 * 2**20),
        cost_estimate=pl.CostEstimate(
            flops=2 * count * width * columns,
            transcendentals=count * columns,
            bytes_accessed=2 * (count * width + width * columns) + 6 * count * columns,
        ),
        name="feed_hidden",
    )(meta, rows, bias, *parts)


def hidden_grad_kernel(grads_ref, hidden_ref, first, second, out_ref, sum_ref):
    values = hidden_ref[...]
    tanh = gelu_parts(values)
    root = math.sqrt(2.0 / math.pi)
    slope = 0.5 * (1.0 + tanh) + (0.5 * root) * values * (1.0 - tanh * tanh) * (
        1.0 + (3.0 * 0.044715) * (values * values)
    )
    width = first.shape[1]
    grads = mm_t(grads_ref[:, :width], first[...]) + mm_t(grads_ref[:, width:], second[...])
    low = (grads * slope).astype(BF16)
    out_ref[...] = low
    sum_ref[...] = jnp.sum(low.astype(F32), axis=0, keepdims=True)


def feed_hidden_grad(grads, hidden, weights):
    count, width = grads.shape
    columns = hidden.shape[1]
    tile = 256
    place = pl.BlockSpec((count, tile), lambda i: (0, i))
    return pl.pallas_call(
        hidden_grad_kernel,
        grid=(columns // tile,),
        in_specs=[pl.BlockSpec((count, width), lambda i: (0, 0)), place]
        + [pl.BlockSpec((tile, width // 2), lambda i: (i, 0))] * 2,
        out_specs=[place, pl.BlockSpec((1, tile), lambda i: (0, i))],
        out_shape=[
            jax.ShapeDtypeStruct((count, columns), BF16),
            jax.ShapeDtypeStruct((1, columns), F32),
        ],
        compiler_params=pltpu.CompilerParams(vmem_limit_bytes=56 * 2**20),
        cost_estimate=pl.CostEstimate(
            flops=2 * count * width * columns,
            transcendentals=count * columns,
            bytes_accessed=2 * (count * width + width * columns) + 6 * count * columns,
        ),
        name="feed_hidden_grad",
    )(grads, hidden, *weights)


def feed_late_kernel(steps, rows_ref, first, second, norm_ref, grads_ref, even_ref, odd_ref, *d_refs):
    at = pl.program_id(0)
    width = first.shape[1]
    for side, out_ref in enumerate((even_ref, odd_ref)):

        @pl.when(at // steps == side)
        def _(out_ref=out_ref):
            out_ref[:, :width] = mm(rows_ref[...], first[...]).astype(BF16)
            out_ref[:, width:] = mm(rows_ref[...], second[...]).astype(BF16)

    @pl.when(at >= 2 * steps)
    def _():
        columns = d_refs[0].shape[1]
        for part, out_ref in enumerate(d_refs):
            out_ref[...] = mm_rows(
                norm_ref[...], grads_ref[:, part * columns : (part + 1) * columns]
            ).astype(BF16)


def feed_late(rows, weights, norm, grads):
    depth, half_width = weights[0].shape
    count, tile = rows.shape[0] // 2, 256
    steps = count // tile
    width, columns = norm.shape[1], grads.shape[1]
    last = 2 * steps - 1
    d_block = pl.BlockSpec((tile, columns // 2), lambda i: (jnp.maximum(i - last - 1, 0), 0))
    return pl.pallas_call(
        functools.partial(feed_late_kernel, steps),
        grid=(2 * steps + width // tile,),
        in_specs=[
            pl.BlockSpec((tile, depth), lambda i: (jnp.minimum(i, last), 0)),
            pl.BlockSpec((depth, half_width), lambda i: (0, 0)),
            pl.BlockSpec((depth, half_width), lambda i: (0, 0)),
            pl.BlockSpec((2 * count, tile), lambda i: (0, jnp.maximum(i - last - 1, 0))),
            pl.BlockSpec((2 * count, columns), lambda i: (0, 0)),
        ],
        out_specs=[
            pl.BlockSpec((tile, 2 * half_width), lambda i: (jnp.minimum(i, steps - 1), 0)),
            pl.BlockSpec((tile, 2 * half_width), lambda i: (jnp.clip(i - steps, 0, steps - 1), 0)),
            d_block,
            d_block,
        ],
        out_shape=[jax.ShapeDtypeStruct((count, 2 * half_width), BF16)] * 2
        + [jax.ShapeDtypeStruct((width, columns // 2), BF16)] * 2,
        compiler_params=pltpu.CompilerParams(vmem_limit_bytes=56 * 2**20),
        cost_estimate=pl.CostEstimate(
            flops=8 * count * depth * half_width + 4 * count * width * columns,
            transcendentals=0,
            bytes_accessed=2 * (6 * count * half_width + 2 * depth * half_width + 4 * count * width),
        ),
        name="feed_late",
    )(rows, *weights, norm, grads)


def feed_grad_kernel(shape, meta, rows_ref, *refs):
    parts, out_ref = refs[:-1], refs[-1]
    for at, offset in enumerate(shape.offsets):
        block = block_of(shape, parts, at)
        size = block.shape[0]
        part = pl.ds(pl.multiple_of((meta[1] ^ offset) * size, size), size)
        out_ref[:, part] = mm_t(rows_ref[...], block).astype(BF16)


def feed_grad(shape, meta, rows, parts, side, count):
    width = shape.fsdp_count * parts[0].shape[1]
    tile = 256
    steps = count // tile
    return pl.pallas_call(
        functools.partial(feed_grad_kernel, shape),
        grid_spec=pltpu.PrefetchScalarGridSpec(
            num_scalar_prefetch=1,
            grid=(steps,),
            in_specs=[
                pl.BlockSpec((tile, rows.shape[1]), lambda i, m: (side * steps + i, 0)),
                *[pl.BlockSpec(part.shape, lambda i, m: (0, 0, 0)) for part in parts],
            ],
            out_specs=pl.BlockSpec((tile, width), lambda i, m: (i, 0)),
        ),
        out_shape=jax.ShapeDtypeStruct((count, width), BF16),
        compiler_params=pltpu.CompilerParams(vmem_limit_bytes=56 * 2**20),
        cost_estimate=pl.CostEstimate(
            flops=2 * count * rows.shape[1] * width,
            transcendentals=0,
            bytes_accessed=2 * (count + width) * rows.shape[1] + 2 * count * width,
        ),
        name="feed_grad",
    )(meta, rows, *parts)


def branch_kernel(layout, grad, meta, rows_ref, *refs):
    parts, out_ref = refs[:-1], refs[-1]
    out_ref[...] = jnp.zeros_like(out_ref)
    for part, (ctx_order, z_order) in zip(parts, layout):
        depth, columns = part.shape[2], part.shape[3]
        for at, ctx_offset in enumerate(ctx_order):
            column = pl.ds(pl.multiple_of((meta[0] ^ ctx_offset) * columns, columns), columns)
            for order, z_offset in enumerate(z_order):
                row = pl.ds(pl.multiple_of((meta[1] ^ z_offset) * depth, depth), depth)
                if grad:
                    out_ref[:, row] += mm_t(rows_ref[:, column], part[at, order])
                else:
                    out_ref[:, column] += mm(rows_ref[:, row], part[at, order])


def times_blocks(meta, rows, parts, layout, grad):
    return pl.pallas_call(
        functools.partial(branch_kernel, layout, grad),
        grid_spec=pltpu.PrefetchScalarGridSpec(
            num_scalar_prefetch=1,
            grid=(1,),
            in_specs=[pl.BlockSpec(memory_space=pltpu.VMEM)] * (1 + len(parts)),
            out_specs=pl.BlockSpec(memory_space=pltpu.VMEM),
        ),
        out_shape=jax.ShapeDtypeStruct(rows.shape, F32),
        compiler_params=pltpu.CompilerParams(vmem_limit_bytes=56 * 2**20),
        cost_estimate=pl.CostEstimate(
            flops=2 * rows.shape[0] * rows.shape[1] ** 2,
            transcendentals=0,
            bytes_accessed=2 * rows.shape[1] ** 2,
        ),
        name="branch_grad" if grad else "branch",
    )(meta, rows, *parts)


def spread_rows_kernel(pieces, steps, meta, *refs):
    out_ref = refs[-1]
    for piece, blocks in enumerate(pieces):

        @pl.when(pl.program_id(0) // steps == piece)
        def _(blocks=blocks):
            for source, block, offset in blocks:
                rows = refs[source].shape[1]
                start = pl.multiple_of((meta[0] ^ offset) * rows, rows)
                out_ref[pl.ds(start, rows), :] = refs[source][block].astype(F32)


def spread_rows(meta, gathered):
    tile = 256
    members, specs, pieces = [], [], []
    for piece, parts in enumerate(gathered):
        blocks = []
        for values, order in parts:
            count, rows, columns = values.shape
            steps = columns // tile
            blocks += [(len(members), at, offset) for at, offset in enumerate(order)]
            members.append(values)

            def place(i, m, piece=piece, steps=steps):
                return (0, 0, jnp.clip(i - piece * steps, 0, steps - 1))

            specs.append(pl.BlockSpec((count, rows, tile), place))
        pieces.append(blocks)
    total = len(pieces[0]) * rows
    return pl.pallas_call(
        functools.partial(spread_rows_kernel, pieces, steps),
        grid_spec=pltpu.PrefetchScalarGridSpec(
            num_scalar_prefetch=1,
            grid=(len(pieces) * steps,),
            in_specs=specs,
            out_specs=pl.BlockSpec((total, tile), lambda i, m: (0, i)),
        ),
        out_shape=jax.ShapeDtypeStruct((total, len(pieces) * columns), F32),
        compiler_params=pltpu.CompilerParams(vmem_limit_bytes=48 * 2**20),
        name="spread_rows",
    )(meta, *members)


def spread_kernel(moves, extras, outs, meta, *refs):
    outs = refs[len(refs) - outs :]
    for source, block, columns, offset, out, start, step, size in moves:
        target = pl.multiple_of(start + (meta[0] ^ offset) * step, size)
        outs[out][:, pl.ds(target, size)] = refs[source][block, :, columns].astype(F32)
    for source, out in extras:
        width = refs[source].shape[1]
        outs[out][:, outs[out].shape[1] - width :] = refs[source][...]


def spread_columns(meta, gathered, groups, joined, extra=None):
    pieces = len(gathered)
    rows, columns = gathered[0][0][0].shape[1:]
    width = columns // groups if joined else columns // pieces
    count = sum(len(order) for _, order in gathered[0])
    if width % 128:
        results = []
        for parts in gathered:
            out = jnp.zeros((count, rows, groups, width), F32)
            for values, order in parts:
                for at, offset in enumerate(order):
                    block = values[at].reshape(rows, groups, width).astype(F32)
                    out = lax.dynamic_update_index_in_dim(out, block, meta[0] ^ offset, 0)
            results.append(jnp.transpose(out, (1, 2, 0, 3)).reshape(rows, -1))
        return [jnp.concatenate(results, axis=1)]
    members, moves = [], []
    for piece, parts in enumerate(gathered):
        if not joined:
            members = []
        for values, order in parts:
            for at, offset in enumerate(order):
                for group in range(groups):
                    start = ((piece if joined else 0) * groups + group) * count * width
                    source = (group if joined else piece) * width
                    moves.append(
                        (
                            len(members),
                            at,
                            slice(source, source + width),
                            offset,
                            0 if joined else piece,
                            start,
                            width,
                            width,
                        )
                    )
            members.append(values)
    sizes = [groups * count * width * pieces] if joined else [count * width] * pieces
    tile = min(rows, 64)
    in_specs = [
        pl.BlockSpec((member.shape[0], tile, columns), lambda i, m: (0, i, 0)) for member in members
    ]
    extras = []
    if extra is not None:
        extras = [(len(members), 0)]
        members.append(extra)
        in_specs.append(pl.BlockSpec((tile, extra.shape[1]), lambda i, m: (i, 0)))
        sizes[0] += extra.shape[1]
    return pl.pallas_call(
        functools.partial(spread_kernel, moves, extras, len(sizes)),
        grid_spec=pltpu.PrefetchScalarGridSpec(
            num_scalar_prefetch=1,
            grid=(rows // tile,),
            in_specs=in_specs,
            out_specs=[pl.BlockSpec((tile, size), lambda i, m: (i, 0)) for size in sizes],
        ),
        out_shape=[jax.ShapeDtypeStruct((rows, size), F32) for size in sizes],
        compiler_params=pltpu.CompilerParams(vmem_limit_bytes=48 * 2**20),
        name="spread_columns",
    )(meta, *members)


def pick_block(pair_table, ctx_at, half_bit):
    ctx_total = pair_table.shape[0]
    chosen = jnp.sum(jnp.where(jnp.arange(ctx_total, dtype=jnp.int32) == ctx_at, pair_table, 0))
    return jnp.where(half_bit == 0, chosen, 2 * ctx_total - 1 - chosen)


def body(
    inputs,
    w_qkv,
    w_out,
    w_fc,
    w_proj,
    ln1_gain,
    ln1_bias,
    bias_q,
    bias_v,
    bias_out,
    ln2_gain,
    ln2_bias,
    bias_fc,
    bias_proj,
    cotangent,
    lengths,
    pair_table,
):
    slots, _, _, rows, width = inputs.shape
    ctx_count, fsdp_count = lax.axis_size("ctx"), lax.axis_size("fsdp")
    c_at, z_at = lax.axis_index("ctx"), lax.axis_index("fsdp")
    shape = Shape(ctx_count, fsdp_count, slots, rows)
    tokens, chips = shape.tokens, shape.chips
    q_width = width // ctx_count
    shard = width // fsdp_count
    hidden_width = w_fc.shape[1]
    unit = hidden_width // (fsdp_count * ctx_count)
    meta = jnp.concatenate(
        [jnp.stack([c_at, z_at]).astype(jnp.int32), lengths.reshape(-1), pair_table]
    ).astype(jnp.int32)

    offsets = jnp.arange(2 * rows, dtype=jnp.int32)
    pos = (
        pick_block(pair_table, c_at, offsets // rows) * shape.block + z_at * rows + offsets % rows
    )
    live = (pos[None, :] < lengths[:, 0:1] + lengths[:, 1:2]).reshape(tokens, 1).astype(F32)

    x_low = inputs.reshape(tokens, width)
    grad_out = cotangent.reshape(tokens, width).astype(F32) * live
    grad_mlp = grad_out.astype(BF16)
    pack_width = q_width + 2 * HD
    w_first = jnp.concatenate(
        [lax.dynamic_slice_in_dim(w_qkv, c_at * q_width, q_width, axis=1), w_qkv[:, width:]], axis=1
    ).astype(BF16)
    vectors = [ln1_gain, ln1_bias, bias_q, bias_v, bias_out, ln2_gain, ln2_bias, bias_fc, bias_proj]
    sizes = [member.shape[0] for member in vectors]
    vector_rows = 16 * math.ceil(sum(sizes) / (16 * HD))
    packed = jnp.concatenate(
        [member.astype(BF16) for member in vectors]
        + [jnp.zeros((vector_rows * HD - sum(sizes),), BF16)]
    ).reshape(vector_rows, HD)
    x_even, x_odd = ctx_gather(after(x_low, w_first))
    half = fsdp_count // 2
    first_held, first_own = z_gather_steps(w_first)
    first_blocks = z_gather_finish(first_held, first_own)
    vector_held = z_gather_held(after(packed, first_held))
    vector_blocks = [vector_held, z_swap(vector_held, 1)]

    def first_plan(ref):
        moves = []
        for at, offset in enumerate(shape.offsets):
            owner, (part, block) = ref[1] ^ offset, shape.part_of(at, len(first_blocks))
            weight_rows = pl.ds(pl.multiple_of(owner * shard, shard), shard)
            q_part, kv_part = pl.ds(0, q_width), pl.ds(q_width, 2 * HD)
            moves += [
                (part, (block, slice(None), q_part), 0, (weight_rows, slice(None))),
                (part, (block, slice(None), kv_part), 1, (weight_rows, slice(None))),
                (len(first_blocks) + at // half, (at % half,), 2, (owner,)),
            ]
        return moves

    w_q, w_kv, packed = place_blocks(
        meta,
        [*first_blocks, *vector_blocks],
        [(width, q_width), (width, 2 * HD), (fsdp_count, vector_rows, HD)],
        first_plan,
        "place_first",
    )
    packed = packed.reshape(fsdp_count, -1)
    full, start = [], 0
    for size in sizes:
        full.append(packed[:, start : start + size].reshape(-1).astype(F32))
        start += size
    gain_one, shift_one, q_bias, v_bias, out_bias, gain_two, shift_two, fc_bias, proj_bias = full
    q_bias = lax.dynamic_slice_in_dim(q_bias, c_at * q_width, q_width)
    fc_bias = lax.dynamic_index_in_dim(
        fc_bias.reshape(fsdp_count, ctx_count, unit), c_at, 1, keepdims=False
    )

    def relative_plan(ref):
        return [
            (
                0,
                (ref[0] ^ (2 * chip + parity),),
                0,
                (pl.ds((parity * chips + chip) * tokens, tokens),),
            )
            for parity in range(2)
            for chip in range(chips)
        ]

    x_own = x_low.astype(F32)
    first_norm, normed_one, inverse_one = layer_norm(x_own, gain_one, shift_one)
    kv_own = mm(first_norm.astype(BF16), w_kv)
    kv_own = jnp.concatenate([kv_own[:, :HD], kv_own[:, HD:] + v_bias], axis=1).astype(BF16)
    kv_z = jnp.concatenate(z_gather_parts(kv_own), axis=0).reshape(fsdp_count * tokens, 2 * HD)
    kv_even, kv_odd = ctx_gather(kv_z)

    out_parts = z_gather_parts(
        after(lax.dynamic_slice_in_dim(w_out, c_at * q_width, q_width, axis=1).astype(BF16), kv_z)
    )

    fc_own = jnp.concatenate(
        [
            lax.dynamic_slice_in_dim(
                w_fc, group * (hidden_width // fsdp_count) + c_at * unit, unit, axis=1
            )
            for group in range(fsdp_count)
        ],
        axis=1,
    ).astype(BF16)
    proj_own = lax.dynamic_slice_in_dim(w_proj, c_at * unit, unit, axis=0).astype(BF16)
    out_halves = out_parts[0], jnp.concatenate(out_parts[1:], axis=0)
    fc_steps = z_gather_steps(after(fc_own, out_parts[0]))

    a_even = layer_norm(x_even.astype(F32), gain_one, shift_one)[0].astype(BF16)
    a_odd = layer_norm(x_odd.astype(F32), gain_one, shift_one)[0].astype(BF16)
    q_even = (mm(a_even, w_q) + q_bias).astype(BF16)
    q_odd = (mm(a_odd, w_q) + q_bias).astype(BF16)
    o_heads, q_all, kv_all, o_t, lse = attend(shape, meta, q_even, q_odd, kv_even, kv_odd)
    out_gathered = ctx_gather_halves(
        *[after(side, kv_even) for side in out_halves],
        wait=lambda part: after(part, kv_odd),
        last=lambda part: after(part, o_heads),
    )
    out_blocks, out_layout = [], []
    for side, parts in enumerate(out_gathered):
        z_order = shape.offsets[side * half : (side + 1) * half]
        for values, order in parts:
            out_blocks.append(values)
            out_layout.append((order, z_order))
    o_own = ctx_exchange(o_heads.reshape(ctx_count, tokens, q_width))
    o_own = jnp.transpose(o_own, (1, 0, 2)).reshape(tokens, width)
    fc_parts = z_gather_finish(*fc_steps)
    proj_own = after(proj_own, fc_parts[-1])
    w_p = [
        z_gather_queued(proj_own[:, at * width // 2 : (at + 1) * width // 2]) for at in range(2)
    ]
    o_own = after(o_own, *fc_steps)
    middle = x_own + (times_blocks(meta, o_own, out_blocks, out_layout, False) + out_bias)
    second_norm, normed_two, inverse_two = layer_norm(middle, gain_two, shift_two)

    o_parts = [ctx_swap(o_own, 2 * at) for at in range(1, chips)]
    cn_own, o_parts = lax.optimization_barrier((second_norm.astype(BF16), o_parts))
    cn_even, cn_odd = ctx_gather(cn_own)
    o_even = jnp.concatenate([o_own, *o_parts], axis=0)
    o_odd = ctx_swap(o_even, 1)
    gm_all = lax.all_gather(grad_mlp, "ctx", axis=0, tiled=False)
    (gm_all,) = place_blocks(
        meta, [gm_all], [(ctx_count * tokens, width)], relative_plan, "place_rows"
    )
    cn_all = jnp.concatenate([cn_even, cn_odd], axis=0)
    half_rows = chips * tokens
    hidden, act = feed_hidden(shape, meta, cn_all, fc_parts, fc_bias.reshape(1, -1))
    d_proj = mm_rows(act, gm_all).astype(BF16)
    g_hidden, g_bias_fc = feed_hidden_grad(gm_all, hidden, w_p)
    g_odd = feed_grad(shape, meta, g_hidden, fc_parts, 1, half_rows)
    g_even = feed_grad(shape, meta, after(g_hidden, g_odd), fc_parts, 0, half_rows)
    g_total, g_low = ctx_scatter_cores(g_even, g_odd)
    cn_late, act_late, g_low = lax.optimization_barrier((cn_all, act, g_low))
    g_parts = ctx_scatter_sent(g_low, tokens)
    late = feed_late(act_late, w_p, cn_late, g_hidden)
    g_parts, late = lax.optimization_barrier((g_parts, late))
    grad_second = ctx_scatter_sum(g_total, g_parts)
    d_proj = [
        z_scatter_queued(after(part, *w_p)) for part in (d_proj[:, : width // 2], d_proj[:, width // 2 :])
    ]
    d_fc = [z_scatter_queued(part) for part in late[2:]]
    r_total, r_low = ctx_scatter_cores(*late[:2])

    grad_mid_norm, grad_gain_two, grad_shift_two = norm_backward(
        grad_second, normed_two, inverse_two, gain_two
    )
    grad_middle = grad_out + grad_mid_norm
    grad_branch = grad_middle.astype(BF16)
    go_own = times_blocks(meta, grad_branch, out_blocks, out_layout, True).astype(BF16)
    grads = jnp.concatenate(
        [
            go_own.reshape(tokens, ctx_count, q_width),
            grad_branch.reshape(tokens, ctx_count, q_width),
        ],
        axis=2,
    )
    grads_sent = jnp.transpose(grads, (1, 0, 2))
    grads = ctx_exchange(grads_sent).reshape(ctx_count * tokens, 2 * q_width)
    grads, r_total = lax.optimization_barrier((grads, r_total))

    gq_even, gq_odd, gkv_even, gkv_odd, ga_even, ga_odd = attend_grad(
        shape, meta, q_all, kv_all, o_t, lse, grads
    )
    first_sent = [ctx_swap(part[None], chip_masks(side)[0]) for side, part in enumerate(d_proj)]
    r_parts = ctx_scatter_sent(r_low, tokens, [grads_sent])
    gkv_odd, first_sent, r_parts = lax.optimization_barrier((gkv_odd, first_sent, r_parts))
    result = (middle + (ctx_scatter_sum(r_total, r_parts) + proj_bias)).astype(BF16)
    gkv_plane = ctx_scatter(gkv_even, gkv_odd)
    d_q = mm_rows(a_even, gq_even) + mm_rows(a_odd, gq_odd)
    d_out = mm_rows(o_even, ga_even) + mm_rows(o_odd, ga_odd)
    d_pair = with_layout_constraint(
        jnp.concatenate([d_q, d_out], axis=1).astype(BF16), Layout(major_to_minor=(0, 1))
    )
    d_pair = z_scatter_queued(d_pair)
    pair = []

    def finish(parts):
        parts, d_done = lax.optimization_barrier((parts, d_pair))
        pair.append(d_done)
        return parts

    d_proj = ctx_gather_halves(
        *d_proj, wait=lambda part: after(part, gkv_plane), begun=first_sent, finish=finish
    )
    (d_pair,) = pair
    gkv_low = z_sum_exchange(gkv_plane.astype(BF16).reshape(fsdp_count, tokens, 2 * HD)).astype(BF16)
    gkv_all = ctx_exchange(jnp.broadcast_to(gkv_low[None], (ctx_count,) + gkv_low.shape))
    gl_total, gl_low = ctx_scatter_cores(mm_t(gq_even, w_q), mm_t(gq_odd, w_q))
    gl_parts = ctx_scatter_sent(gl_low, tokens, [gkv_plane])
    gkv_all, gl_parts = lax.optimization_barrier((gkv_all, gl_parts))
    (gkv_all,) = place_blocks(
        meta,
        [gkv_all],
        [(ctx_count * tokens, 2 * HD)],
        relative_plan,
        "place_keys",
    )
    gkv_even, gkv_odd = gkv_all[: chips * tokens], gkv_all[chips * tokens :]
    grad_first = ctx_scatter_sum(gl_total, gl_parts)
    grad_in_norm, grad_gain_one, grad_shift_one = norm_backward(
        grad_first + mm_t(gkv_low, w_kv), normed_one, inverse_one, gain_one
    )
    grad_inputs = grad_middle + grad_in_norm

    grad_w_proj = spread_rows(meta, d_proj)
    d_fc = ctx_gather_halves(
        *[after(part, gkv_low) for part in d_fc], last=lambda part: after(part, grad_w_proj)
    )
    (grad_w_fc,) = spread_columns(meta, d_fc, fsdp_count // 2, True)
    d_kv = (mm_rows(a_even, gkv_even) + mm_rows(a_odd, gkv_odd)).astype(BF16)
    d_kv = z_scatter_queued(d_kv).astype(F32)
    d_pair = [
        (values.reshape(chips, shard, 2 * q_width), [2 * at + parity for at in range(chips)])
        for parity, values in enumerate(ctx_gather(d_pair))
    ]
    grad_w_qkv, grad_w_out = spread_columns(meta, [d_pair] * 2, 1, False, d_kv)

    def column_sum(*parts):
        return sum(jnp.sum(part, axis=0, dtype=F32) for part in parts)

    g_bias_q = lax.dynamic_update_index_in_dim(
        jnp.zeros((ctx_count, q_width), F32), column_sum(gq_even, gq_odd), c_at, 0
    ).reshape(-1)
    g_bias_fc = lax.dynamic_update_index_in_dim(
        jnp.zeros((fsdp_count, ctx_count, unit), F32), g_bias_fc.reshape(fsdp_count, unit), c_at, 1
    ).reshape(-1)
    g_vectors = [
        grad_gain_one,
        grad_shift_one,
        g_bias_q,
        column_sum(gkv_low[:, HD:]),
        column_sum(grad_branch),
        grad_gain_two,
        grad_shift_two,
        g_bias_fc,
        column_sum(grad_mlp),
    ]
    stacked = jnp.concatenate(
        [member.reshape(fsdp_count, -1) for member in g_vectors], axis=1
    ).astype(BF16)
    stacked, grad_w_proj = lax.optimization_barrier((stacked, grad_w_proj))
    own = z_sum_exchange(stacked).astype(BF16)
    own = ctx_exchange(jnp.broadcast_to(own[None], (ctx_count,) + own.shape))
    summed = jnp.sum(own, axis=0, dtype=F32)
    vector_grads, start = [], 0
    for size in sizes:
        vector_grads.append(summed[start : start + size].astype(BF16).astype(F32))
        start += size
    return (
        result.reshape(inputs.shape),
        grad_inputs.reshape(inputs.shape),
        grad_w_qkv,
        grad_w_out,
        grad_w_fc,
        grad_w_proj,
        *vector_grads,
    )


def solution(mesh):
    rows_placed = P(None, "ctx", None, "fsdp", None)
    matrix, vector = P("fsdp", None), P("fsdp")
    return jax.shard_map(
        body,
        mesh=mesh,
        in_specs=(rows_placed,) + (matrix,) * 4 + (vector,) * 9 + (rows_placed, P(), P()),
        out_specs=(rows_placed, rows_placed) + (matrix,) * 4 + (vector,) * 9,
        check_vma=False,
    )
```

```python
import functools
import math

import jax
import jax.numpy as jnp
from jax import lax
from jax.experimental.layout import Layout, with_layout_constraint
from jax.experimental import pallas as pl
from jax.experimental.pallas import tpu as pltpu
from jax.sharding import PartitionSpec as P

HEADS = 16
HD = 128
NORM_EPS = 1e-05
MASKED = -1e30
KEY_TILE = 512
LANE_ROWS = 256
SCALE = 1.0 / math.sqrt(HD)
F32 = jnp.float32
BF16 = jnp.bfloat16


def layer_norm(values, gain_vec, shift_vec):
    centred = values - jnp.mean(values, axis=-1, keepdims=True)
    inverse = lax.rsqrt(jnp.mean(centred * centred, axis=-1, keepdims=True) + NORM_EPS)
    normed = centred * inverse
    return (normed * gain_vec + shift_vec, normed, inverse)


def norm_backward(grad_norm, normed, inverse, gain_vec):
    scaled = grad_norm * gain_vec
    centred = scaled - jnp.mean(scaled, axis=-1, keepdims=True)
    centred = centred - normed * jnp.mean(scaled * normed, axis=-1, keepdims=True)
    return (centred * inverse, jnp.sum(grad_norm * normed, axis=0), jnp.sum(grad_norm, axis=0))


def gelu_tanh(values):
    return jax.nn.gelu(values, approximate=True)


def mm(left, right):
    return jnp.dot(left, right, preferred_element_type=F32)


def mm_t(left, right):
    return lax.dot_general(left, right, (((1,), (1,)), ((), ())), preferred_element_type=F32)


def mm_rows(left, right):
    return lax.dot_general(left, right, (((0,), (0,)), ((), ())), preferred_element_type=F32)


def after(values, *ready):
    return lax.optimization_barrier((values, *ready))[0] if ready else values


def ctx_swap(values, mask):
    count = lax.axis_size("ctx")
    return lax.ppermute(values, "ctx", [(at, at ^ mask) for at in range(count)])


def ctx_gather(values, ready=()):
    chips = lax.axis_size("ctx") // 2
    mine = jnp.concatenate([values] + [ctx_swap(values, 2 * at) for at in range(1, chips)], axis=0)
    mine = after(mine, *ready)
    return mine, ctx_swap(mine, 1)


def ctx_gather_all(values):
    return jnp.concatenate(ctx_gather(values), axis=0)


def ctx_scatter(even, odd, ready=(), finish=()):
    return ctx_scatter_chips(*ctx_scatter_cores(even, odd), ready, finish)


def ctx_scatter_cores(even, odd):
    rows = even.shape[0] // (lax.axis_size("ctx") // 2)
    both = even.astype(F32) + ctx_swap(odd.astype(BF16), 1).astype(F32)
    return both[:rows], both[rows:].astype(BF16)


def ctx_scatter_chips(total, low, ready=(), finish=()):
    return ctx_scatter_sum(total, ctx_scatter_sent(low, total.shape[0], ready), finish)


def ctx_scatter_sent(low, rows, ready=()):
    low = after(low, *ready)
    return [
        ctx_swap(low[(at - 1) * rows : at * rows], 2 * at)
        for at in range(1, lax.axis_size("ctx") // 2)
    ]


def ctx_scatter_sum(total, parts, finish=()):
    for part in parts:
        total = total + after(part, *finish).astype(F32)
    return total


def chip_masks(side):
    masks, mask = [], lax.axis_size("ctx") // 2
    while mask > 1:
        masks.append(mask)
        mask //= 2
    return masks[1:] + masks[:1] if side else masks


def ctx_gather_halves(
    first, second, wait=lambda values: values, last=lambda values: values, begun=None, finish=None
):
    held, offsets = [first[None], second[None]], [[0], [0]]
    steps = len(chip_masks(0))
    for step in range(steps):
        sent = []
        for side in range(2):
            mask = chip_masks(side)[step]
            got = begun[side] if begun and step == 0 else ctx_swap(held[side], mask)
            sent.append((got, [at ^ mask for at in offsets[side]]))
        if step < steps - 1:
            for side in range(2):
                held[side] = jnp.concatenate([held[side], wait(sent[side][0])], axis=0)
                offsets[side] = offsets[side] + sent[side][1]
    if finish:
        came = finish([got for got, _ in sent])
        sent = [(got, order) for got, (_, order) in zip(came, sent)]
    gathered = []
    for side in range(2):
        parts = [(held[side], offsets[side]), (last(sent[side][0]), sent[side][1])]
        gathered.append(
            parts + [(ctx_swap(block, 1), [at ^ 1 for at in order]) for block, order in parts]
        )
    return gathered


def ctx_scatter_halves(even, odd, ready=(), finish=()):
    chips = lax.axis_size("ctx") // 2
    rows = even.shape[0] // chips
    both = even.astype(F32) + ctx_swap(odd.astype(BF16), 1).astype(F32)
    both = both.reshape(chips, 2, rows // 2, -1)
    totals = []
    for side in range(2):
        blocks = {2 * at: both[at, side] for at in range(chips)}
        for step, mask in enumerate(reversed(chip_masks(side))):
            kept = [offset for offset in sorted(blocks) if not offset & mask]
            sent = jnp.stack([blocks[offset ^ mask].astype(BF16) for offset in kept])
            got = ctx_swap(after(sent, *ready) if step == 0 else sent, mask)
            if len(kept) == 1:
                got = after(got, *finish)
            blocks = {offset: blocks[offset] + got[at].astype(F32) for at, offset in enumerate(kept)}
        totals.append(blocks[0])
    return jnp.concatenate(totals, axis=0)


def in_order(parts, parity):
    blocks = {
        offset: values[at]
        for values, order in parts
        for at, offset in enumerate(order)
        if offset % 2 == parity
    }
    return jnp.concatenate([blocks[offset] for offset in sorted(blocks)], axis=0)


def ctx_exchange(values):
    return lax.all_to_all(values, "ctx", 0, 0, tiled=True)


def z_masks(count):
    masks = []
    while count > 1:
        masks.append(count - 1)
        count //= 2
    return masks


def z_offsets(count):
    offsets = [0]
    for mask in z_masks(count):
        offsets = offsets + [at ^ mask for at in offsets]
    return offsets


def z_swap(values, mask):
    count = lax.axis_size("fsdp")
    return lax.ppermute(values, "fsdp", [(at, at ^ mask) for at in range(count)])


def z_gather_steps(values):
    held = values[None]
    own = z_swap(held, 1)
    for mask in z_masks(lax.axis_size("fsdp"))[:-1]:
        held = jnp.concatenate([held, z_swap(held, mask)], axis=0)
    return held, own


def z_gather_finish(held, own):
    if held.shape[0] == 1:
        return [held, own]
    return [held, own, z_swap(held[1:], 1)]


def z_gather_parts(values):
    return z_gather_finish(*z_gather_steps(values))


def z_gather_held(values):
    held = values[None]
    for mask in z_masks(lax.axis_size("fsdp"))[:-1]:
        held = jnp.concatenate([held, z_swap(held, mask)], axis=0)
    return held


def z_sum_exchange(values):
    return jnp.sum(lax.all_to_all(values, "fsdp", 0, 0, tiled=True), axis=0, dtype=F32)


def z_gather_queued(values):
    return lax.all_gather(values, "fsdp", axis=0, tiled=True)


def z_scatter_queued(values):
    return lax.psum_scatter(values, "fsdp", scatter_dimension=0, tiled=True)


def place_kernel(plan, n_in, meta, *refs):
    ins, outs = refs[:n_in], refs[n_in:]
    for source, rows_in, target, rows_out in plan(meta):
        outs[target][rows_out] = ins[source][rows_in]


def place_blocks(meta, sources, outs, plan, name):
    return pl.pallas_call(
        functools.partial(place_kernel, plan, len(sources)),
        grid_spec=pltpu.PrefetchScalarGridSpec(
            num_scalar_prefetch=1,
            grid=(1,),
            in_specs=[pl.BlockSpec(memory_space=pltpu.VMEM)] * len(sources),
            out_specs=[pl.BlockSpec(memory_space=pltpu.VMEM)] * len(outs),
        ),
        out_shape=[jax.ShapeDtypeStruct(out, sources[0].dtype) for out in outs],
        compiler_params=pltpu.CompilerParams(vmem_limit_bytes=56 * 2**20),
        name=name,
    )(meta, *sources)


class Shape:
    def __init__(self, ctx_count, fsdp_count, slots, rows):
        self.ctx_count, self.fsdp_count, self.slots, self.rows = ctx_count, fsdp_count, slots, rows
        self.heads = HEADS // ctx_count
        self.block = rows * fsdp_count
        self.blocks = 2 * ctx_count
        self.keys = self.block * self.blocks
        self.tokens = slots * 2 * rows
        self.q_blocks = LANE_ROWS // (self.heads * rows)
        self.head_rows = self.q_blocks * rows
        self.q_tiles = self.blocks // self.q_blocks
        self.q_rows = self.q_tiles * LANE_ROWS
        self.chips = ctx_count // 2
        self.offsets = z_offsets(fsdp_count)


    def part_starts(self, count):
        half = self.fsdp_count // 2
        return [0, half, half + 1][:count]

    def part_of(self, at, count):
        starts = self.part_starts(count)
        part = max(index for index, start in enumerate(starts) if at >= start)
        return part, at - starts[part]


def for_blocks(shape, meta, act):
    me = meta[0]

    def step(chip, carry):
        for parity in range(2):
            first = meta[6 + (me ^ (2 * chip + parity))]
            for slot in range(shape.slots):
                for half in range(2):
                    block = first if half == 0 else shape.blocks - 1 - first
                    act(parity, chip, slot, half, block)
        return carry

    lax.fori_loop(0, shape.chips, step, 0)


def at_rows(start, size, unit):
    return pl.ds(pl.multiple_of(start, unit), size)


def q_source(shape, chip, slot, half):
    return at_rows(chip * shape.tokens + (slot * 2 + half) * shape.rows, shape.rows, shape.rows)


def q_target(shape, block, head):
    start = (block // shape.q_blocks) * LANE_ROWS + (block % shape.q_blocks) * shape.rows
    return at_rows(start + head * shape.head_rows, shape.rows, shape.rows)


def kv_source(shape, chip, order, slot, half):
    start = (chip * shape.fsdp_count + order) * shape.tokens + (slot * 2 + half) * shape.rows
    return at_rows(start, shape.rows, shape.rows)


def kv_target(shape, meta, block, order):
    start = block * shape.block + (meta[1] ^ shape.offsets[order]) * shape.rows
    return at_rows(start, shape.rows, shape.rows)


def query_bounds(shape, meta, slot, tile):
    lane = lax.broadcasted_iota(jnp.int32, (1, LANE_ROWS), 1)
    row = lane % shape.head_rows
    pos = (tile * shape.q_blocks + row // shape.rows) * shape.block + meta[1] * shape.rows + row % shape.rows
    first_end = meta[2 + 2 * slot]
    second_end = first_end + meta[3 + 2 * slot]

    def start_of(at):
        return jnp.where(at < first_end, 0, jnp.where(at < second_end, first_end, second_end))

    first_pos = tile * shape.q_blocks * shape.block + meta[1] * shape.rows
    last_pos = first_pos + (shape.q_blocks - 1) * shape.block + shape.rows - 1
    return pos, start_of(pos), start_of(first_pos) // KEY_TILE, last_pos // KEY_TILE + 1


def visible(pos, start, tile):
    key_pos = tile * KEY_TILE + lax.broadcasted_iota(jnp.int32, (KEY_TILE, LANE_ROWS), 0)
    return (key_pos <= pos) & (key_pos >= start)


def device_rows(shape, meta, parity, chip, slot, half):
    device = meta[0] ^ (2 * chip + parity)
    return at_rows(device * shape.tokens + (slot * 2 + half) * shape.rows, shape.rows, shape.rows)


def attend_kernel(shape, meta, q_even, q_odd, kv_even, kv_odd, o_out, q_all, kv_all, o_t, lse, o_rows):
    queries, keys = (q_even, q_odd), (kv_even, kv_odd)

    def place(parity, chip, slot, half, block):
        for head in range(shape.heads):
            q_all[slot, q_target(shape, block, head), :] = queries[parity][
                q_source(shape, chip, slot, half), head * HD : (head + 1) * HD
            ]
        for order in range(shape.fsdp_count):
            kv_all[slot, kv_target(shape, meta, block, order), :] = keys[parity][
                kv_source(shape, chip, order, slot, half), :
            ]

    for_blocks(shape, meta, place)

    def tile_step(item, carry):
        slot, tile = item // shape.q_tiles, item % shape.q_tiles
        pos, start, low, high = query_bounds(shape, meta, slot, tile)
        q_tile = q_all[slot, at_rows(tile * LANE_ROWS, LANE_ROWS, LANE_ROWS), :]

        def key_step(at, state):
            peak, total, acc = state
            part = at_rows(at * KEY_TILE, KEY_TILE, KEY_TILE)
            scores = mm_t(kv_all[slot, part, :HD], q_tile) * SCALE
            scores = jnp.where(visible(pos, start, at), scores, MASKED)
            new_peak = jnp.maximum(peak, jnp.max(scores, axis=0, keepdims=True))
            fade = jnp.exp(peak - new_peak)
            weights = jnp.exp(scores - new_peak)
            total = total * fade + jnp.sum(weights, axis=0, keepdims=True)
            acc = acc * fade + mm_rows(kv_all[slot, part, HD:], weights.astype(BF16))
            return new_peak, total, acc

        begin = (
            jnp.full((1, LANE_ROWS), MASKED, F32),
            jnp.zeros((1, LANE_ROWS), F32),
            jnp.zeros((HD, LANE_ROWS), F32),
        )
        peak, total, acc = lax.fori_loop(low, high, key_step, begin)
        acc = acc / total
        o_t[item] = acc
        lse[item] = peak + jnp.log(total)
        o_rows[slot, at_rows(tile * LANE_ROWS, LANE_ROWS, LANE_ROWS), :] = acc.T.astype(BF16)
        return carry

    lax.fori_loop(0, shape.slots * shape.q_tiles, tile_step, 0)

    def put_back(parity, chip, slot, half, block):
        for head in range(shape.heads):
            o_out[device_rows(shape, meta, parity, chip, slot, half), head * HD : (head + 1) * HD] = o_rows[
                slot, q_target(shape, block, head), :
            ]

    for_blocks(shape, meta, put_back)


def attend_grad_kernel(
    shape, meta, q_all, kv_all, o_t, lse, grads, gq_even, gq_odd, gkv_even, gkv_odd, ga_even, ga_odd, go_all, gq_all, gkv_all
):
    g_queries, g_keys, g_branch = (gq_even, gq_odd), (gkv_even, gkv_odd), (ga_even, ga_odd)

    def place(parity, chip, slot, half, block):
        source = device_rows(shape, meta, parity, chip, slot, half)
        for head in range(shape.heads):
            go_all[slot, q_target(shape, block, head), :] = grads[source, head * HD : (head + 1) * HD]
        g_branch[parity][q_source(shape, chip, slot, half), :] = grads[source, shape.heads * HD :]

    for_blocks(shape, meta, place)
    gkv_all[...] = jnp.zeros_like(gkv_all)

    def tile_step(item, carry):
        slot, tile = item // shape.q_tiles, item % shape.q_tiles
        pos, start, low, high = query_bounds(shape, meta, slot, tile)
        rows = at_rows(tile * LANE_ROWS, LANE_ROWS, LANE_ROWS)
        q_tile = q_all[slot, rows, :]
        go_tile = go_all[slot, rows, :]
        delta = jnp.sum(go_tile.astype(F32).T * o_t[item], axis=0, keepdims=True)
        lse_row = lse[item]

        def key_step(at, acc):
            part = at_rows(at * KEY_TILE, KEY_TILE, KEY_TILE)
            key_part, value_part = kv_all[slot, part, :HD], kv_all[slot, part, HD:]
            scores = mm_t(key_part, q_tile) * SCALE
            probs = jnp.where(visible(pos, start, at), jnp.exp(scores - lse_row), 0.0)
            g_scores = (probs * (mm_t(value_part, go_tile) - delta)).astype(BF16)
            gkv_all[slot, part, :HD] += mm(g_scores, q_tile)
            gkv_all[slot, part, HD:] += mm(probs.astype(BF16), go_tile)
            return acc + mm_rows(key_part, g_scores)

        acc = lax.fori_loop(low, high, key_step, jnp.zeros((HD, LANE_ROWS), F32))
        gq_all[slot, rows, :] = (acc * SCALE).T.astype(BF16)
        return carry

    lax.fori_loop(0, shape.slots * shape.q_tiles, tile_step, 0)

    def put_back(parity, chip, slot, half, block):
        for head in range(shape.heads):
            g_queries[parity][q_source(shape, chip, slot, half), head * HD : (head + 1) * HD] = gq_all[
                slot, q_target(shape, block, head), :
            ]
        for order in range(shape.fsdp_count):
            target = kv_target(shape, meta, block, order)
            source = kv_source(shape, chip, meta[1] ^ shape.offsets[order], slot, half)
            g_keys[parity][source, :HD] = (gkv_all[slot, target, :HD] * SCALE).astype(BF16)
            g_keys[parity][source, HD:] = gkv_all[slot, target, HD:].astype(BF16)

    for_blocks(shape, meta, put_back)


def attend(shape, meta, q_even, q_odd, kv_even, kv_odd):
    items = shape.slots * shape.q_tiles
    pairs = items * LANE_ROWS * shape.keys // 2
    return pl.pallas_call(
        functools.partial(attend_kernel, shape),
        grid_spec=pltpu.PrefetchScalarGridSpec(
            num_scalar_prefetch=1,
            grid=(1,),
            in_specs=[pl.BlockSpec(memory_space=pltpu.VMEM)] * 4,
            out_specs=[pl.BlockSpec(memory_space=pltpu.VMEM)] * 5,
            scratch_shapes=[pltpu.VMEM((shape.slots, shape.q_rows, HD), BF16)],
        ),
        out_shape=[
            jax.ShapeDtypeStruct((shape.ctx_count * shape.tokens, shape.heads * HD), BF16),
            jax.ShapeDtypeStruct((shape.slots, shape.q_rows, HD), BF16),
            jax.ShapeDtypeStruct((shape.slots, shape.keys, 2 * HD), BF16),
            jax.ShapeDtypeStruct((items, HD, LANE_ROWS), F32),
            jax.ShapeDtypeStruct((items, 1, LANE_ROWS), F32),
        ],
        compiler_params=pltpu.CompilerParams(vmem_limit_bytes=56 * 2**20),
        cost_estimate=pl.CostEstimate(flops=pairs * HD * 4, transcendentals=pairs, bytes_accessed=8 * 2**20),
        name="attend",
    )(meta, q_even, q_odd, kv_even, kv_odd)


def attend_grad(shape, meta, q_all, kv_all, o_t, lse, grads):
    items = shape.slots * shape.q_tiles
    q_like = jax.ShapeDtypeStruct((shape.chips * shape.tokens, shape.heads * HD), BF16)
    kv_like = jax.ShapeDtypeStruct((shape.chips * shape.fsdp_count * shape.tokens, 2 * HD), BF16)
    pairs = items * LANE_ROWS * shape.keys // 2
    return pl.pallas_call(
        functools.partial(attend_grad_kernel, shape),
        grid_spec=pltpu.PrefetchScalarGridSpec(
            num_scalar_prefetch=1,
            grid=(1,),
            in_specs=[pl.BlockSpec(memory_space=pltpu.VMEM)] * 5,
            out_specs=[pl.BlockSpec(memory_space=pltpu.VMEM)] * 6,
            scratch_shapes=[
                pltpu.VMEM((shape.slots, shape.q_rows, HD), BF16),
                pltpu.VMEM((shape.slots, shape.q_rows, HD), BF16),
                pltpu.VMEM((shape.slots, shape.keys, 2 * HD), F32),
            ],
        ),
        out_shape=[q_like, q_like, kv_like, kv_like, q_like, q_like],
        compiler_params=pltpu.CompilerParams(vmem_limit_bytes=56 * 2**20),
        cost_estimate=pl.CostEstimate(flops=pairs * HD * 10, transcendentals=pairs, bytes_accessed=10 * 2**20),
        name="attend_grad",
    )(meta, q_all, kv_all, o_t, lse, grads)


def block_of(shape, parts, at):
    part, block = shape.part_of(at, len(parts))
    return parts[part][block]


def gelu_parts(values):
    root = math.sqrt(2.0 / math.pi)
    return jnp.tanh(root * (values + 0.044715 * (values * values * values)))


def hidden_kernel(shape, meta, rows_ref, bias_ref, *refs):
    parts, (hidden_ref, act_ref) = refs[:-2], refs[-2:]
    depth = parts[0].shape[1]
    total = bias_ref[...]
    for at, offset in enumerate(shape.offsets):
        part = pl.ds(pl.multiple_of((meta[1] ^ offset) * depth, depth), depth)
        total = total + mm(rows_ref[:, part], block_of(shape, parts, at))
    hidden_ref[...] = total
    act_ref[...] = (0.5 * total * (1.0 + gelu_parts(total))).astype(BF16)


def feed_hidden(shape, meta, rows, parts, bias):
    count, width = rows.shape
    _, depth, columns = parts[0].shape
    tile = 256
    weights = [
        pl.BlockSpec((part.shape[0], depth, tile), lambda i, m: (0, 0, i)) for part in parts
    ]
    out = pl.BlockSpec((count, tile), lambda i, m: (0, i))
    return pl.pallas_call(
        functools.partial(hidden_kernel, shape),
        grid_spec=pltpu.PrefetchScalarGridSpec(
            num_scalar_prefetch=1,
            grid=(columns // tile,),
            in_specs=[
                pl.BlockSpec((count, width), lambda i, m: (0, 0)),
                pl.BlockSpec((1, tile), lambda i, m: (0, i)),
                *weights,
            ],
            out_specs=[out, out],
        ),
        out_shape=[
            jax.ShapeDtypeStruct((count, columns), F32),
            jax.ShapeDtypeStruct((count, columns), BF16),
        ],
        compiler_params=pltpu.CompilerParams(vmem_limit_bytes=56 * 2**20),
        cost_estimate=pl.CostEstimate(
            flops=2 * count * width * columns,
            transcendentals=count * columns,
            bytes_accessed=2 * (count * width + width * columns) + 6 * count * columns,
        ),
        name="feed_hidden",
    )(meta, rows, bias, *parts)


def hidden_grad_kernel(grads_ref, hidden_ref, first, second, out_ref, sum_ref):
    values = hidden_ref[...]
    tanh = gelu_parts(values)
    root = math.sqrt(2.0 / math.pi)
    slope = 0.5 * (1.0 + tanh) + (0.5 * root) * values * (1.0 - tanh * tanh) * (
        1.0 + (3.0 * 0.044715) * (values * values)
    )
    width = first.shape[1]
    grads = mm_t(grads_ref[:, :width], first[...]) + mm_t(grads_ref[:, width:], second[...])
    low = (grads * slope).astype(BF16)
    out_ref[...] = low
    sum_ref[...] = jnp.sum(low.astype(F32), axis=0, keepdims=True)


def feed_hidden_grad(grads, hidden, weights):
    count, width = grads.shape
    columns = hidden.shape[1]
    tile = 256
    place = pl.BlockSpec((count, tile), lambda i: (0, i))
    return pl.pallas_call(
        hidden_grad_kernel,
        grid=(columns // tile,),
        in_specs=[pl.BlockSpec((count, width), lambda i: (0, 0)), place]
        + [pl.BlockSpec((tile, width // 2), lambda i: (i, 0))] * 2,
        out_specs=[place, pl.BlockSpec((1, tile), lambda i: (0, i))],
        out_shape=[
            jax.ShapeDtypeStruct((count, columns), BF16),
            jax.ShapeDtypeStruct((1, columns), F32),
        ],
        compiler_params=pltpu.CompilerParams(vmem_limit_bytes=56 * 2**20),
        cost_estimate=pl.CostEstimate(
            flops=2 * count * width * columns,
            transcendentals=count * columns,
            bytes_accessed=2 * (count * width + width * columns) + 6 * count * columns,
        ),
        name="feed_hidden_grad",
    )(grads, hidden, *weights)


def feed_late_kernel(steps, rows_ref, first, second, norm_ref, grads_ref, even_ref, odd_ref, *d_refs):
    at = pl.program_id(0)
    width = first.shape[1]
    for side, out_ref in enumerate((even_ref, odd_ref)):

        @pl.when(at // steps == side)
        def _(out_ref=out_ref):
            out_ref[:, :width] = mm(rows_ref[...], first[...]).astype(BF16)
            out_ref[:, width:] = mm(rows_ref[...], second[...]).astype(BF16)

    @pl.when(at >= 2 * steps)
    def _():
        columns = d_refs[0].shape[1]
        for part, out_ref in enumerate(d_refs):
            out_ref[...] = mm_rows(
                norm_ref[...], grads_ref[:, part * columns : (part + 1) * columns]
            ).astype(BF16)


def feed_late(rows, weights, norm, grads):
    depth, half_width = weights[0].shape
    count, tile = rows.shape[0] // 2, 256
    steps = count // tile
    width, columns = norm.shape[1], grads.shape[1]
    last = 2 * steps - 1
    d_block = pl.BlockSpec((tile, columns // 2), lambda i: (jnp.maximum(i - last - 1, 0), 0))
    return pl.pallas_call(
        functools.partial(feed_late_kernel, steps),
        grid=(2 * steps + width // tile,),
        in_specs=[
            pl.BlockSpec((tile, depth), lambda i: (jnp.minimum(i, last), 0)),
            pl.BlockSpec((depth, half_width), lambda i: (0, 0)),
            pl.BlockSpec((depth, half_width), lambda i: (0, 0)),
            pl.BlockSpec((2 * count, tile), lambda i: (0, jnp.maximum(i - last - 1, 0))),
            pl.BlockSpec((2 * count, columns), lambda i: (0, 0)),
        ],
        out_specs=[
            pl.BlockSpec((tile, 2 * half_width), lambda i: (jnp.minimum(i, steps - 1), 0)),
            pl.BlockSpec((tile, 2 * half_width), lambda i: (jnp.clip(i - steps, 0, steps - 1), 0)),
            d_block,
            d_block,
        ],
        out_shape=[jax.ShapeDtypeStruct((count, 2 * half_width), BF16)] * 2
        + [jax.ShapeDtypeStruct((width, columns // 2), BF16)] * 2,
        compiler_params=pltpu.CompilerParams(vmem_limit_bytes=56 * 2**20),
        cost_estimate=pl.CostEstimate(
            flops=8 * count * depth * half_width + 4 * count * width * columns,
            transcendentals=0,
            bytes_accessed=2 * (6 * count * half_width + 2 * depth * half_width + 4 * count * width),
        ),
        name="feed_late",
    )(rows, *weights, norm, grads)


def feed_grad_kernel(shape, meta, rows_ref, *refs):
    parts, out_ref = refs[:-1], refs[-1]
    for at, offset in enumerate(shape.offsets):
        block = block_of(shape, parts, at)
        size = block.shape[0]
        part = pl.ds(pl.multiple_of((meta[1] ^ offset) * size, size), size)
        out_ref[:, part] = mm_t(rows_ref[...], block).astype(BF16)


def feed_grad(shape, meta, rows, parts, side, count):
    width = shape.fsdp_count * parts[0].shape[1]
    tile = 256
    steps = count // tile
    return pl.pallas_call(
        functools.partial(feed_grad_kernel, shape),
        grid_spec=pltpu.PrefetchScalarGridSpec(
            num_scalar_prefetch=1,
            grid=(steps,),
            in_specs=[
                pl.BlockSpec((tile, rows.shape[1]), lambda i, m: (side * steps + i, 0)),
                *[pl.BlockSpec(part.shape, lambda i, m: (0, 0, 0)) for part in parts],
            ],
            out_specs=pl.BlockSpec((tile, width), lambda i, m: (i, 0)),
        ),
        out_shape=jax.ShapeDtypeStruct((count, width), BF16),
        compiler_params=pltpu.CompilerParams(vmem_limit_bytes=56 * 2**20),
        cost_estimate=pl.CostEstimate(
            flops=2 * count * rows.shape[1] * width,
            transcendentals=0,
            bytes_accessed=2 * (count + width) * rows.shape[1] + 2 * count * width,
        ),
        name="feed_grad",
    )(meta, rows, *parts)


def branch_kernel(layout, grad, meta, rows_ref, *refs):
    parts, out_ref = refs[:-1], refs[-1]
    out_ref[...] = jnp.zeros_like(out_ref)
    for part, (ctx_order, z_order) in zip(parts, layout):
        depth, columns = part.shape[2], part.shape[3]
        for at, ctx_offset in enumerate(ctx_order):
            column = pl.ds(pl.multiple_of((meta[0] ^ ctx_offset) * columns, columns), columns)
            for order, z_offset in enumerate(z_order):
                row = pl.ds(pl.multiple_of((meta[1] ^ z_offset) * depth, depth), depth)
                if grad:
                    out_ref[:, row] += mm_t(rows_ref[:, column], part[at, order])
                else:
                    out_ref[:, column] += mm(rows_ref[:, row], part[at, order])


def times_blocks(meta, rows, parts, layout, grad):
    return pl.pallas_call(
        functools.partial(branch_kernel, layout, grad),
        grid_spec=pltpu.PrefetchScalarGridSpec(
            num_scalar_prefetch=1,
            grid=(1,),
            in_specs=[pl.BlockSpec(memory_space=pltpu.VMEM)] * (1 + len(parts)),
            out_specs=pl.BlockSpec(memory_space=pltpu.VMEM),
        ),
        out_shape=jax.ShapeDtypeStruct(rows.shape, F32),
        compiler_params=pltpu.CompilerParams(vmem_limit_bytes=56 * 2**20),
        cost_estimate=pl.CostEstimate(
            flops=2 * rows.shape[0] * rows.shape[1] ** 2,
            transcendentals=0,
            bytes_accessed=2 * rows.shape[1] ** 2,
        ),
        name="branch_grad" if grad else "branch",
    )(meta, rows, *parts)


def spread_rows_kernel(pieces, steps, meta, *refs):
    out_ref = refs[-1]
    for piece, blocks in enumerate(pieces):

        @pl.when(pl.program_id(0) // steps == piece)
        def _(blocks=blocks):
            for source, block, offset in blocks:
                rows = refs[source].shape[1]
                start = pl.multiple_of((meta[0] ^ offset) * rows, rows)
                out_ref[pl.ds(start, rows), :] = refs[source][block].astype(F32)


def spread_rows(meta, gathered):
    tile = 256
    members, specs, pieces = [], [], []
    for piece, parts in enumerate(gathered):
        blocks = []
        for values, order in parts:
            count, rows, columns = values.shape
            steps = columns // tile
            blocks += [(len(members), at, offset) for at, offset in enumerate(order)]
            members.append(values)

            def place(i, m, piece=piece, steps=steps):
                return (0, 0, jnp.clip(i - piece * steps, 0, steps - 1))

            specs.append(pl.BlockSpec((count, rows, tile), place))
        pieces.append(blocks)
    total = len(pieces[0]) * rows
    return pl.pallas_call(
        functools.partial(spread_rows_kernel, pieces, steps),
        grid_spec=pltpu.PrefetchScalarGridSpec(
            num_scalar_prefetch=1,
            grid=(len(pieces) * steps,),
            in_specs=specs,
            out_specs=pl.BlockSpec((total, tile), lambda i, m: (0, i)),
        ),
        out_shape=jax.ShapeDtypeStruct((total, len(pieces) * columns), F32),
        compiler_params=pltpu.CompilerParams(vmem_limit_bytes=48 * 2**20),
        name="spread_rows",
    )(meta, *members)


def spread_kernel(moves, extras, outs, meta, *refs):
    outs = refs[len(refs) - outs :]
    for source, block, columns, offset, out, start, step, size in moves:
        target = pl.multiple_of(start + (meta[0] ^ offset) * step, size)
        outs[out][:, pl.ds(target, size)] = refs[source][block, :, columns].astype(F32)
    for source, out in extras:
        width = refs[source].shape[1]
        outs[out][:, outs[out].shape[1] - width :] = refs[source][...]


def spread_columns(meta, gathered, groups, joined, extra=None):
    pieces = len(gathered)
    rows, columns = gathered[0][0][0].shape[1:]
    width = columns // groups if joined else columns // pieces
    count = sum(len(order) for _, order in gathered[0])
    if width % 128:
        results = []
        for parts in gathered:
            out = jnp.zeros((count, rows, groups, width), F32)
            for values, order in parts:
                for at, offset in enumerate(order):
                    block = values[at].reshape(rows, groups, width).astype(F32)
                    out = lax.dynamic_update_index_in_dim(out, block, meta[0] ^ offset, 0)
            results.append(jnp.transpose(out, (1, 2, 0, 3)).reshape(rows, -1))
        return [jnp.concatenate(results, axis=1)]
    members, moves = [], []
    for piece, parts in enumerate(gathered):
        if not joined:
            members = []
        for values, order in parts:
            for at, offset in enumerate(order):
                for group in range(groups):
                    start = ((piece if joined else 0) * groups + group) * count * width
                    source = (group if joined else piece) * width
                    moves.append(
                        (
                            len(members),
                            at,
                            slice(source, source + width),
                            offset,
                            0 if joined else piece,
                            start,
                            width,
                            width,
                        )
                    )
            members.append(values)
    sizes = [groups * count * width * pieces] if joined else [count * width] * pieces
    tile = min(rows, 64)
    in_specs = [
        pl.BlockSpec((member.shape[0], tile, columns), lambda i, m: (0, i, 0)) for member in members
    ]
    extras = []
    if extra is not None:
        extras = [(len(members), 0)]
        members.append(extra)
        in_specs.append(pl.BlockSpec((tile, extra.shape[1]), lambda i, m: (i, 0)))
        sizes[0] += extra.shape[1]
    return pl.pallas_call(
        functools.partial(spread_kernel, moves, extras, len(sizes)),
        grid_spec=pltpu.PrefetchScalarGridSpec(
            num_scalar_prefetch=1,
            grid=(rows // tile,),
            in_specs=in_specs,
            out_specs=[pl.BlockSpec((tile, size), lambda i, m: (i, 0)) for size in sizes],
        ),
        out_shape=[jax.ShapeDtypeStruct((rows, size), F32) for size in sizes],
        compiler_params=pltpu.CompilerParams(vmem_limit_bytes=48 * 2**20),
        name="spread_columns",
    )(meta, *members)


def pick_block(pair_table, ctx_at, half_bit):
    ctx_total = pair_table.shape[0]
    chosen = jnp.sum(jnp.where(jnp.arange(ctx_total, dtype=jnp.int32) == ctx_at, pair_table, 0))
    return jnp.where(half_bit == 0, chosen, 2 * ctx_total - 1 - chosen)


def body(
    inputs,
    w_qkv,
    w_out,
    w_fc,
    w_proj,
    ln1_gain,
    ln1_bias,
    bias_q,
    bias_v,
    bias_out,
    ln2_gain,
    ln2_bias,
    bias_fc,
    bias_proj,
    cotangent,
    lengths,
    pair_table,
):
    slots, _, _, rows, width = inputs.shape
    ctx_count, fsdp_count = lax.axis_size("ctx"), lax.axis_size("fsdp")
    c_at, z_at = lax.axis_index("ctx"), lax.axis_index("fsdp")
    shape = Shape(ctx_count, fsdp_count, slots, rows)
    tokens, chips = shape.tokens, shape.chips
    q_width = width // ctx_count
    shard = width // fsdp_count
    hidden_width = w_fc.shape[1]
    unit = hidden_width // (fsdp_count * ctx_count)
    meta = jnp.concatenate(
        [jnp.stack([c_at, z_at]).astype(jnp.int32), lengths.reshape(-1), pair_table]
    ).astype(jnp.int32)

    offsets = jnp.arange(2 * rows, dtype=jnp.int32)
    pos = (
        pick_block(pair_table, c_at, offsets // rows) * shape.block + z_at * rows + offsets % rows
    )
    live = (pos[None, :] < lengths[:, 0:1] + lengths[:, 1:2]).reshape(tokens, 1).astype(F32)

    x_low = inputs.reshape(tokens, width)
    grad_out = cotangent.reshape(tokens, width).astype(F32) * live
    grad_mlp = grad_out.astype(BF16)
    pack_width = q_width + 2 * HD
    w_first = jnp.concatenate(
        [lax.dynamic_slice_in_dim(w_qkv, c_at * q_width, q_width, axis=1), w_qkv[:, width:]], axis=1
    ).astype(BF16)
    vectors = [ln1_gain, ln1_bias, bias_q, bias_v, bias_out, ln2_gain, ln2_bias, bias_fc, bias_proj]
    sizes = [member.shape[0] for member in vectors]
    vector_rows = 16 * math.ceil(sum(sizes) / (16 * HD))
    packed = jnp.concatenate(
        [member.astype(BF16) for member in vectors]
        + [jnp.zeros((vector_rows * HD - sum(sizes),), BF16)]
    ).reshape(vector_rows, HD)
    x_even, x_odd = ctx_gather(after(x_low, w_first))
    half = fsdp_count // 2
    first_held, first_own = z_gather_steps(w_first)
    first_blocks = z_gather_finish(first_held, first_own)
    vector_held = z_gather_held(after(packed, first_held))
    vector_blocks = [vector_held, z_swap(vector_held, 1)]

    def first_plan(ref):
        moves = []
        for at, offset in enumerate(shape.offsets):
            owner, (part, block) = ref[1] ^ offset, shape.part_of(at, len(first_blocks))
            weight_rows = pl.ds(pl.multiple_of(owner * shard, shard), shard)
            q_part, kv_part = pl.ds(0, q_width), pl.ds(q_width, 2 * HD)
            moves += [
                (part, (block, slice(None), q_part), 0, (weight_rows, slice(None))),
                (part, (block, slice(None), kv_part), 1, (weight_rows, slice(None))),
                (len(first_blocks) + at // half, (at % half,), 2, (owner,)),
            ]
        return moves

    w_q, w_kv, packed = place_blocks(
        meta,
        [*first_blocks, *vector_blocks],
        [(width, q_width), (width, 2 * HD), (fsdp_count, vector_rows, HD)],
        first_plan,
        "place_first",
    )
    packed = packed.reshape(fsdp_count, -1)
    full, start = [], 0
    for size in sizes:
        full.append(packed[:, start : start + size].reshape(-1).astype(F32))
        start += size
    gain_one, shift_one, q_bias, v_bias, out_bias, gain_two, shift_two, fc_bias, proj_bias = full
    q_bias = lax.dynamic_slice_in_dim(q_bias, c_at * q_width, q_width)
    fc_bias = lax.dynamic_index_in_dim(
        fc_bias.reshape(fsdp_count, ctx_count, unit), c_at, 1, keepdims=False
    )

    def relative_plan(ref):
        return [
            (
                0,
                (ref[0] ^ (2 * chip + parity),),
                0,
                (pl.ds((parity * chips + chip) * tokens, tokens),),
            )
            for parity in range(2)
            for chip in range(chips)
        ]

    x_own = x_low.astype(F32)
    first_norm, normed_one, inverse_one = layer_norm(x_own, gain_one, shift_one)
    kv_own = mm(first_norm.astype(BF16), w_kv)
    kv_own = jnp.concatenate([kv_own[:, :HD], kv_own[:, HD:] + v_bias], axis=1).astype(BF16)
    kv_z = jnp.concatenate(z_gather_parts(kv_own), axis=0).reshape(fsdp_count * tokens, 2 * HD)
    kv_even, kv_odd = ctx_gather(kv_z)

    out_parts = z_gather_parts(
        after(lax.dynamic_slice_in_dim(w_out, c_at * q_width, q_width, axis=1).astype(BF16), kv_z)
    )

    fc_own = jnp.concatenate(
        [
            lax.dynamic_slice_in_dim(
                w_fc, group * (hidden_width // fsdp_count) + c_at * unit, unit, axis=1
            )
            for group in range(fsdp_count)
        ],
        axis=1,
    ).astype(BF16)
    proj_own = lax.dynamic_slice_in_dim(w_proj, c_at * unit, unit, axis=0).astype(BF16)
    out_halves = out_parts[0], jnp.concatenate(out_parts[1:], axis=0)
    fc_steps = z_gather_steps(after(fc_own, out_parts[0]))

    a_even = layer_norm(x_even.astype(F32), gain_one, shift_one)[0].astype(BF16)
    a_odd = layer_norm(x_odd.astype(F32), gain_one, shift_one)[0].astype(BF16)
    q_even = (mm(a_even, w_q) + q_bias).astype(BF16)
    q_odd = (mm(a_odd, w_q) + q_bias).astype(BF16)
    o_heads, q_all, kv_all, o_t, lse = attend(shape, meta, q_even, q_odd, kv_even, kv_odd)
    out_gathered = ctx_gather_halves(
        *[after(side, kv_even) for side in out_halves],
        wait=lambda part: after(part, kv_odd),
        last=lambda part: after(part, o_heads),
    )
    out_blocks, out_layout = [], []
    for side, parts in enumerate(out_gathered):
        z_order = shape.offsets[side * half : (side + 1) * half]
        for values, order in parts:
            out_blocks.append(values)
            out_layout.append((order, z_order))
    o_own = ctx_exchange(o_heads.reshape(ctx_count, tokens, q_width))
    o_own = jnp.transpose(o_own, (1, 0, 2)).reshape(tokens, width)
    fc_parts = z_gather_finish(*fc_steps)
    proj_own = after(proj_own, fc_parts[-1])
    w_p = [
        z_gather_queued(proj_own[:, at * width // 2 : (at + 1) * width // 2]) for at in range(2)
    ]
    o_own = after(o_own, *fc_steps)
    middle = x_own + (times_blocks(meta, o_own, out_blocks, out_layout, False) + out_bias)
    second_norm, normed_two, inverse_two = layer_norm(middle, gain_two, shift_two)

    o_parts = [ctx_swap(o_own, 2 * at) for at in range(1, chips)]
    cn_own, o_parts = lax.optimization_barrier((second_norm.astype(BF16), o_parts))
    cn_even, cn_odd = ctx_gather(cn_own)
    o_even = jnp.concatenate([o_own, *o_parts], axis=0)
    o_odd = ctx_swap(o_even, 1)
    gm_all = lax.all_gather(grad_mlp, "ctx", axis=0, tiled=False)
    (gm_all,) = place_blocks(
        meta, [gm_all], [(ctx_count * tokens, width)], relative_plan, "place_rows"
    )
    cn_all = jnp.concatenate([cn_even, cn_odd], axis=0)
    half_rows = chips * tokens
    hidden, act = feed_hidden(shape, meta, cn_all, fc_parts, fc_bias.reshape(1, -1))
    d_proj = mm_rows(act, gm_all).astype(BF16)
    g_hidden, g_bias_fc = feed_hidden_grad(gm_all, hidden, w_p)
    g_odd = feed_grad(shape, meta, g_hidden, fc_parts, 1, half_rows)
    g_even = feed_grad(shape, meta, after(g_hidden, g_odd), fc_parts, 0, half_rows)
    g_total, g_low = ctx_scatter_cores(g_even, g_odd)
    cn_late, act_late, g_low = lax.optimization_barrier((cn_all, act, g_low))
    g_parts = ctx_scatter_sent(g_low, tokens)
    late = feed_late(act_late, w_p, cn_late, g_hidden)
    g_parts, late = lax.optimization_barrier((g_parts, late))
    grad_second = ctx_scatter_sum(g_total, g_parts)
    d_proj = [
        z_scatter_queued(after(part, *w_p)) for part in (d_proj[:, : width // 2], d_proj[:, width // 2 :])
    ]
    d_fc = [z_scatter_queued(part) for part in late[2:]]
    r_total, r_low = ctx_scatter_cores(*late[:2])

    grad_mid_norm, grad_gain_two, grad_shift_two = norm_backward(
        grad_second, normed_two, inverse_two, gain_two
    )
    grad_middle = grad_out + grad_mid_norm
    grad_branch = grad_middle.astype(BF16)
    go_own = times_blocks(meta, grad_branch, out_blocks, out_layout, True).astype(BF16)
    grads = jnp.concatenate(
        [
            go_own.reshape(tokens, ctx_count, q_width),
            grad_branch.reshape(tokens, ctx_count, q_width),
        ],
        axis=2,
    )
    grads_sent = jnp.transpose(grads, (1, 0, 2))
    grads = ctx_exchange(grads_sent).reshape(ctx_count * tokens, 2 * q_width)
    grads, r_total = lax.optimization_barrier((grads, r_total))

    gq_even, gq_odd, gkv_even, gkv_odd, ga_even, ga_odd = attend_grad(
        shape, meta, q_all, kv_all, o_t, lse, grads
    )
    first_sent = [ctx_swap(part[None], chip_masks(side)[0]) for side, part in enumerate(d_proj)]
    r_parts = ctx_scatter_sent(r_low, tokens, [grads_sent])
    gkv_odd, first_sent, r_parts = lax.optimization_barrier((gkv_odd, first_sent, r_parts))
    result = (middle + (ctx_scatter_sum(r_total, r_parts) + proj_bias)).astype(BF16)
    gkv_plane = ctx_scatter(gkv_even, gkv_odd)
    d_q = mm_rows(a_even, gq_even) + mm_rows(a_odd, gq_odd)
    d_out = mm_rows(o_even, ga_even) + mm_rows(o_odd, ga_odd)
    d_pair = with_layout_constraint(
        jnp.concatenate([d_q, d_out], axis=1).astype(BF16), Layout(major_to_minor=(0, 1))
    )
    d_pair = z_scatter_queued(d_pair)
    pair = []

    def finish(parts):
        parts, d_done = lax.optimization_barrier((parts, d_pair))
        pair.append(d_done)
        return parts

    d_proj = ctx_gather_halves(
        *d_proj, wait=lambda part: after(part, gkv_plane), begun=first_sent, finish=finish
    )
    (d_pair,) = pair
    gkv_low = z_sum_exchange(gkv_plane.astype(BF16).reshape(fsdp_count, tokens, 2 * HD)).astype(BF16)
    gkv_all = ctx_exchange(jnp.broadcast_to(gkv_low[None], (ctx_count,) + gkv_low.shape))
    gl_total, gl_low = ctx_scatter_cores(mm_t(gq_even, w_q), mm_t(gq_odd, w_q))
    gl_parts = ctx_scatter_sent(gl_low, tokens, [gkv_plane])
    gkv_all, gl_parts = lax.optimization_barrier((gkv_all, gl_parts))
    (gkv_all,) = place_blocks(
        meta,
        [gkv_all],
        [(ctx_count * tokens, 2 * HD)],
        relative_plan,
        "place_keys",
    )
    gkv_even, gkv_odd = gkv_all[: chips * tokens], gkv_all[chips * tokens :]
    grad_first = ctx_scatter_sum(gl_total, gl_parts)
    grad_in_norm, grad_gain_one, grad_shift_one = norm_backward(
        grad_first + mm_t(gkv_low, w_kv), normed_one, inverse_one, gain_one
    )
    grad_inputs = grad_middle + grad_in_norm

    grad_w_proj = spread_rows(meta, d_proj)
    d_fc = ctx_gather_halves(
        *[after(part, gkv_low) for part in d_fc], last=lambda part: after(part, grad_w_proj)
    )
    (grad_w_fc,) = spread_columns(meta, d_fc, fsdp_count // 2, True)
    d_kv = (mm_rows(a_even, gkv_even) + mm_rows(a_odd, gkv_odd)).astype(BF16)
    d_kv = z_scatter_queued(d_kv).astype(F32)
    d_pair = [
        (values.reshape(chips, shard, 2 * q_width), [2 * at + parity for at in range(chips)])
        for parity, values in enumerate(ctx_gather(d_pair))
    ]
    grad_w_qkv, grad_w_out = spread_columns(meta, [d_pair] * 2, 1, False, d_kv)

    def column_sum(*parts):
        return sum(jnp.sum(part, axis=0, dtype=F32) for part in parts)

    g_bias_q = lax.dynamic_update_index_in_dim(
        jnp.zeros((ctx_count, q_width), F32), column_sum(gq_even, gq_odd), c_at, 0
    ).reshape(-1)
    g_bias_fc = lax.dynamic_update_index_in_dim(
        jnp.zeros((fsdp_count, ctx_count, unit), F32), g_bias_fc.reshape(fsdp_count, unit), c_at, 1
    ).reshape(-1)
    g_vectors = [
        grad_gain_one,
        grad_shift_one,
        g_bias_q,
        column_sum(gkv_low[:, HD:]),
        column_sum(grad_branch),
        grad_gain_two,
        grad_shift_two,
        g_bias_fc,
        column_sum(grad_mlp),
    ]
    stacked = jnp.concatenate(
        [member.reshape(fsdp_count, -1) for member in g_vectors], axis=1
    ).astype(BF16)
    own = z_sum_exchange(stacked).astype(BF16)
    own, grad_w_proj = lax.optimization_barrier((own, grad_w_proj))
    own = ctx_exchange(jnp.broadcast_to(own[None], (ctx_count,) + own.shape))
    summed = jnp.sum(own, axis=0, dtype=F32)
    vector_grads, start = [], 0
    for size in sizes:
        vector_grads.append(summed[start : start + size].astype(BF16).astype(F32))
        start += size
    return (
        result.reshape(inputs.shape),
        grad_inputs.reshape(inputs.shape),
        grad_w_qkv,
        grad_w_out,
        grad_w_fc,
        grad_w_proj,
        *vector_grads,
    )


def solution(mesh):
    rows_placed = P(None, "ctx", None, "fsdp", None)
    matrix, vector = P("fsdp", None), P("fsdp")
    return jax.shard_map(
        body,
        mesh=mesh,
        in_specs=(rows_placed,) + (matrix,) * 4 + (vector,) * 9 + (rows_placed, P(), P()),
        out_specs=(rows_placed, rows_placed) + (matrix,) * 4 + (vector,) * 9,
        check_vma=False,
    )
```
